128 devices in a mesh: gx: 8 (over z, core), gy: 16 (over x, y).
Axes of the slice: x: 4, y: 4, z: 4, core: 2. Of those that a mesh axis runs over, the one named last changes fastest.
Arguments:
- initial_state: float32 [2, 32, 48, 2048], P(None, 'gx', None, 'gy'), may hold values from -6 to 6
- eddy_diffusivity: float32 [32, 48, 2048], P('gx', None, 'gy'), may hold values from 0.02 to 0.12
- velocity: float32 [3, 32, 48, 2048], P(None, 'gx', None, 'gy'), may hold values from -0.08 to 0.08
- target: float32 [2, 32, 48, 2048], P(None, 'gx', None, 'gy'), may hold values from -6 to 6
- sensor_cell: int32 [32768], P(('gx', 'gy')), may hold values from 0 to 24575
- sensor_owner: int32 [32768, 1], P(('gx', 'gy')), may hold values from 0 to 127; in each aligned block of 256 rows (0 to 255, 256 to 511, ...) at most 4 rows name the same one
- observations: float32 [32768, 2, 4], P(('gx', 'gy')), may hold values from -6 to 6
- actuator_block: int32 [4096], P(('gx', 'gy')), may hold values from 0 to 191
- actuator_owner: int32 [4096, 1], P(('gx', 'gy')), may hold values from 0 to 15; in each aligned block of 32 rows (0 to 31, 32 to 63, ...) at most 4 rows name the same one
- controls: float32 [4096, 2], P(('gx', 'gy')), may hold values from -6 to 6
- footprint: float32 [4096, 128], P(('gx', 'gy')), may hold values from 0 to 1
Outputs:
- final_state: float32 [2, 32, 48, 2048], P(None, 'gx', None, 'gy')
- initial_sensitivity: float32 [2, 32, 48, 2048], P(None, 'gx', None, 'gy')
- actuator_gradient: float32 [4096, 2], P(('gx', 'gy'))
The draws below stay inside these ranges and needn't reach their ends.
Inputs may be any that keep to these rules, and one draw needn't show every extreme that they name: `sensor_owner`: among the 256 rows of one device, no owner is named more than 4 times, a bound that some block reaches. `actuator_owner`: among the 32 rows of one device, no owner is named more than 4 times, a bound that some block reaches.
All inputs are finite; a program needn't handle non-finite values.
Results may differ from the reference program's by a relative error of at most 0.00002.
Values sent between devices are 32-bit elements; how exact they have to be, the bound alone decides.
A program may use at most 128 MiB of HBM per device.

```python
import math
import jax
import jax.numpy as jnp
import numpy as np

CX = 4
CY = 128
NZ = 48
NSTEPS = 4
FX = 4
FZ = 8
FY = 4
CAPS = 4
CAPA = 4
FOOT = 128
NX = 32
NY = 2048
OWNERS = 128
SENS_DEV = 256
SENSORS = 32768
ACT_DEV = 32
ACTS = 4096
CELLS_DEV = 24576
BLOCKS_DEV = 192
N_GY = 16


def set_ends(drawn, stream_key, least, largest):
    longest = drawn.shape.index(max(drawn.shape))
    spots = []
    for shift in (0, 1):
        where = [jax.random.randint(jax.random.fold_in(stream_key, axis), (), 0, length) for axis, length in enumerate(drawn.shape)]
        where[longest] = (where[longest] + shift) % drawn.shape[longest]
        spots.append(tuple(where))
    return drawn.at[spots[0]].set(least).at[spots[1]].set(largest)


def levels(stream_key, shape, shards, smallest, largest):
    def one(axis_at, blocks):
        heights = jax.random.uniform(jax.random.fold_in(jax.random.fold_in(stream_key, 6), axis_at), (blocks,), jnp.float32, smallest / len(shards), largest / len(shards))
        return jnp.repeat(jnp.exp(heights), shape[axis_at] // blocks).reshape((-1,) + (1,) * (len(shape) - axis_at - 1))

    factor_of = one(*shards[0])
    for cut in shards[1:]:
        factor_of = factor_of * one(*cut)
    return factor_of


def assign_block(key, own, number, rows, amount, top, limit, skew):
    order = jax.random.permutation(key, amount)
    packed, usual = portions_of(amount, rows * top, limit, skew, True), portions_of(amount, rows * top, limit, skew, False)
    places = jnp.arange(amount)

    def named(tallies, turn):
        used = int((tallies > 0).sum())
        fixed = max(1, used // 4)
        passed = fixed + (places - fixed + turn * (used - fixed)) % max(1, amount - fixed)
        return jnp.zeros((amount,), jnp.int32).at[order[jnp.where(places < fixed, places, passed)]].set(jnp.asarray(tallies, jnp.int32))

    tallies = jnp.where(number % 4 == 0, named(packed, number // 4), named(usual, number - number // 4 - 1))
    mixed = jax.random.permutation(jax.random.fold_in(own, 3), amount)
    source_of, sink = mixed[0:amount // 2 * 2:2], mixed[1:amount // 2 * 2:2]
    margin = jnp.minimum(tallies[source_of] - 1, limit - tallies[sink]) // 2
    margin = jnp.where((source_of == order[0]) | (sink == order[0]) | (tallies[sink] == 0), 0, jnp.maximum(margin, 0))
    passed = jax.random.randint(jax.random.fold_in(own, 4), (amount // 2,), 0, 1 << 20) % (margin + 1)
    tallies = tallies.at[source_of].add(-passed).at[sink].add(passed)
    items = jnp.searchsorted(jnp.cumsum(tallies), jnp.arange(rows * top), side="right").astype(jnp.int32)
    grid = items.reshape(top, rows).T
    grid = grid[jax.random.permutation(jax.random.fold_in(own, 1), rows)]
    turn = jax.random.randint(jax.random.fold_in(own, 2), (rows, 1), 0, top)
    return jnp.take_along_axis(grid, (jnp.arange(top)[None, :] + turn) % top, axis=1)


def portions_of(count, total, most, slope, full):
    weights = [(1 << 20) // math.isqrt(rank ** slope) + 1 for rank in range(1, count + 1)]
    largest = most if full else min(most, max(-(-total // count), total * weights[0] // sum(weights)))
    least = 1 if total - largest >= count - 1 else 0
    given, spare = [largest] + [least] * (count - 1), total - largest - least * (count - 1)
    while spare > 0:
        movable = [i for i in range(1, count) if given[i] < largest] or [i for i in range(1, count) if given[i] < most]
        mass, left = sum([weights[i] for i in movable]), spare
        for i in movable:
            extra = min(most - given[i], max(1, left * weights[i] // mass), spare)
            given[i] = given[i] + extra
            spare = spare - extra
    return np.array(given)


def bell_draw(rng, extent, deviation, reach, shards=(), kind=jnp.bfloat16):
    values = jax.random.normal(rng, extent, jnp.float32) * deviation
    if len(shards) > 0:
        values = levels(rng, extent, shards, -0.22, 0.18) * values
    return jnp.clip(values, min=-reach, max=reach).astype(kind)


def setup_inputs(seed: int = 0) -> dict:
    key_list = jax.random.split(jax.random.key(seed), 12)
    initial_state = bell_draw(key_list[0], (2, NX, NZ, NY), 1.0, 6.0, ((1, 8), (3, 16)), jnp.float32)
    eddy_diffusivity = jnp.clip(jnp.exp(math.log(0.12) - 1.7917595 * jax.random.uniform(key_list[1], (NX, NZ, NY), jnp.float32) ** levels(key_list[1], (NX, NZ, NY), ((0, 8), (2, 16)), -0.2, 0.2)), 0.02, 0.12)
    velocity = jnp.clip(jax.random.uniform(key_list[2], (3, NX, NZ, NY), jnp.float32, -0.08, 0.08) * levels(key_list[2], (3, NX, NZ, NY), ((1, 8), (3, 16)), -0.4, 0.0), -0.08, 0.08)
    target = bell_draw(key_list[3], (2, NX, NZ, NY), 1.0, 6.0, ((1, 8), (3, 16)), jnp.float32)
    sensor_cell = set_ends(jax.random.randint(key_list[4], (SENSORS,), 0, CELLS_DEV), jax.random.fold_in(key_list[4], 1), 0, CELLS_DEV - 1).astype(jnp.int32)
    sensor_owner_keys = jax.random.split(jax.random.fold_in(key_list[5], 1), SENSORS // SENS_DEV)
    sensor_owner_turns = jax.random.permutation(jax.random.fold_in(key_list[5], 3), SENSORS // SENS_DEV)
    sensor_owner = jax.vmap(lambda own, number: assign_block(jax.random.fold_in(key_list[5], 2), own, number, SENS_DEV, OWNERS, 1, CAPS, 2))(sensor_owner_keys, sensor_owner_turns).reshape((SENSORS, 1))
    observations = bell_draw(key_list[6], (SENSORS, 2, NSTEPS), 1.0, 6.0, ((0, 128),), jnp.float32)
    actuator_block = set_ends(jax.random.randint(key_list[7], (ACTS,), 0, BLOCKS_DEV), jax.random.fold_in(key_list[7], 1), 0, BLOCKS_DEV - 1).astype(jnp.int32)
    actuator_owner_keys = jax.random.split(jax.random.fold_in(key_list[8], 1), ACTS // ACT_DEV)
    actuator_owner_turns = jax.random.permutation(jax.random.fold_in(key_list[8], 3), ACTS // ACT_DEV)
    actuator_owner = jax.vmap(lambda own, number: assign_block(jax.random.fold_in(key_list[8], 2), own, number, ACT_DEV, N_GY, 1, CAPA, 2))(actuator_owner_keys, actuator_owner_turns).reshape((ACTS, 1))
    controls = bell_draw(key_list[9], (ACTS, 2), 1.0, 6.0, ((0, 128),), jnp.float32)
    footprint = jnp.clip(1.0 * jax.random.uniform(key_list[10], (ACTS, FOOT), jnp.float32) ** levels(key_list[10], (ACTS, FOOT), ((0, 128),), -0.2, 0.2), 0.0, 1.0)
    return {"initial_state": initial_state, "eddy_diffusivity": eddy_diffusivity, "velocity": velocity, "target": target, "sensor_cell": sensor_cell, "sensor_owner": sensor_owner, "observations": observations, "actuator_block": actuator_block, "actuator_owner": actuator_owner, "controls": controls, "footprint": footprint}


prandtl = 0.85


def species_scale():
    return jnp.array([1.0, 1.0 / prandtl], jnp.float32).reshape(2, 1, 1, 1)


def shift_z(values, upward):
    blank = jnp.zeros_like(values[..., :1, :])
    if upward:
        return jnp.concatenate([values[..., 1:, :], blank], axis=-2)
    return jnp.concatenate([blank, values[..., :-1, :]], axis=-2)


def neighbours(values):
    centre = values[..., 1:-1, :, 1:-1]
    return (centre, values[..., 2:, :, 1:-1], values[..., :-2, :, 1:-1],
            values[..., 1:-1, :, 2:], values[..., 1:-1, :, :-2],
            shift_z(centre, True), shift_z(centre, False))


def diffusion(beside_all, kappas):
    centre = beside_all[0]
    summed = jnp.zeros_like(centre)
    for side_id in range(1, 7):
        summed = summed + 0.5 * (kappas[0] + kappas[side_id]) * (beside_all[side_id] - centre)
    return summed * species_scale()


def forward_step(padded, coeffs):
    beside_all = neighbours(padded)
    kappas = neighbours(coeffs[0])
    vel_x = coeffs[1][1:-1, :, 1:-1]
    vel_y = coeffs[2][1:-1, :, 1:-1]
    vel_z = coeffs[3][1:-1, :, 1:-1]
    source = coeffs[4:6][:, 1:-1, :, 1:-1]
    advect = vel_x * (beside_all[1] - beside_all[2]) + vel_y * (beside_all[3] - beside_all[4]) + vel_z * (beside_all[5] - beside_all[6])
    return beside_all[0] + diffusion(beside_all, kappas) - 0.5 * advect + source


def adjoint_step(padded, coeffs):
    beside_all = neighbours(padded)
    kappas = neighbours(coeffs[0])
    carried = jnp.zeros_like(beside_all[0])
    for axis_id, pair_ids in enumerate(((1, 2), (3, 4), (5, 6))):
        shifted = neighbours(coeffs[1 + axis_id] * padded)
        carried = carried + shifted[pair_ids[0]] - shifted[pair_ids[1]]
    return beside_all[0] + diffusion(beside_all, kappas) + 0.5 * carried


def pad_grid(values):
    return jnp.pad(values, ((0, 0), (1, 1), (0, 0), (1, 1)))


def reference(initial_state, eddy_diffusivity, velocity, target, sensor_cell, sensor_owner, observations, actuator_block, actuator_owner, controls, footprint):
    cell_total = NX * NZ * NY
    record_id = jnp.arange(ACTS, dtype=jnp.int32)
    row_x = (record_id // ACT_DEV) // N_GY
    col_y = actuator_owner[:, 0]
    blocks_z = NZ // FZ
    blocks_y = CY // FY
    block_x = actuator_block // (blocks_z * blocks_y)
    block_z = (actuator_block // blocks_y) % blocks_z
    block_y = actuator_block % blocks_y
    foot_pos = jnp.arange(FOOT, dtype=jnp.int32)
    foot_x = foot_pos // (FZ * FY)
    foot_z = (foot_pos // FY) % FZ
    foot_y = foot_pos % FY
    cell_x = row_x[:, None] * CX + block_x[:, None] * FX + foot_x[None, :]
    cell_z = block_z[:, None] * FZ + foot_z[None, :]
    cell_y = col_y[:, None] * CY + block_y[:, None] * FY + foot_y[None, :]
    act_index = ((cell_x * NZ + cell_z) * NY + cell_y).astype(jnp.int32)
    strength = controls[:, :, None] * footprint[:, None, :]
    source = jnp.zeros((2, cell_total), jnp.float32).at[:, act_index.reshape(-1)].add(
        jnp.transpose(strength, (1, 0, 2)).reshape(2, -1)).reshape(2, NX, NZ, NY)

    owner_ids = sensor_owner[:, 0]
    local_x = sensor_cell // (NZ * CY)
    local_z = (sensor_cell // CY) % NZ
    local_y = sensor_cell % CY
    sensor_index = (((owner_ids // N_GY) * CX + local_x) * NZ + local_z) * NY + (owner_ids % N_GY) * CY + local_y
    sensor_index = sensor_index.astype(jnp.int32)

    coeffs = pad_grid(jnp.concatenate([eddy_diffusivity[None], velocity, source], axis=0))

    def inject(residual):
        return jnp.zeros((2, cell_total), jnp.float32).at[:, sensor_index].add(residual).reshape(2, NX, NZ, NY)

    current = initial_state
    misfits = []
    for step_id in range(NSTEPS):
        current = forward_step(pad_grid(current), coeffs)
        values = current.reshape(2, -1)[:, sensor_index]
        misfits.append(values - observations[:, :, step_id].T)

    adjoint = current - target + inject(misfits[NSTEPS - 1])
    summed = adjoint
    for step_id in range(NSTEPS - 1, 0, -1):
        adjoint = adjoint_step(pad_grid(adjoint), coeffs) + inject(misfits[step_id - 1])
        summed = summed + adjoint
    sensitivity = adjoint_step(pad_grid(adjoint), coeffs)

    flat_summed = summed.reshape(2, -1)
    picked = flat_summed[:, act_index]
    gradient = jnp.sum(picked * footprint[None, :, :], axis=2).T
    return current, sensitivity, gradient
```

```python
import functools

import jax
import jax.numpy as jnp
from jax import lax
from jax.experimental import pallas as pl
from jax.experimental.pallas import tpu as pltpu
from jax.sharding import PartitionSpec as P

MESH = pl.DeviceIdType.MESH
F32 = jnp.float32
BF16 = jnp.bfloat16
HIGH = lax.Precision.HIGHEST

CX = 4
NZ = 48
CY = 128
FX = 4
FZ = 8
FY = 4
BZ = NZ // FZ
STEPS = 4
ZV = NZ // 8
PZ = NZ + 16
Z0 = 8
prandtl = 0.85
SCALES = (1.0, 1.0 / prandtl)


def iota(shape, dim):
    return lax.broadcasted_iota(jnp.int32, shape, dim)


def dot_nn(a, b, precision=None):
    return lax.dot_general(
        a, b, (((1,), (0,)), ((), ())), precision=precision, preferred_element_type=F32
    )


def dot_nt(a, b, precision=None):
    return lax.dot_general(
        a, b, (((1,), (1,)), ((), ())), precision=precision, preferred_element_type=F32
    )


def split3(x):
    hi = x.astype(BF16)
    rest = x - hi.astype(F32)
    mid = rest.astype(BF16)
    low = (rest - mid.astype(F32)).astype(BF16)
    return hi, mid, low


def rank_of(onehot):
    count = onehot.shape[1]
    earlier = (iota((count, count), 0) < iota((count, count), 1)).astype(F32)
    before = dot_nn(onehot, earlier)
    return jnp.sum(onehot * before, axis=0, keepdims=True).astype(jnp.int32)


def pack_edges(planes):
    lane = iota((8, CY), 1)
    packed = jnp.zeros((8, CY), F32)
    for zv in range(ZV):
        for p, plane in enumerate(planes):
            q = zv * len(planes) + p
            turned = pltpu.roll(plane[zv * 8 : zv * 8 + 8], 2 * q + 1, 1)
            packed = jnp.where(lax.shift_right_logical(lane, 1) == q, turned, packed)
    return packed


def unpack_edges(left, right, number):
    lane = iota((8, CY), 1)
    both = jnp.where((lane & 1) == 0, pltpu.roll(right, CY - 1, 1), pltpu.roll(left, 1, 1))
    planes = []
    for p in range(number):
        parts = [
            pltpu.roll(both, CY - (2 * (zv * number + p) + 1), 1) for zv in range(ZV)
        ]
        planes.append(jnp.concatenate(parts, axis=0))
    return planes


def beside_y(plane, halo):
    lane = iota(plane.shape, 1)
    above = jnp.where(lane == CY - 1, halo, pltpu.roll(plane, CY - 1, 1))
    below = jnp.where(lane == 0, halo, pltpu.roll(plane, 1, 1))
    return above, below


def whole_kernel(
    gxn,
    gyn,
    c0_h,
    kap_h,
    vel_h,
    tgt_h,
    cell_r,
    own_r,
    obs_r,
    ablk_r,
    aown_r,
    ctl_r,
    foot_r,
    out_c,
    out_s,
    out_g,
    fields,
    kap,
    velx,
    velyz,
    tgt,
    cof_f,
    cof_a,
    src,
    cnt,
    obsf,
    summed,
    act_o,
    act_i,
    sen_o,
    sen_i,
    sn2_o,
    sn2_i,
    edge_o,
    edge_l,
    edge_r,
    grad_o,
    grad_i,
    loc_sem,
    xs_sem,
    xr_sem,
    es_sem,
    er_sem,
    as_sem,
    ar_sem,
    ss_sem,
    sr_sem,
    ts_sem,
    tr_sem,
    gs_sem,
    gr_sem,
):
    me_x = lax.axis_index("gx")
    me_y = lax.axis_index("gy")
    lg_y = gyn.bit_length() - 1
    mid = slice(Z0, Z0 + NZ)

    loads = [
        pltpu.make_async_copy(c0_h, fields.at[0, :, 1 : 1 + CX, mid, :], loc_sem.at[0]),
        pltpu.make_async_copy(kap_h, kap.at[1 : 1 + CX, mid, :], loc_sem.at[1]),
        pltpu.make_async_copy(vel_h.at[0], velx.at[1 : 1 + CX, mid, :], loc_sem.at[2]),
        pltpu.make_async_copy(vel_h.at[1:3], velyz.at[:, :, mid, :], loc_sem.at[3]),
        pltpu.make_async_copy(tgt_h, tgt, loc_sem.at[4]),
    ]
    for load in loads:
        load.start()

    barrier = pltpu.get_barrier_semaphore()

    @pl.loop(1, gyn)
    def _(t):
        pl.semaphore_signal(
            barrier, inc=1, device_id=(me_x, lax.rem(me_y + t, gyn)), device_id_type=MESH
        )

    @pl.loop(1, gxn)
    def _(t):
        pl.semaphore_signal(
            barrier, inc=1, device_id=(lax.rem(me_x + t, gxn), me_y), device_id_type=MESH
        )

    rows = gyn * 8
    acts = aown_r.shape[1]
    aown = aown_r[...]
    slot_row = iota((rows, acts), 0)
    arank = rank_of((iota((gyn, acts), 0) == aown).astype(F32))
    to_tile = lax.shift_right_logical(slot_row, 3) == aown
    pick_foot = (to_tile & ((slot_row & 7) == arank)).astype(F32)
    pick_meta = (to_tile & ((slot_row & 7) == arank + 4)).astype(F32)
    meta_row = iota((CY, acts), 0)
    meta = jnp.where(
        meta_row == 0,
        ablk_r[...].astype(F32) + 1.0,
        jnp.where(
            meta_row == 1, ctl_r[0:1, :], jnp.where(meta_row == 2, ctl_r[1:2, :], 0.0)
        ),
    )
    act_o[...] = dot_nn(pick_foot, foot_r[...], HIGH) + dot_nt(pick_meta, meta, HIGH)

    sens = own_r.shape[1]
    owner = own_r[...]
    spot = (owner & (gyn - 1)) * 8 + lax.shift_right_logical(owner, lg_y)
    pick_sens = (iota((rows, sens), 0) == spot).astype(F32)
    srank = rank_of(pick_sens)
    datum = jnp.concatenate(
        [
            cell_r[...].astype(F32) + 1.0,
            obs_r[0],
            obs_r[1],
            jnp.zeros((7, sens), F32),
        ],
        axis=0,
    )
    spread = [jnp.where(srank == k, datum, 0.0) for k in range(4)]
    spread.append(jnp.zeros((64, sens), F32))
    sen_o[...] = dot_nt(pick_sens, jnp.concatenate(spread, axis=0), HIGH)

    zero_rows = jnp.zeros((8, CY), F32)
    for slot in range(8):
        for s in range(2):
            for x in range(1, 1 + CX):
                fields[slot, s, x, 0:8, :] = zero_rows
                fields[slot, s, x, Z0 + NZ : PZ, :] = zero_rows
    for x in range(1, 1 + CX):
        kap[x, 0:8, :] = zero_rows
        kap[x, Z0 + NZ : PZ, :] = zero_rows
        velyz[1, x - 1, 0:8, :] = zero_rows
        velyz[1, x - 1, Z0 + NZ : PZ, :] = zero_rows
    zero_plane = jnp.zeros((NZ, CY), F32)

    def zero_side(x):
        for slot in range(8):
            for s in range(2):
                fields[slot, s, x, mid, :] = zero_plane
        kap[x, mid, :] = zero_plane
        velx[x, mid, :] = zero_plane

    @pl.when(me_x == 0)
    def _():
        zero_side(0)

    @pl.when(me_x == gxn - 1)
    def _():
        zero_side(CX + 1)

    @pl.when(me_y == 0)
    def _():
        edge_l[...] = jnp.zeros_like(edge_l)

    @pl.when(me_y == gyn - 1)
    def _():
        edge_r[...] = jnp.zeros_like(edge_r)

    for load in loads[:4]:
        load.wait()

    state_planes = [fields[0, s, 1 + x, mid, :] for s in range(2) for x in range(CX)]
    edge_o[0] = pack_edges(state_planes)
    coef_planes = [kap[1 + x, mid, :] for x in range(CX)]
    coef_planes += [velyz[0, x, mid, :] for x in range(CX)]
    edge_o[8] = pack_edges(coef_planes)

    pl.semaphore_wait(barrier, gyn - 1 + gxn - 1)

    def to_peer_y(source, sink, send, recv):
        def make(t):
            there = lax.rem(me_y + t, gyn)
            return pltpu.make_async_remote_copy(
                src_ref=source(there),
                dst_ref=sink(me_y),
                send_sem=send.at[t],
                recv_sem=recv.at[t],
                device_id=(me_x, there),
                device_id_type=MESH,
            )

        return make

    def of_peer_y(source, sink, send, recv):
        def make(t):
            there = lax.rem(me_y + gyn - t, gyn)
            return pltpu.make_async_remote_copy(
                src_ref=source(there),
                dst_ref=sink(there),
                send_sem=send.at[t],
                recv_sem=recv.at[t],
                device_id=(me_x, there),
                device_id_type=MESH,
            )

        return make

    def tile_of(ref):
        return lambda d: ref.at[pl.ds(pl.multiple_of(d * 8, 8), 8), :]

    act_to = to_peer_y(tile_of(act_o), tile_of(act_i), as_sem, ar_sem)
    act_of = of_peer_y(tile_of(act_o), tile_of(act_i), as_sem, ar_sem)
    sen_to = to_peer_y(tile_of(sen_o), tile_of(sen_i), ss_sem, sr_sem)
    sen_of = of_peer_y(tile_of(sen_o), tile_of(sen_i), ss_sem, sr_sem)
    same = lambda d: grad_o
    grad_to = to_peer_y(same, tile_of(grad_i), gs_sem, gr_sem)
    grad_of = of_peer_y(same, tile_of(grad_i), gs_sem, gr_sem)

    def edge_copy(slot, side):
        there = me_y - 1 if side == 0 else me_y + 1
        sink = edge_r if side == 0 else edge_l
        return pltpu.make_async_remote_copy(
            src_ref=edge_o.at[slot],
            dst_ref=sink.at[slot],
            send_sem=es_sem.at[slot, side],
            recv_sem=er_sem.at[slot, side],
            device_id=(me_x, there),
            device_id_type=MESH,
        )

    def x_copy(slot, side):
        there = me_x - 1 if side == 0 else me_x + 1
        sink = CX + 1 if side == 0 else 0
        own = 0 if side == 0 else CX - 1
        if slot == 0:
            source = c0_h.at[:, own]
            dest = fields.at[0, :, sink, mid, :]
        elif slot < 8:
            source = fields.at[slot, :, own + 1, mid, :]
            dest = fields.at[slot, :, sink, mid, :]
        elif slot == 8:
            source = kap_h.at[own]
            dest = kap.at[sink, mid, :]
        else:
            source = vel_h.at[0, own]
            dest = velx.at[sink, mid, :]
        return pltpu.make_async_remote_copy(
            src_ref=source,
            dst_ref=dest,
            send_sem=xs_sem.at[slot, side],
            recv_sem=xr_sem.at[slot, side],
            device_id=(there, me_y),
            device_id_type=MESH,
        )

    has = (
        (me_x > 0, me_x < gxn - 1),
        (me_y > 0, me_y < gyn - 1),
    )

    def both_sides(maker, axis, action, slots):
        for side in (0, 1):

            @pl.when(has[axis][side])
            def _(side=side):
                for slot in slots:
                    action(maker(slot, side))

    def start(copy):
        copy.start()

    def wait_send(copy):
        copy.wait_send()

    def wait_recv_x(slots):
        for side in (0, 1):

            @pl.when(has[0][1 - side])
            def _(side=side):
                for slot in slots:
                    x_copy(slot, side).wait_recv()

    def wait_recv_e(slots):
        for side in (0, 1):

            @pl.when(has[1][1 - side])
            def _(side=side):
                for slot in slots:
                    edge_copy(slot, side).wait_recv()

    @pl.loop(1, gyn)
    def _(t):
        act_to(t).start()

    both_sides(edge_copy, 1, start, (8, 0))
    both_sides(x_copy, 0, start, (8, 9, 0))

    @pl.loop(1, gyn)
    def _(t):
        sen_to(t).start()

    own_tile = pl.ds(pl.multiple_of(me_y * 8, 8), 8)
    act_i[own_tile, :] = act_o[own_tile, :]
    sen_i[own_tile, :] = sen_o[own_tile, :]

    wait_recv_x((8, 9))
    wait_recv_e((8,))
    halos = unpack_edges(edge_l[8], edge_r[8], 2 * CX)
    for x in range(CX):
        here = kap[1 + x, mid, :]
        kyp, kym = beside_y(here, halos[x])
        around = (
            kap[2 + x, mid, :],
            kap[x, mid, :],
            kyp,
            kym,
            kap[1 + x, Z0 + 1 : Z0 + NZ + 1, :],
            kap[1 + x, Z0 - 1 : Z0 + NZ - 1, :],
        )
        faces = [0.5 * (here + other) for other in around]
        total = faces[0] + faces[1] + faces[2] + faces[3] + faces[4] + faces[5]
        uy = velyz[0, x, mid, :]
        uyp, uym = beside_y(uy, halos[CX + x])
        ux = velx[1 + x, mid, :]
        uz = velyz[1, x, mid, :]
        drift_f = (-0.5 * ux, 0.5 * ux, -0.5 * uy, 0.5 * uy, -0.5 * uz, 0.5 * uz)
        drift_a = (
            0.5 * velx[2 + x, mid, :],
            -0.5 * velx[x, mid, :],
            0.5 * uyp,
            -0.5 * uym,
            0.5 * velyz[1, x, Z0 + 1 : Z0 + NZ + 1, :],
            -0.5 * velyz[1, x, Z0 - 1 : Z0 + NZ - 1, :],
        )
        for s in range(2):
            scale = SCALES[s]
            cof_f[s, 6, x] = 1.0 - scale * total
            for f in range(6):
                scaled = faces[f] if s == 0 else scale * faces[f]
                cof_f[s, f, x] = scaled + drift_f[f]
                cof_a[s, f, x] = scaled + drift_a[f]

    def stencil(slot, cof, s, x, halo):
        here = fields[slot, s, 1 + x, mid, :]
        yp, ym = beside_y(here, halo)
        return (
            cof_f[s, 6, x] * here
            + cof[s, 0, x] * fields[slot, s, 2 + x, mid, :]
            + cof[s, 1, x] * fields[slot, s, x, mid, :]
            + cof[s, 2, x] * yp
            + cof[s, 3, x] * ym
            + cof[s, 4, x] * fields[slot, s, 1 + x, Z0 + 1 : Z0 + NZ + 1, :]
            + cof[s, 5, x] * fields[slot, s, 1 + x, Z0 - 1 : Z0 + NZ - 1, :]
        )

    def send_field(slot):
        planes = [fields[slot, s, 1 + x, mid, :] for s in range(2) for x in range(CX)]
        edge_o[slot] = pack_edges(planes)
        both_sides(edge_copy, 1, start, (slot,))
        both_sides(x_copy, 0, start, (slot,))

    def take_field(slot):
        wait_recv_x((slot,))
        wait_recv_e((slot,))
        return unpack_edges(edge_l[slot], edge_r[slot], 2 * CX)

    halos = take_field(0)
    for s in range(2):
        for x in range(CX):
            fields[1, s, 1 + x, mid, :] = stencil(0, cof_f, s, x, halos[s * CX + x])

    @pl.loop(1, gyn)
    def _(t):
        act_of(t).wait_recv()

    got = act_i[...]
    moved = pltpu.roll(got, rows - 4, 0)
    sel = (iota((8, CY), 0) == iota((8, CY), 1)).astype(F32)
    metas = dot_nt(sel, moved, HIGH)
    blk_row = (metas[0:1] + 0.5).astype(jnp.int32) - 1
    live_row = ((iota((1, rows), 1) & 7) < 4) & (blk_row >= 0)
    bz_row = jnp.where(live_row, lax.shift_right_arithmetic(blk_row, 5), -1)
    blk_col = (moved[:, 0:1] + 0.5).astype(jnp.int32) - 1
    live_col = ((iota((rows, 1), 0) & 7) < 4) & (blk_col >= 0)
    first_y = jnp.where(live_col, (blk_col & 31) * FY, -8)
    at_y = [(iota((rows, CY), 1) == first_y + fy).astype(F32) for fy in range(FY)]
    perm_row = iota((CY, CY), 0)
    perm = (
        iota((CY, CY), 1) == (perm_row & 31) * FY + lax.shift_right_logical(perm_row, 5)
    ).astype(F32)
    foot_t = dot_nt(perm, got, HIGH)
    weights = [
        jnp.where(bz_row == bz, metas[1 + s : 2 + s], 0.0)
        for s in range(2)
        for bz in range(BZ)
    ]
    placed = jnp.zeros((2 * BZ * 32, CY), F32)
    for fy in range(FY):
        part = foot_t[fy * 32 : fy * 32 + 32]
        left = jnp.concatenate([part * w for w in weights], axis=0)
        placed = placed + dot_nn(left, at_y[fy], HIGH)
    for s in range(2):
        for bz in range(BZ):
            for fx in range(FX):
                row = (s * BZ + bz) * 32 + fx * 8
                src[s, fx, bz * 8 : bz * 8 + 8, :] = placed[row : row + 8]

    for s in range(2):
        for x in range(CX):
            fields[1, s, 1 + x, mid, :] = fields[1, s, 1 + x, mid, :] + src[s, x]
    send_field(1)

    @pl.loop(1, gyn)
    def _(t):
        sen_of(t).wait_recv()

    for d in range(gxn):
        sn2_o[d] = sen_i[pl.ds(d, gyn, stride=8), :]

    def sn2_copy(t, sending):
        there = lax.rem(me_x + t, gxn) if sending else lax.rem(me_x + gxn - t, gxn)
        return pltpu.make_async_remote_copy(
            src_ref=sn2_o.at[there],
            dst_ref=sn2_i.at[me_x] if sending else sn2_i.at[there],
            send_sem=ts_sem.at[t],
            recv_sem=tr_sem.at[t],
            device_id=(there, me_y),
            device_id_type=MESH,
        )

    @pl.loop(1, gxn)
    def _(t):
        sn2_copy(t, True).start()

    sn2_i[me_x] = sn2_o[me_x]

    def step_forward(slot, sink):
        halos = take_field(slot)
        for s in range(2):
            for x in range(CX):
                sink(s, x, stencil(slot, cof_f, s, x, halos[s * CX + x]) + src[s, x])

    def into(slot):
        def put(s, x, value):
            fields[slot, s, 1 + x, mid, :] = value

        return put

    step_forward(1, into(2))
    send_field(2)

    @pl.loop(1, gxn)
    def _(t):
        sn2_copy(t, False).wait_recv()

    records = jnp.concatenate([sn2_i[d] for d in range(gxn)], axis=0)
    many = records.shape[0]
    sel = (iota((8, CY), 0) * 16 == iota((8, CY), 1)).astype(F32)
    cell_rows = (dot_nt(sel, records, HIGH) + 0.5).astype(jnp.int32) - 1
    zx = lax.shift_right_arithmetic(cell_rows, 7)
    pick_zx = jnp.concatenate(
        [(iota((CX * NZ, many), 0) == zx[k : k + 1]).astype(BF16) for k in range(4)], axis=1
    )
    at_lane = []
    for k in range(4):
        cell_col = (records[:, 16 * k : 16 * k + 1] + 0.5).astype(jnp.int32) - 1
        lane = jnp.where(cell_col >= 0, cell_col & (CY - 1), -1)
        at_lane.append(iota((many, CY), 1) == lane)
    cnt[...] = dot_nn(
        pick_zx, jnp.concatenate([a.astype(F32).astype(BF16) for a in at_lane], axis=0)
    )
    for ch in range(2 * STEPS):
        values = jnp.concatenate(
            [
                jnp.where(at_lane[k], records[:, 16 * k + 1 + ch : 16 * k + 2 + ch], 0.0)
                for k in range(4)
            ],
            axis=0,
        )
        hi, mid_part, low = split3(values)
        obsf[ch] = (dot_nn(pick_zx, hi) + dot_nn(pick_zx, mid_part)) + dot_nn(pick_zx, low)

    step_forward(2, into(3))
    send_field(3)

    def forcing(state, s, x, n):
        span = slice(x * NZ, x * NZ + NZ)
        return cnt[span] * state - obsf[s * STEPS + n - 1, span]

    loads[4].wait()

    def last(s, x, value):
        out_c[s, x] = value
        adj = value - tgt[s, x] + forcing(value, s, x, 4)
        fields[4, s, 1 + x, mid, :] = adj
        summed[s, x] = adj

    step_forward(3, last)
    send_field(4)

    for n in (3, 2, 1):
        slot = 7 - n
        halos = take_field(slot)
        for s in range(2):
            for x in range(CX):
                adj = stencil(slot, cof_a, s, x, halos[s * CX + x]) + forcing(
                    fields[n, s, 1 + x, mid, :], s, x, n
                )
                fields[slot + 1, s, 1 + x, mid, :] = adj
                summed[s, x] = summed[s, x] + adj
        send_field(slot + 1)

    stacked = jnp.concatenate(
        [
            summed[s, fx, bz * 8 : bz * 8 + 8, :]
            for s in range(2)
            for bz in range(BZ)
            for fx in range(FX)
        ],
        axis=0,
    )
    totals = [jnp.zeros((32, rows), F32) for _ in range(2)]
    picked = [dot_nt(stacked, at_y[fy], HIGH) for fy in range(FY)]
    for s in range(2):
        for bz in range(BZ):
            base = (s * BZ + bz) * 32
            part = jnp.zeros((32, rows), F32)
            for fy in range(FY):
                part = part + foot_t[fy * 32 : fy * 32 + 32] * picked[fy][base : base + 32]
            totals[s] = totals[s] + jnp.where(bz_row == bz, part, 0.0)
    sums = [jnp.sum(t, axis=0, keepdims=True) for t in totals]
    if rows < CY:
        sums = [jnp.concatenate([v, jnp.zeros((1, CY - rows), F32)], axis=1) for v in sums]
    grad_o[...] = jnp.concatenate(sums + [jnp.zeros((6, CY), F32)], axis=0)

    @pl.loop(1, gyn)
    def _(t):
        grad_to(t).start()

    grad_i[own_tile, :] = grad_o[...]

    halos = take_field(7)
    for s in range(2):
        for x in range(CX):
            out_s[s, x] = stencil(7, cof_a, s, x, halos[s * CX + x])

    @pl.loop(1, gyn)
    def _(t):
        grad_of(t).wait_recv()

    pick_lane = (iota((CY, acts), 0) == me_y * 8 + arank).astype(F32)
    brought = dot_nn(grad_i[...], pick_lane, HIGH)
    mine = jnp.where(to_tile, brought, 0.0)
    for s in range(2):
        out_g[s : s + 1, :] = jnp.sum(
            jnp.where((slot_row & 7) == s, mine, 0.0), axis=0, keepdims=True
        )

    both_sides(edge_copy, 1, wait_send, range(9))
    both_sides(x_copy, 0, wait_send, range(10))

    @pl.loop(1, gyn)
    def _(t):
        act_to(t).wait_send()
        sen_to(t).wait_send()
        grad_to(t).wait_send()

    @pl.loop(1, gxn)
    def _(t):
        sn2_copy(t, True).wait_send()


def per_device(
    gxn,
    gyn,
    initial_state,
    eddy_diffusivity,
    velocity,
    target,
    sensor_cell,
    sensor_owner,
    observations,
    actuator_block,
    actuator_owner,
    controls,
    footprint,
):
    sens = sensor_cell.shape[0]
    acts = actuator_block.shape[0]
    rows = gyn * 8
    hbm = pl.BlockSpec(memory_space=pl.ANY)
    vmem = pl.BlockSpec(memory_space=pltpu.VMEM)
    dma = pltpu.SemaphoreType.DMA
    big = jax.ShapeDtypeStruct((2, CX, NZ, CY), F32)
    state, sensitivity, gradient = pl.pallas_call(
        functools.partial(whole_kernel, gxn, gyn),
        out_shape=(big, big, jax.ShapeDtypeStruct((2, acts), F32)),
        in_specs=[hbm] * 4 + [vmem] * 7,
        out_specs=(vmem, vmem, vmem),
        scratch_shapes=[
            pltpu.VMEM((8, 2, CX + 2, PZ, CY), F32),
            pltpu.VMEM((CX + 2, PZ, CY), F32),
            pltpu.VMEM((CX + 2, PZ, CY), F32),
            pltpu.VMEM((2, CX, PZ, CY), F32),
            pltpu.VMEM((2, CX, NZ, CY), F32),
            pltpu.VMEM((2, 7, CX, NZ, CY), F32),
            pltpu.VMEM((2, 6, CX, NZ, CY), F32),
            pltpu.VMEM((2, CX, NZ, CY), F32),
            pltpu.VMEM((CX * NZ, CY), F32),
            pltpu.VMEM((2 * STEPS, CX * NZ, CY), F32),
            pltpu.VMEM((2, CX, NZ, CY), F32),
            pltpu.VMEM((rows, CY), F32),
            pltpu.VMEM((rows, CY), F32),
            pltpu.VMEM((rows, CY), F32),
            pltpu.VMEM((rows, CY), F32),
            pltpu.VMEM((gxn, gyn, CY), F32),
            pltpu.VMEM((gxn, gyn, CY), F32),
            pltpu.VMEM((9, 8, CY), F32),
            pltpu.VMEM((9, 8, CY), F32),
            pltpu.VMEM((9, 8, CY), F32),
            pltpu.VMEM((8, CY), F32),
            pltpu.VMEM((rows, CY), F32),
            dma((5,)),
            dma((10, 2)),
            dma((10, 2)),
            dma((9, 2)),
            dma((9, 2)),
            dma((gyn,)),
            dma((gyn,)),
            dma((gyn,)),
            dma((gyn,)),
            dma((gxn,)),
            dma((gxn,)),
            dma((gyn,)),
            dma((gyn,)),
        ],
        compiler_params=pltpu.CompilerParams(
            collective_id=0, has_side_effects=True, vmem_limit_bytes=48 * 1024 * 1024
        ),
        name="whole",
    )(
        initial_state,
        eddy_diffusivity,
        velocity,
        target,
        sensor_cell.reshape(1, sens),
        sensor_owner.reshape(1, sens),
        jnp.transpose(observations, (1, 2, 0)),
        actuator_block.reshape(1, acts),
        actuator_owner.reshape(1, acts),
        controls.T,
        footprint,
    )
    return state, sensitivity, gradient.T


def solution(mesh):
    in_specs = (
        P(None, "gx", None, "gy"),
        P("gx", None, "gy"),
        P(None, "gx", None, "gy"),
        P(None, "gx", None, "gy"),
        P(("gx", "gy")),
        P(("gx", "gy"), None),
        P(("gx", "gy"), None, None),
        P(("gx", "gy")),
        P(("gx", "gy"), None),
        P(("gx", "gy"), None),
        P(("gx", "gy"), None),
    )
    out_specs = (P(None, "gx", None, "gy"), P(None, "gx", None, "gy"), P(("gx", "gy"), None))
    return jax.shard_map(
        functools.partial(per_device, mesh.shape["gx"], mesh.shape["gy"]),
        mesh=mesh,
        in_specs=in_specs,
        out_specs=out_specs,
        check_vma=False,
    )
```

```python
import functools

import jax
import jax.numpy as jnp
from jax import lax
from jax.experimental import pallas as pl
from jax.experimental.pallas import tpu as pltpu
from jax.sharding import PartitionSpec as P

MESH = pl.DeviceIdType.MESH
F32 = jnp.float32
BF16 = jnp.bfloat16
HIGH = lax.Precision.HIGHEST

CX = 4
NZ = 48
CY = 128
FX = 4
FZ = 8
FY = 4
BZ = NZ // FZ
STEPS = 4
ZV = NZ // 8
PZ = NZ + 16
Z0 = 8
prandtl = 0.85
SCALES = (1.0, 1.0 / prandtl)


def iota(shape, dim):
    return lax.broadcasted_iota(jnp.int32, shape, dim)


def dot_nn(a, b, precision=None):
    return lax.dot_general(
        a, b, (((1,), (0,)), ((), ())), precision=precision, preferred_element_type=F32
    )


def dot_nt(a, b, precision=None):
    return lax.dot_general(
        a, b, (((1,), (1,)), ((), ())), precision=precision, preferred_element_type=F32
    )


def split3(x):
    hi = x.astype(BF16)
    rest = x - hi.astype(F32)
    mid = rest.astype(BF16)
    low = (rest - mid.astype(F32)).astype(BF16)
    return hi, mid, low


def rank_of(onehot):
    count = onehot.shape[1]
    earlier = (iota((count, count), 0) < iota((count, count), 1)).astype(F32)
    before = dot_nn(onehot, earlier)
    return jnp.sum(onehot * before, axis=0, keepdims=True).astype(jnp.int32)


def pack_edges(planes):
    lane = iota((8, CY), 1)
    packed = jnp.zeros((8, CY), F32)
    for zv in range(ZV):
        for p, plane in enumerate(planes):
            q = zv * len(planes) + p
            turned = pltpu.roll(plane[zv * 8 : zv * 8 + 8], 2 * q + 1, 1)
            packed = jnp.where(lax.shift_right_logical(lane, 1) == q, turned, packed)
    return packed


def unpack_edges(left, right, number):
    lane = iota((8, CY), 1)
    both = jnp.where((lane & 1) == 0, pltpu.roll(right, CY - 1, 1), pltpu.roll(left, 1, 1))
    planes = []
    for p in range(number):
        parts = [
            pltpu.roll(both, CY - (2 * (zv * number + p) + 1), 1) for zv in range(ZV)
        ]
        planes.append(jnp.concatenate(parts, axis=0))
    return planes


def beside_y(plane, halo):
    lane = iota(plane.shape, 1)
    above = jnp.where(lane == CY - 1, halo, pltpu.roll(plane, CY - 1, 1))
    below = jnp.where(lane == 0, halo, pltpu.roll(plane, 1, 1))
    return above, below


def whole_kernel(
    gxn,
    gyn,
    c0_h,
    kap_h,
    vel_h,
    tgt_h,
    cell_h,
    own_h,
    obs_h,
    ablk_h,
    aown_h,
    ctl_h,
    foot_h,
    out_c,
    out_s,
    out_g,
    cell_r,
    own_r,
    obs_r,
    ablk_r,
    aown_r,
    ctl_r,
    foot_r,
    fields,
    kap,
    velx,
    velyz,
    tgt,
    cof_f,
    cof_a,
    src,
    cnt,
    obsf,
    summed,
    act_o,
    act_i,
    sen_o,
    sen_i,
    sn2_o,
    sn2_i,
    edge_o,
    edge_l,
    edge_r,
    grad_o,
    grad_i,
    loc_sem,
    xs_sem,
    xr_sem,
    es_sem,
    er_sem,
    as_sem,
    ar_sem,
    ss_sem,
    sr_sem,
    ts_sem,
    tr_sem,
    gs_sem,
    gr_sem,
):
    me_x = lax.axis_index("gx")
    me_y = lax.axis_index("gy")
    lg_y = gyn.bit_length() - 1
    mid = slice(Z0, Z0 + NZ)

    smalls = [
        pltpu.make_async_copy(source, sink, loc_sem.at[5 + i])
        for i, (source, sink) in enumerate(
            (
                (aown_h, aown_r),
                (ablk_h, ablk_r),
                (ctl_h, ctl_r),
                (foot_h, foot_r),
                (own_h, own_r),
                (cell_h, cell_r),
                (obs_h, obs_r),
            )
        )
    ]
    for load in smalls:
        load.start()
    loads = [
        pltpu.make_async_copy(c0_h, fields.at[0, :, 1 : 1 + CX, mid, :], loc_sem.at[0]),
        pltpu.make_async_copy(kap_h, kap.at[1 : 1 + CX, mid, :], loc_sem.at[1]),
        pltpu.make_async_copy(vel_h.at[0], velx.at[1 : 1 + CX, mid, :], loc_sem.at[2]),
        pltpu.make_async_copy(vel_h.at[1:3], velyz.at[:, :, mid, :], loc_sem.at[3]),
        pltpu.make_async_copy(tgt_h, tgt, loc_sem.at[4]),
    ]
    for load in loads:
        load.start()

    barrier = pltpu.get_barrier_semaphore()

    @pl.loop(1, gyn)
    def _(t):
        pl.semaphore_signal(
            barrier, inc=1, device_id=(me_x, lax.rem(me_y + t, gyn)), device_id_type=MESH
        )

    @pl.loop(1, gxn)
    def _(t):
        pl.semaphore_signal(
            barrier, inc=1, device_id=(lax.rem(me_x + t, gxn), me_y), device_id_type=MESH
        )

    for load in smalls:
        load.wait()
    rows = gyn * 8
    acts = aown_r.shape[1]
    aown = aown_r[...]
    slot_row = iota((rows, acts), 0)
    arank = rank_of((iota((gyn, acts), 0) == aown).astype(F32))
    to_tile = lax.shift_right_logical(slot_row, 3) == aown
    pick_foot = (to_tile & ((slot_row & 7) == arank)).astype(F32)
    pick_meta = (to_tile & ((slot_row & 7) == arank + 4)).astype(F32)
    meta_row = iota((CY, acts), 0)
    meta = jnp.where(
        meta_row == 0,
        ablk_r[...].astype(F32) + 1.0,
        jnp.where(
            meta_row == 1, ctl_r[0:1, :], jnp.where(meta_row == 2, ctl_r[1:2, :], 0.0)
        ),
    )
    act_o[...] = dot_nn(pick_foot, foot_r[...], HIGH) + dot_nt(pick_meta, meta, HIGH)

    sens = own_r.shape[1]
    owner = own_r[...]
    spot = (owner & (gyn - 1)) * 8 + lax.shift_right_logical(owner, lg_y)
    pick_sens = (iota((rows, sens), 0) == spot).astype(F32)
    srank = rank_of(pick_sens)
    datum = jnp.concatenate(
        [
            cell_r[...].astype(F32) + 1.0,
            obs_r[0],
            obs_r[1],
            jnp.zeros((7, sens), F32),
        ],
        axis=0,
    )
    spread = [jnp.where(srank == k, datum, 0.0) for k in range(4)]
    spread.append(jnp.zeros((64, sens), F32))
    sen_o[...] = dot_nt(pick_sens, jnp.concatenate(spread, axis=0), HIGH)

    zero_rows = jnp.zeros((8, CY), F32)
    for slot in range(8):
        for s in range(2):
            for x in range(1, 1 + CX):
                fields[slot, s, x, 0:8, :] = zero_rows
                fields[slot, s, x, Z0 + NZ : PZ, :] = zero_rows
    for x in range(1, 1 + CX):
        kap[x, 0:8, :] = zero_rows
        kap[x, Z0 + NZ : PZ, :] = zero_rows
        velyz[1, x - 1, 0:8, :] = zero_rows
        velyz[1, x - 1, Z0 + NZ : PZ, :] = zero_rows
    zero_plane = jnp.zeros((NZ, CY), F32)

    def zero_side(x):
        for slot in range(8):
            for s in range(2):
                fields[slot, s, x, mid, :] = zero_plane
        kap[x, mid, :] = zero_plane
        velx[x, mid, :] = zero_plane

    @pl.when(me_x == 0)
    def _():
        zero_side(0)

    @pl.when(me_x == gxn - 1)
    def _():
        zero_side(CX + 1)

    @pl.when(me_y == 0)
    def _():
        edge_l[...] = jnp.zeros_like(edge_l)

    @pl.when(me_y == gyn - 1)
    def _():
        edge_r[...] = jnp.zeros_like(edge_r)

    for load in loads[:4]:
        load.wait()

    state_planes = [fields[0, s, 1 + x, mid, :] for s in range(2) for x in range(CX)]
    edge_o[0] = pack_edges(state_planes)
    coef_planes = [kap[1 + x, mid, :] for x in range(CX)]
    coef_planes += [velyz[0, x, mid, :] for x in range(CX)]
    edge_o[8] = pack_edges(coef_planes)

    pl.semaphore_wait(barrier, gyn - 1 + gxn - 1)

    def to_peer_y(source, sink, send, recv):
        def make(t):
            there = lax.rem(me_y + t, gyn)
            return pltpu.make_async_remote_copy(
                src_ref=source(there),
                dst_ref=sink(me_y),
                send_sem=send.at[t],
                recv_sem=recv.at[t],
                device_id=(me_x, there),
                device_id_type=MESH,
            )

        return make

    def of_peer_y(source, sink, send, recv):
        def make(t):
            there = lax.rem(me_y + gyn - t, gyn)
            return pltpu.make_async_remote_copy(
                src_ref=source(there),
                dst_ref=sink(there),
                send_sem=send.at[t],
                recv_sem=recv.at[t],
                device_id=(me_x, there),
                device_id_type=MESH,
            )

        return make

    def tile_of(ref):
        return lambda d: ref.at[pl.ds(pl.multiple_of(d * 8, 8), 8), :]

    act_to = to_peer_y(tile_of(act_o), tile_of(act_i), as_sem, ar_sem)
    act_of = of_peer_y(tile_of(act_o), tile_of(act_i), as_sem, ar_sem)
    sen_to = to_peer_y(tile_of(sen_o), tile_of(sen_i), ss_sem, sr_sem)
    sen_of = of_peer_y(tile_of(sen_o), tile_of(sen_i), ss_sem, sr_sem)
    same = lambda d: grad_o
    grad_to = to_peer_y(same, tile_of(grad_i), gs_sem, gr_sem)
    grad_of = of_peer_y(same, tile_of(grad_i), gs_sem, gr_sem)

    def edge_copy(slot, side):
        there = me_y - 1 if side == 0 else me_y + 1
        sink = edge_r if side == 0 else edge_l
        return pltpu.make_async_remote_copy(
            src_ref=edge_o.at[slot],
            dst_ref=sink.at[slot],
            send_sem=es_sem.at[slot, side],
            recv_sem=er_sem.at[slot, side],
            device_id=(me_x, there),
            device_id_type=MESH,
        )

    def x_copy(slot, side):
        there = me_x - 1 if side == 0 else me_x + 1
        sink = CX + 1 if side == 0 else 0
        own = 0 if side == 0 else CX - 1
        if slot == 0:
            source = c0_h.at[:, own]
            dest = fields.at[0, :, sink, mid, :]
        elif slot < 8:
            source = fields.at[slot, :, own + 1, mid, :]
            dest = fields.at[slot, :, sink, mid, :]
        elif slot == 8:
            source = kap_h.at[own]
            dest = kap.at[sink, mid, :]
        else:
            source = vel_h.at[0, own]
            dest = velx.at[sink, mid, :]
        return pltpu.make_async_remote_copy(
            src_ref=source,
            dst_ref=dest,
            send_sem=xs_sem.at[slot, side],
            recv_sem=xr_sem.at[slot, side],
            device_id=(there, me_y),
            device_id_type=MESH,
        )

    has = (
        (me_x > 0, me_x < gxn - 1),
        (me_y > 0, me_y < gyn - 1),
    )

    def both_sides(maker, axis, action, slots):
        for side in (0, 1):

            @pl.when(has[axis][side])
            def _(side=side):
                for slot in slots:
                    action(maker(slot, side))

    def start(copy):
        copy.start()

    def wait_send(copy):
        copy.wait_send()

    def wait_recv_x(slots):
        for side in (0, 1):

            @pl.when(has[0][1 - side])
            def _(side=side):
                for slot in slots:
                    x_copy(slot, side).wait_recv()

    def wait_recv_e(slots):
        for side in (0, 1):

            @pl.when(has[1][1 - side])
            def _(side=side):
                for slot in slots:
                    edge_copy(slot, side).wait_recv()

    @pl.loop(1, gyn)
    def _(t):
        act_to(t).start()

    both_sides(edge_copy, 1, start, (8, 0))
    both_sides(x_copy, 0, start, (8, 9, 0))

    @pl.loop(1, gyn)
    def _(t):
        sen_to(t).start()

    own_tile = pl.ds(pl.multiple_of(me_y * 8, 8), 8)
    act_i[own_tile, :] = act_o[own_tile, :]
    sen_i[own_tile, :] = sen_o[own_tile, :]

    wait_recv_x((8, 9))
    wait_recv_e((8,))
    halos = unpack_edges(edge_l[8], edge_r[8], 2 * CX)
    for x in range(CX):
        here = kap[1 + x, mid, :]
        kyp, kym = beside_y(here, halos[x])
        around = (
            kap[2 + x, mid, :],
            kap[x, mid, :],
            kyp,
            kym,
            kap[1 + x, Z0 + 1 : Z0 + NZ + 1, :],
            kap[1 + x, Z0 - 1 : Z0 + NZ - 1, :],
        )
        faces = [0.5 * (here + other) for other in around]
        total = faces[0] + faces[1] + faces[2] + faces[3] + faces[4] + faces[5]
        uy = velyz[0, x, mid, :]
        uyp, uym = beside_y(uy, halos[CX + x])
        ux = velx[1 + x, mid, :]
        uz = velyz[1, x, mid, :]
        drift_f = (-0.5 * ux, 0.5 * ux, -0.5 * uy, 0.5 * uy, -0.5 * uz, 0.5 * uz)
        drift_a = (
            0.5 * velx[2 + x, mid, :],
            -0.5 * velx[x, mid, :],
            0.5 * uyp,
            -0.5 * uym,
            0.5 * velyz[1, x, Z0 + 1 : Z0 + NZ + 1, :],
            -0.5 * velyz[1, x, Z0 - 1 : Z0 + NZ - 1, :],
        )
        for s in range(2):
            scale = SCALES[s]
            cof_f[s, 6, x] = 1.0 - scale * total
            for f in range(6):
                scaled = faces[f] if s == 0 else scale * faces[f]
                cof_f[s, f, x] = scaled + drift_f[f]
                cof_a[s, f, x] = scaled + drift_a[f]

    def stencil(slot, cof, s, x, halo):
        here = fields[slot, s, 1 + x, mid, :]
        yp, ym = beside_y(here, halo)
        return (
            cof_f[s, 6, x] * here
            + cof[s, 0, x] * fields[slot, s, 2 + x, mid, :]
            + cof[s, 1, x] * fields[slot, s, x, mid, :]
            + cof[s, 2, x] * yp
            + cof[s, 3, x] * ym
            + cof[s, 4, x] * fields[slot, s, 1 + x, Z0 + 1 : Z0 + NZ + 1, :]
            + cof[s, 5, x] * fields[slot, s, 1 + x, Z0 - 1 : Z0 + NZ - 1, :]
        )

    def send_field(slot):
        planes = [fields[slot, s, 1 + x, mid, :] for s in range(2) for x in range(CX)]
        edge_o[slot] = pack_edges(planes)
        both_sides(edge_copy, 1, start, (slot,))
        both_sides(x_copy, 0, start, (slot,))

    def take_field(slot):
        wait_recv_x((slot,))
        wait_recv_e((slot,))
        return unpack_edges(edge_l[slot], edge_r[slot], 2 * CX)

    halos = take_field(0)
    for s in range(2):
        for x in range(CX):
            fields[1, s, 1 + x, mid, :] = stencil(0, cof_f, s, x, halos[s * CX + x])

    @pl.loop(1, gyn)
    def _(t):
        act_of(t).wait_recv()

    got = act_i[...]
    moved = pltpu.roll(got, rows - 4, 0)
    sel = (iota((8, CY), 0) == iota((8, CY), 1)).astype(F32)
    metas = dot_nt(sel, moved, HIGH)
    blk_row = (metas[0:1] + 0.5).astype(jnp.int32) - 1
    live_row = ((iota((1, rows), 1) & 7) < 4) & (blk_row >= 0)
    bz_row = jnp.where(live_row, lax.shift_right_arithmetic(blk_row, 5), -1)
    blk_col = (moved[:, 0:1] + 0.5).astype(jnp.int32) - 1
    live_col = ((iota((rows, 1), 0) & 7) < 4) & (blk_col >= 0)
    first_y = jnp.where(live_col, (blk_col & 31) * FY, -8)
    at_y = [(iota((rows, CY), 1) == first_y + fy).astype(F32) for fy in range(FY)]
    perm_row = iota((CY, CY), 0)
    perm = (
        iota((CY, CY), 1) == (perm_row & 31) * FY + lax.shift_right_logical(perm_row, 5)
    ).astype(F32)
    foot_t = dot_nt(perm, got, HIGH)
    weights = [
        jnp.where(bz_row == bz, metas[1 + s : 2 + s], 0.0)
        for s in range(2)
        for bz in range(BZ)
    ]
    placed = jnp.zeros((2 * BZ * 32, CY), F32)
    for fy in range(FY):
        part = foot_t[fy * 32 : fy * 32 + 32]
        left = jnp.concatenate([part * w for w in weights], axis=0)
        placed = placed + dot_nn(left, at_y[fy], HIGH)
    for s in range(2):
        for bz in range(BZ):
            for fx in range(FX):
                row = (s * BZ + bz) * 32 + fx * 8
                src[s, fx, bz * 8 : bz * 8 + 8, :] = placed[row : row + 8]

    for s in range(2):
        for x in range(CX):
            fields[1, s, 1 + x, mid, :] = fields[1, s, 1 + x, mid, :] + src[s, x]
    send_field(1)

    @pl.loop(1, gyn)
    def _(t):
        sen_of(t).wait_recv()

    for d in range(gxn):
        sn2_o[d] = sen_i[pl.ds(d, gyn, stride=8), :]

    def sn2_copy(t, sending):
        there = lax.rem(me_x + t, gxn) if sending else lax.rem(me_x + gxn - t, gxn)
        return pltpu.make_async_remote_copy(
            src_ref=sn2_o.at[there],
            dst_ref=sn2_i.at[me_x] if sending else sn2_i.at[there],
            send_sem=ts_sem.at[t],
            recv_sem=tr_sem.at[t],
            device_id=(there, me_y),
            device_id_type=MESH,
        )

    @pl.loop(1, gxn)
    def _(t):
        sn2_copy(t, True).start()

    sn2_i[me_x] = sn2_o[me_x]

    def step_forward(slot, sink):
        halos = take_field(slot)
        for s in range(2):
            for x in range(CX):
                sink(s, x, stencil(slot, cof_f, s, x, halos[s * CX + x]) + src[s, x])

    def into(slot):
        def put(s, x, value):
            fields[slot, s, 1 + x, mid, :] = value

        return put

    step_forward(1, into(2))
    send_field(2)

    @pl.loop(1, gxn)
    def _(t):
        sn2_copy(t, False).wait_recv()

    records = jnp.concatenate([sn2_i[d] for d in range(gxn)], axis=0)
    many = records.shape[0]
    sel = (iota((8, CY), 0) * 16 == iota((8, CY), 1)).astype(F32)
    cell_rows = (dot_nt(sel, records, HIGH) + 0.5).astype(jnp.int32) - 1
    zx = lax.shift_right_arithmetic(cell_rows, 7)
    pick_zx = jnp.concatenate(
        [(iota((CX * NZ, many), 0) == zx[k : k + 1]).astype(BF16) for k in range(4)], axis=1
    )
    at_lane = []
    for k in range(4):
        cell_col = (records[:, 16 * k : 16 * k + 1] + 0.5).astype(jnp.int32) - 1
        lane = jnp.where(cell_col >= 0, cell_col & (CY - 1), -1)
        at_lane.append(iota((many, CY), 1) == lane)
    cnt[...] = dot_nn(
        pick_zx, jnp.concatenate([a.astype(F32).astype(BF16) for a in at_lane], axis=0)
    )
    for ch in range(2 * STEPS):
        values = jnp.concatenate(
            [
                jnp.where(at_lane[k], records[:, 16 * k + 1 + ch : 16 * k + 2 + ch], 0.0)
                for k in range(4)
            ],
            axis=0,
        )
        hi, mid_part, low = split3(values)
        obsf[ch] = (dot_nn(pick_zx, hi) + dot_nn(pick_zx, mid_part)) + dot_nn(pick_zx, low)

    step_forward(2, into(3))
    send_field(3)

    def forcing(state, s, x, n):
        span = slice(x * NZ, x * NZ + NZ)
        return cnt[span] * state - obsf[s * STEPS + n - 1, span]

    loads[4].wait()

    def last(s, x, value):
        out_c[s, x] = value
        adj = value - tgt[s, x] + forcing(value, s, x, 4)
        fields[4, s, 1 + x, mid, :] = adj
        summed[s, x] = adj

    step_forward(3, last)
    send_field(4)

    for n in (3, 2, 1):
        slot = 7 - n
        halos = take_field(slot)
        for s in range(2):
            for x in range(CX):
                adj = stencil(slot, cof_a, s, x, halos[s * CX + x]) + forcing(
                    fields[n, s, 1 + x, mid, :], s, x, n
                )
                fields[slot + 1, s, 1 + x, mid, :] = adj
                summed[s, x] = summed[s, x] + adj
        send_field(slot + 1)

    stacked = jnp.concatenate(
        [
            summed[s, fx, bz * 8 : bz * 8 + 8, :]
            for s in range(2)
            for bz in range(BZ)
            for fx in range(FX)
        ],
        axis=0,
    )
    totals = [jnp.zeros((32, rows), F32) for _ in range(2)]
    picked = [dot_nt(stacked, at_y[fy], HIGH) for fy in range(FY)]
    for s in range(2):
        for bz in range(BZ):
            base = (s * BZ + bz) * 32
            part = jnp.zeros((32, rows), F32)
            for fy in range(FY):
                part = part + foot_t[fy * 32 : fy * 32 + 32] * picked[fy][base : base + 32]
            totals[s] = totals[s] + jnp.where(bz_row == bz, part, 0.0)
    sums = [jnp.sum(t, axis=0, keepdims=True) for t in totals]
    if rows < CY:
        sums = [jnp.concatenate([v, jnp.zeros((1, CY - rows), F32)], axis=1) for v in sums]
    grad_o[...] = jnp.concatenate(sums + [jnp.zeros((6, CY), F32)], axis=0)

    @pl.loop(1, gyn)
    def _(t):
        grad_to(t).start()

    grad_i[own_tile, :] = grad_o[...]

    halos = take_field(7)
    for s in range(2):
        for x in range(CX):
            out_s[s, x] = stencil(7, cof_a, s, x, halos[s * CX + x])

    @pl.loop(1, gyn)
    def _(t):
        grad_of(t).wait_recv()

    pick_lane = (iota((CY, acts), 0) == me_y * 8 + arank).astype(F32)
    brought = dot_nn(grad_i[...], pick_lane, HIGH)
    mine = jnp.where(to_tile, brought, 0.0)
    for s in range(2):
        out_g[s : s + 1, :] = jnp.sum(
            jnp.where((slot_row & 7) == s, mine, 0.0), axis=0, keepdims=True
        )

    both_sides(edge_copy, 1, wait_send, range(9))
    both_sides(x_copy, 0, wait_send, range(10))

    @pl.loop(1, gyn)
    def _(t):
        act_to(t).wait_send()
        sen_to(t).wait_send()
        grad_to(t).wait_send()

    @pl.loop(1, gxn)
    def _(t):
        sn2_copy(t, True).wait_send()


def store_kernel(state, sensitivity, gradient, out_c, out_s, out_g, sem):
    copies = [
        pltpu.make_async_copy(source, sink, sem.at[i])
        for i, (source, sink) in enumerate(
            ((state, out_c), (sensitivity, out_s), (gradient, out_g))
        )
    ]
    for copy in copies:
        copy.start()
    for copy in copies:
        copy.wait()


def per_device(
    gxn,
    gyn,
    initial_state,
    eddy_diffusivity,
    velocity,
    target,
    sensor_cell,
    sensor_owner,
    observations,
    actuator_block,
    actuator_owner,
    controls,
    footprint,
):
    sens = sensor_cell.shape[0]
    acts = actuator_block.shape[0]
    rows = gyn * 8
    hbm = pl.BlockSpec(memory_space=pltpu.HBM)
    vmem = pl.BlockSpec(memory_space=pltpu.VMEM)
    dma = pltpu.SemaphoreType.DMA
    big = jax.ShapeDtypeStruct((2, CX, NZ, CY), F32)
    state, sensitivity, gradient = pl.pallas_call(
        functools.partial(whole_kernel, gxn, gyn),
        out_shape=(
            pltpu.VMEM((2, CX, NZ, CY), F32),
            pltpu.VMEM((2, CX, NZ, CY), F32),
            pltpu.VMEM((2, acts), F32),
        ),
        in_specs=[hbm] * 11,
        out_specs=(vmem, vmem, vmem),
        scratch_shapes=[
            pltpu.VMEM((1, sens), jnp.int32),
            pltpu.VMEM((1, sens), jnp.int32),
            pltpu.VMEM((2, STEPS, sens), F32),
            pltpu.VMEM((1, acts), jnp.int32),
            pltpu.VMEM((1, acts), jnp.int32),
            pltpu.VMEM((2, acts), F32),
            pltpu.VMEM((acts, CY), F32),
            pltpu.VMEM((8, 2, CX + 2, PZ, CY), F32),
            pltpu.VMEM((CX + 2, PZ, CY), F32),
            pltpu.VMEM((CX + 2, PZ, CY), F32),
            pltpu.VMEM((2, CX, PZ, CY), F32),
            pltpu.VMEM((2, CX, NZ, CY), F32),
            pltpu.VMEM((2, 7, CX, NZ, CY), F32),
            pltpu.VMEM((2, 6, CX, NZ, CY), F32),
            pltpu.VMEM((2, CX, NZ, CY), F32),
            pltpu.VMEM((CX * NZ, CY), F32),
            pltpu.VMEM((2 * STEPS, CX * NZ, CY), F32),
            pltpu.VMEM((2, CX, NZ, CY), F32),
            pltpu.VMEM((rows, CY), F32),
            pltpu.VMEM((rows, CY), F32),
            pltpu.VMEM((rows, CY), F32),
            pltpu.VMEM((rows, CY), F32),
            pltpu.VMEM((gxn, gyn, CY), F32),
            pltpu.VMEM((gxn, gyn, CY), F32),
            pltpu.VMEM((9, 8, CY), F32),
            pltpu.VMEM((9, 8, CY), F32),
            pltpu.VMEM((9, 8, CY), F32),
            pltpu.VMEM((8, CY), F32),
            pltpu.VMEM((rows, CY), F32),
            dma((12,)),
            dma((10, 2)),
            dma((10, 2)),
            dma((9, 2)),
            dma((9, 2)),
            dma((gyn,)),
            dma((gyn,)),
            dma((gyn,)),
            dma((gyn,)),
            dma((gxn,)),
            dma((gxn,)),
            dma((gyn,)),
            dma((gyn,)),
        ],
        compiler_params=pltpu.CompilerParams(
            collective_id=0, has_side_effects=True, vmem_limit_bytes=64000000
        ),
        name="whole",
    )(
        initial_state,
        eddy_diffusivity,
        velocity,
        target,
        sensor_cell.reshape(1, sens),
        sensor_owner.reshape(1, sens),
        jnp.transpose(observations, (1, 2, 0)),
        actuator_block.reshape(1, acts),
        actuator_owner.reshape(1, acts),
        controls.T,
        footprint,
    )
    state, sensitivity, gradient = pl.pallas_call(
        store_kernel,
        out_shape=(big, big, jax.ShapeDtypeStruct((2, acts), F32)),
        in_specs=[vmem] * 3,
        out_specs=(hbm,) * 3,
        scratch_shapes=[dma((3,))],
        compiler_params=pltpu.CompilerParams(vmem_limit_bytes=1 << 20),
        name="store",
    )(state, sensitivity, gradient)
    return state, sensitivity, gradient.T


def solution(mesh):
    in_specs = (
        P(None, "gx", None, "gy"),
        P("gx", None, "gy"),
        P(None, "gx", None, "gy"),
        P(None, "gx", None, "gy"),
        P(("gx", "gy")),
        P(("gx", "gy"), None),
        P(("gx", "gy"), None, None),
        P(("gx", "gy")),
        P(("gx", "gy"), None),
        P(("gx", "gy"), None),
        P(("gx", "gy"), None),
    )
    out_specs = (P(None, "gx", None, "gy"), P(None, "gx", None, "gy"), P(("gx", "gy"), None))
    return jax.shard_map(
        functools.partial(per_device, mesh.shape["gx"], mesh.shape["gy"]),
        mesh=mesh,
        in_specs=in_specs,
        out_specs=out_specs,
        check_vma=False,
    )
```

```python
import functools

import jax
import jax.numpy as jnp
from jax import lax
from jax.experimental import pallas as pl
from jax.experimental.pallas import tpu as pltpu
from jax.sharding import PartitionSpec as P

MESH = pl.DeviceIdType.MESH
F32 = jnp.float32
BF16 = jnp.bfloat16
HIGH = lax.Precision.HIGHEST

CX = 4
NZ = 48
CY = 128
FX = 4
FZ = 8
FY = 4
BZ = NZ // FZ
STEPS = 4
ZV = NZ // 8
PZ = NZ + 16
Z0 = 8
prandtl = 0.85
SCALES = (1.0, 1.0 / prandtl)


def iota(shape, dim):
    return lax.broadcasted_iota(jnp.int32, shape, dim)


def dot_nn(a, b, precision=None):
    return lax.dot_general(
        a, b, (((1,), (0,)), ((), ())), precision=precision, preferred_element_type=F32
    )


def dot_nt(a, b, precision=None):
    return lax.dot_general(
        a, b, (((1,), (1,)), ((), ())), precision=precision, preferred_element_type=F32
    )


def split3(x):
    hi = x.astype(BF16)
    rest = x - hi.astype(F32)
    mid = rest.astype(BF16)
    low = (rest - mid.astype(F32)).astype(BF16)
    return hi, mid, low


def rank_of(onehot):
    count = onehot.shape[1]
    earlier = (iota((count, count), 0) < iota((count, count), 1)).astype(F32)
    before = dot_nn(onehot, earlier)
    return jnp.sum(onehot * before, axis=0, keepdims=True).astype(jnp.int32)


def pack_edges(planes):
    lane = iota((8, CY), 1)
    packed = jnp.zeros((8, CY), F32)
    for zv in range(ZV):
        for p, plane in enumerate(planes):
            if plane is None:
                continue
            q = zv * len(planes) + p
            turned = pltpu.roll(plane[zv * 8 : zv * 8 + 8], 2 * q + 1, 1)
            packed = jnp.where(lax.shift_right_logical(lane, 1) == q, turned, packed)
    return packed


def merge_edges(left, right):
    lane = iota((8, CY), 1)
    return jnp.where((lane & 1) == 0, pltpu.roll(right, CY - 1, 1), pltpu.roll(left, 1, 1))


def unpack_edges(both, number):
    planes = []
    for p in range(number):
        parts = [
            pltpu.roll(both, CY - (2 * (zv * number + p) + 1), 1) for zv in range(ZV)
        ]
        planes.append(jnp.concatenate(parts, axis=0))
    return planes


def beside_y(plane, halo):
    lane = iota(plane.shape, 1)
    above = jnp.where(lane == CY - 1, halo, pltpu.roll(plane, CY - 1, 1))
    below = jnp.where(lane == 0, halo, pltpu.roll(plane, 1, 1))
    return above, below


def whole_kernel(
    gxn,
    gyn,
    c0_h,
    kap_h,
    vel_h,
    tgt_h,
    cell_h,
    own_h,
    obs_h,
    ablk_h,
    aown_h,
    ctl_h,
    foot_h,
    out_c,
    out_s,
    out_g,
    cell_r,
    own_r,
    obs_r,
    ablk_r,
    aown_r,
    ctl_r,
    foot_r,
    fields,
    kap,
    velx,
    velyz,
    tgt,
    cof,
    pcy,
    pcx,
    bas,
    src,
    cnt,
    obsf,
    summed,
    act_o,
    act_i,
    sen_o,
    sen_i,
    sn2_o,
    sn2_i,
    edge_o,
    edge_l,
    edge_r,
    edge_d,
    edge_u,
    grad_o,
    grad_i,
    loc_sem,
    xs_sem,
    xr_sem,
    es_sem,
    er_sem,
    fs_sem,
    fr_sem,
    as_sem,
    ar_sem,
    ss_sem,
    sr_sem,
    ts_sem,
    tr_sem,
    gs_sem,
    gr_sem,
):
    me_x = lax.axis_index("gx")
    me_y = lax.axis_index("gy")
    lg_y = gyn.bit_length() - 1
    mid = slice(Z0, Z0 + NZ)

    smalls = [
        pltpu.make_async_copy(source, sink, loc_sem.at[5 + i])
        for i, (source, sink) in enumerate(
            (
                (aown_h, aown_r),
                (ablk_h, ablk_r),
                (ctl_h, ctl_r),
                (foot_h, foot_r),
                (own_h, own_r),
                (cell_h, cell_r),
                (obs_h, obs_r),
            )
        )
    ]
    for load in smalls:
        load.start()
    loads = [
        pltpu.make_async_copy(c0_h, fields.at[0, :, 1 : 1 + CX, mid, :], loc_sem.at[0]),
        pltpu.make_async_copy(kap_h, kap.at[1 : 1 + CX, mid, :], loc_sem.at[1]),
        pltpu.make_async_copy(vel_h.at[0], velx.at[1 : 1 + CX, mid, :], loc_sem.at[2]),
        pltpu.make_async_copy(vel_h.at[1:3], velyz.at[:, :, mid, :], loc_sem.at[3]),
        pltpu.make_async_copy(tgt_h, tgt, loc_sem.at[4]),
    ]
    for load in loads:
        load.start()

    barrier = pltpu.get_barrier_semaphore()

    @pl.loop(1, gyn)
    def _(t):
        pl.semaphore_signal(
            barrier, inc=1, device_id=(me_x, lax.rem(me_y + t, gyn)), device_id_type=MESH
        )

    @pl.loop(1, gxn)
    def _(t):
        pl.semaphore_signal(
            barrier, inc=1, device_id=(lax.rem(me_x + t, gxn), me_y), device_id_type=MESH
        )

    for load in smalls:
        load.wait()
    rows = gyn * 8
    acts = aown_r.shape[1]
    aown = aown_r[...]
    slot_row = iota((rows, acts), 0)
    arank = rank_of((iota((gyn, acts), 0) == aown).astype(F32))
    to_tile = lax.shift_right_logical(slot_row, 3) == aown
    pick_foot = (to_tile & ((slot_row & 7) == arank)).astype(F32)
    pick_meta = (to_tile & ((slot_row & 7) == arank + 4)).astype(F32)
    meta_row = iota((CY, acts), 0)
    meta = jnp.where(
        meta_row == 0,
        ablk_r[...].astype(F32) + 1.0,
        jnp.where(
            meta_row == 1, ctl_r[0:1, :], jnp.where(meta_row == 2, ctl_r[1:2, :], 0.0)
        ),
    )
    act_o[...] = dot_nn(pick_foot, foot_r[...], HIGH) + dot_nt(pick_meta, meta, HIGH)

    sens = own_r.shape[1]
    owner = own_r[...]
    spot = (owner & (gyn - 1)) * 8 + lax.shift_right_logical(owner, lg_y)
    pick_sens = (iota((rows, sens), 0) == spot).astype(F32)
    srank = rank_of(pick_sens)
    datum = jnp.concatenate(
        [
            cell_r[...].astype(F32) + 1.0,
            obs_r[0],
            obs_r[1],
            jnp.zeros((7, sens), F32),
        ],
        axis=0,
    )
    spread = [jnp.where(srank == k, datum, 0.0) for k in range(4)]
    spread.append(jnp.zeros((64, sens), F32))
    sen_o[...] = dot_nt(pick_sens, jnp.concatenate(spread, axis=0), HIGH)

    zero_rows = jnp.zeros((8, CY), F32)
    for slot in range(8):
        for s in range(2):
            for x in range(1, 1 + CX):
                fields[slot, s, x, 0:8, :] = zero_rows
                fields[slot, s, x, Z0 + NZ : PZ, :] = zero_rows
    for x in range(1, 1 + CX):
        kap[x, 0:8, :] = zero_rows
        kap[x, Z0 + NZ : PZ, :] = zero_rows
        velyz[1, x - 1, 0:8, :] = zero_rows
        velyz[1, x - 1, Z0 + NZ : PZ, :] = zero_rows
    zero_plane = jnp.zeros((NZ, CY), F32)

    def zero_side(x):
        for slot in range(8):
            for s in range(2):
                fields[slot, s, x, mid, :] = zero_plane
        kap[x, mid, :] = zero_plane
        velx[x, mid, :] = zero_plane

    @pl.when(me_x == 0)
    def _():
        zero_side(0)
        edge_d[...] = jnp.zeros_like(edge_d)

    @pl.when(me_x == gxn - 1)
    def _():
        zero_side(CX + 1)
        edge_u[...] = jnp.zeros_like(edge_u)

    @pl.when(me_y == 0)
    def _():
        edge_l[...] = jnp.zeros_like(edge_l)

    @pl.when(me_y == gyn - 1)
    def _():
        edge_r[...] = jnp.zeros_like(edge_r)

    for load in loads[:4]:
        load.wait()

    state_planes = [fields[0, s, 1 + x, mid, :] for s in range(2) for x in range(CX)]
    edge_o[0] = pack_edges(state_planes)
    coef_planes = [kap[1 + x, mid, :] for x in range(CX)]
    coef_planes += [velyz[0, x, mid, :] for x in range(CX)]
    edge_o[8] = pack_edges(coef_planes)

    pl.semaphore_wait(barrier, gyn - 1 + gxn - 1)

    def to_peer_y(source, sink, send, recv):
        def make(t):
            there = lax.rem(me_y + t, gyn)
            return pltpu.make_async_remote_copy(
                src_ref=source(there),
                dst_ref=sink(me_y),
                send_sem=send.at[t],
                recv_sem=recv.at[t],
                device_id=(me_x, there),
                device_id_type=MESH,
            )

        return make

    def of_peer_y(source, sink, send, recv):
        def make(t):
            there = lax.rem(me_y + gyn - t, gyn)
            return pltpu.make_async_remote_copy(
                src_ref=source(there),
                dst_ref=sink(there),
                send_sem=send.at[t],
                recv_sem=recv.at[t],
                device_id=(me_x, there),
                device_id_type=MESH,
            )

        return make

    def tile_of(ref):
        return lambda d: ref.at[pl.ds(pl.multiple_of(d * 8, 8), 8), :]

    act_to = to_peer_y(tile_of(act_o), tile_of(act_i), as_sem, ar_sem)
    act_of = of_peer_y(tile_of(act_o), tile_of(act_i), as_sem, ar_sem)
    sen_to = to_peer_y(tile_of(sen_o), tile_of(sen_i), ss_sem, sr_sem)
    sen_of = of_peer_y(tile_of(sen_o), tile_of(sen_i), ss_sem, sr_sem)
    same = lambda d: grad_o
    grad_to = to_peer_y(same, tile_of(grad_i), gs_sem, gr_sem)
    grad_of = of_peer_y(same, tile_of(grad_i), gs_sem, gr_sem)

    def edge_copy(slot, side):
        there = me_y - 1 if side == 0 else me_y + 1
        sink = edge_r if side == 0 else edge_l
        return pltpu.make_async_remote_copy(
            src_ref=edge_o.at[slot],
            dst_ref=sink.at[slot],
            send_sem=es_sem.at[slot, side],
            recv_sem=er_sem.at[slot, side],
            device_id=(me_x, there),
            device_id_type=MESH,
        )

    def edge_x_copy(slot, side):
        there = me_x - 1 if side == 0 else me_x + 1
        sink = edge_u if side == 0 else edge_d
        return pltpu.make_async_remote_copy(
            src_ref=edge_o.at[slot],
            dst_ref=sink.at[slot],
            send_sem=fs_sem.at[slot, side],
            recv_sem=fr_sem.at[slot, side],
            device_id=(there, me_y),
            device_id_type=MESH,
        )

    def x_copy(slot, side):
        there = me_x - 1 if side == 0 else me_x + 1
        sink = CX + 1 if side == 0 else 0
        own = 0 if side == 0 else CX - 1
        if slot == 0:
            source = c0_h.at[:, own]
            dest = fields.at[0, :, sink, mid, :]
        elif slot < 8:
            source = fields.at[slot, :, own + 1, mid, :]
            dest = fields.at[slot, :, sink, mid, :]
        elif slot == 8:
            source = kap_h.at[own]
            dest = kap.at[sink, mid, :]
        else:
            source = vel_h.at[0, own]
            dest = velx.at[sink, mid, :]
        return pltpu.make_async_remote_copy(
            src_ref=source,
            dst_ref=dest,
            send_sem=xs_sem.at[slot, side],
            recv_sem=xr_sem.at[slot, side],
            device_id=(there, me_y),
            device_id_type=MESH,
        )

    has = (
        (me_x > 0, me_x < gxn - 1),
        (me_y > 0, me_y < gyn - 1),
    )

    def both_sides(maker, axis, action, slots):
        for side in (0, 1):

            @pl.when(has[axis][side])
            def _(side=side):
                for slot in slots:
                    action(maker(slot, side))

    def start(copy):
        copy.start()

    def wait_send(copy):
        copy.wait_send()

    def wait_recv(maker, axis, slots):
        for side in (0, 1):

            @pl.when(has[axis][1 - side])
            def _(side=side):
                for slot in slots:
                    maker(slot, side).wait_recv()

    @pl.loop(1, gyn)
    def _(t):
        act_to(t).start()

    both_sides(edge_copy, 1, start, (8, 0))
    both_sides(x_copy, 0, start, (8, 9, 0))

    @pl.loop(1, gyn)
    def _(t):
        sen_to(t).start()

    own_tile = pl.ds(pl.multiple_of(me_y * 8, 8), 8)
    act_i[own_tile, :] = act_o[own_tile, :]
    sen_i[own_tile, :] = sen_o[own_tile, :]

    wait_recv(x_copy, 0, (8, 9))
    wait_recv(edge_copy, 1, (8,))
    halos = unpack_edges(merge_edges(edge_l[8], edge_r[8]), 2 * CX)
    lane = iota((NZ, CY), 1)
    rim_y = [[None] * (2 * CX) for _ in range(2)]
    rim_x = [[None] * (2 * CX) for _ in range(2)]
    for x in range(CX):
        here = kap[1 + x, mid, :]
        kyp, kym = beside_y(here, halos[x])
        around = (
            kap[2 + x, mid, :],
            kap[x, mid, :],
            kyp,
            kym,
            kap[1 + x, Z0 + 1 : Z0 + NZ + 1, :],
            kap[1 + x, Z0 - 1 : Z0 + NZ - 1, :],
        )
        faces = [0.5 * (here + other) for other in around]
        total = faces[0] + faces[1] + faces[2] + faces[3] + faces[4] + faces[5]
        uy = velyz[0, x, mid, :]
        uyp, uym = beside_y(uy, halos[CX + x])
        ux = velx[1 + x, mid, :]
        uz = velyz[1, x, mid, :]
        drifts = (
            (-0.5 * ux, 0.5 * ux, -0.5 * uy, 0.5 * uy, -0.5 * uz, 0.5 * uz),
            (
                0.5 * velx[2 + x, mid, :],
                -0.5 * velx[x, mid, :],
                0.5 * uyp,
                -0.5 * uym,
                0.5 * velyz[1, x, Z0 + 1 : Z0 + NZ + 1, :],
                -0.5 * velyz[1, x, Z0 - 1 : Z0 + NZ - 1, :],
            ),
        )
        for s in range(2):
            scale = SCALES[s]
            cof[0, s, 7, x] = 1.0 - scale * total
            for d in range(2):
                parts = []
                for f in range(6):
                    scaled = faces[f] if s == 0 else scale * faces[f]
                    parts.append(scaled + drifts[d][f])
                for f in (0, 1, 4, 5):
                    cof[d, s, f, x] = parts[f]
                cof[d, s, 2, x] = jnp.where(lane == CY - 1, 0.0, parts[2])
                cof[d, s, 3, x] = jnp.where(lane == 0, 0.0, parts[3])
                rim = jnp.where(lane == CY - 1, parts[2], jnp.where(lane == 0, parts[3], 0.0))
                cof[d, s, 6, x] = rim
                rim_y[d][s * CX + x] = rim
                if x == 0:
                    rim_x[d][s * CX + x] = parts[1]
                if x == CX - 1:
                    rim_x[d][s * CX + x] = parts[0]
    for d in range(2):
        pcy[d] = pack_edges(rim_y[d])
        pcx[d] = pack_edges(rim_x[d])

    cells = [(s, x) for x in (0, CX - 1, 1, 2) for s in range(2)]
    x_lane = lax.shift_right_logical(iota((8, CY), 1), 1) & (CX - 1)

    def base(slot, d, s, x):
        here = fields[slot, s, 1 + x, mid, :]
        value = (
            cof[0, s, 7, x] * here
            + cof[d, s, 2, x] * pltpu.roll(here, CY - 1, 1)
            + cof[d, s, 3, x] * pltpu.roll(here, 1, 1)
            + cof[d, s, 4, x] * fields[slot, s, 1 + x, Z0 + 1 : Z0 + NZ + 1, :]
            + cof[d, s, 5, x] * fields[slot, s, 1 + x, Z0 - 1 : Z0 + NZ - 1, :]
        )
        if x < CX - 1:
            value = value + cof[d, s, 0, x] * fields[slot, s, 2 + x, mid, :]
        if x > 0:
            value = value + cof[d, s, 1, x] * fields[slot, s, x, mid, :]
        return value

    def base_all(slot, d, extra):
        planes = [None] * (2 * CX)
        for s, x in cells:
            value = base(slot, d, s, x)
            if extra is not None:
                value = value + extra(s, x)
            bas[s, x] = value
            planes[s * CX + x] = value
        return planes

    def finish(slot, d, s, x, halo):
        value = bas[s, x] + cof[d, s, 6, x] * halo
        if x == 0:
            value = value + cof[d, s, 1, x] * fields[slot, s, 0, mid, :]
        if x == CX - 1:
            value = value + cof[d, s, 0, x] * fields[slot, s, CX + 1, mid, :]
        return value

    def take_y(slot):
        wait_recv(edge_copy, 1, (slot,))
        return merge_edges(edge_l[slot], edge_r[slot])

    def next_edges(slot, d, rim, packed):
        wait_recv(edge_x_copy, 0, (slot,))
        across = jnp.where(
            x_lane == 0, pltpu.roll(edge_d[slot], CY - 6, 1), pltpu.roll(edge_u[slot], 6, 1)
        )
        return packed + pcy[d] * rim + pcx[d] * across

    def send_edges(slot, value):
        edge_o[slot] = value
        both_sides(edge_copy, 1, start, (slot,))
        if slot < 7:
            both_sides(edge_x_copy, 0, start, (slot,))

    def put_field(slot, s, x, value):
        fields[slot, s, 1 + x, mid, :] = value
        if x == CX - 1 and s == 1:
            both_sides(x_copy, 0, start, (slot,))

    base_all(0, 0, None)
    rim = take_y(0)
    wait_recv(x_copy, 0, (0,))
    halos = unpack_edges(rim, 2 * CX)
    for s, x in cells:
        bas[s, x] = finish(0, 0, s, x, halos[s * CX + x])

    @pl.loop(1, gyn)
    def _(t):
        act_of(t).wait_recv()

    many_a = gyn * 4
    sub = iota((8, CY), 0)
    foots, metas = [], []
    for i in range(gyn // 2):
        one, two = act_i[16 * i : 16 * i + 8, :], act_i[16 * i + 8 : 16 * i + 16, :]
        foots.append(jnp.where(sub < 4, one, pltpu.roll(two, 4, 0)))
        metas.append(jnp.where(sub < 4, pltpu.roll(one, 4, 0), two))
    foot = jnp.concatenate(foots * 2, axis=0)
    meta = jnp.concatenate(metas * 2, axis=0)
    sel = (iota((8, CY), 0) == iota((8, CY), 1)).astype(BF16)
    meta_parts = split3(meta)
    m0, m1, m2 = [dot_nt(sel, part) for part in meta_parts]
    meta_rows = m0 + m1 + m2
    blk_row = (meta_rows[0:1] + 0.5).astype(jnp.int32) - 1
    bz_row = jnp.where(blk_row >= 0, lax.shift_right_arithmetic(blk_row, 5), -1)
    blk_col = (meta[:, 0:1] + 0.5).astype(jnp.int32) - 1
    half_col = (iota((2 * many_a, 1), 0) >= many_a).astype(jnp.int32)
    first_y = jnp.where(blk_col >= 0, (blk_col & 31) * FY + half_col, -8)
    at_y = [
        (iota((2 * many_a, CY), 1) == first_y + 2 * g).astype(F32).astype(BF16)
        for g in range(2)
    ]
    perm_row = iota((CY, CY), 0)
    perm = (
        (iota((CY, CY), 1) == (perm_row & 31) * FY + lax.shift_right_logical(perm_row, 5))
        .astype(F32)
        .astype(BF16)
    )
    f0, f1, f2 = [dot_nt(perm, part) for part in split3(foot)]
    foot_t = f0 + f1 + f2
    half_row = iota((32, 2 * many_a), 1) < many_a
    foot_g = [
        jnp.where(half_row, foot_t[64 * g : 64 * g + 32], foot_t[64 * g + 32 : 64 * g + 64])
        for g in range(2)
    ]
    weights = [
        jnp.where(bz_row == bz, meta_rows[1 + s : 2 + s], 0.0)
        for s in range(2)
        for bz in range(BZ)
    ]
    spots = jnp.concatenate(at_y, axis=0)
    for s in range(2):
        left = jnp.concatenate(
            [
                jnp.concatenate([foot_g[g] * weights[s * BZ + bz] for bz in range(BZ)], axis=0)
                for g in range(2)
            ],
            axis=1,
        )
        p0, p1, p2 = [dot_nn(part, spots) for part in split3(left)]
        placed = p0 + p1 + p2
        for bz in range(BZ):
            for fx in range(FX):
                row = bz * 32 + fx * 8
                src[s, fx, bz * 8 : bz * 8 + 8, :] = placed[row : row + 8]

    planes = [None] * (2 * CX)
    for s, x in cells:
        value = bas[s, x] + src[s, x]
        planes[s * CX + x] = value
        fields[1, s, 1 + x, mid, :] = value
    send_edges(1, pack_edges(planes))
    both_sides(x_copy, 0, start, (1,))

    @pl.loop(1, gyn)
    def _(t):
        sen_of(t).wait_recv()

    for d in range(gxn):
        sn2_o[d] = sen_i[pl.ds(d, gyn, stride=8), :]

    def sn2_copy(t, sending):
        there = lax.rem(me_x + t, gxn) if sending else lax.rem(me_x + gxn - t, gxn)
        return pltpu.make_async_remote_copy(
            src_ref=sn2_o.at[there],
            dst_ref=sn2_i.at[me_x] if sending else sn2_i.at[there],
            send_sem=ts_sem.at[t],
            recv_sem=tr_sem.at[t],
            device_id=(there, me_y),
            device_id_type=MESH,
        )

    @pl.loop(1, gxn)
    def _(t):
        sn2_copy(t, True).start()

    sn2_i[me_x] = sn2_o[me_x]

    supply = lambda s, x: src[s, x]
    packed = pack_edges(base_all(1, 0, supply))

    rim = take_y(1)
    send_edges(2, next_edges(1, 0, rim, packed))
    wait_recv(x_copy, 0, (1,))
    halos = unpack_edges(rim, 2 * CX)
    for s, x in cells:
        put_field(2, s, x, finish(1, 0, s, x, halos[s * CX + x]))
    packed = pack_edges(base_all(2, 0, supply))

    @pl.loop(1, gxn)
    def _(t):
        sn2_copy(t, False).wait_recv()

    records = jnp.concatenate([sn2_i[d] for d in range(gxn)], axis=0)
    many = records.shape[0]
    take = (iota((64, CY), 0) == iota((64, CY), 1)).astype(BF16)
    r0, r1, r2 = [dot_nt(take, part) for part in split3(records)]
    lanes_t = r0 + r1 + r2
    pick_zx, at_lane = [], []
    for k in range(4):
        cell_row = (lanes_t[16 * k : 16 * k + 1] + 0.5).astype(jnp.int32) - 1
        zx = lax.shift_right_arithmetic(cell_row, 7)
        pick_zx.append(iota((CX * NZ, many), 0) == zx)
        cell_col = (records[:, 16 * k : 16 * k + 1] + 0.5).astype(jnp.int32) - 1
        where_y = jnp.where(cell_col >= 0, cell_col & (CY - 1), -1)
        at_lane.append((iota((many, CY), 1) == where_y).astype(F32).astype(BF16))
    at_lanes = jnp.concatenate(at_lane, axis=0)
    one_zx = jnp.concatenate([p.astype(F32).astype(BF16) for p in pick_zx], axis=1)
    cnt[...] = dot_nn(one_zx, at_lanes)

    def sensor_field(ch):
        rows_of = [lanes_t[16 * k + 1 + ch : 16 * k + 2 + ch] for k in range(4)]
        left = jnp.concatenate(
            [jnp.where(pick_zx[k], rows_of[k], 0.0) for k in range(4)], axis=1
        )
        o0, o1, o2 = [dot_nn(part, at_lanes) for part in split3(left)]
        obsf[ch] = o0 + o1 + o2

    for s in range(2):
        for n in (4, 3):
            sensor_field(s * STEPS + n - 1)

    rim = take_y(2)
    send_edges(3, next_edges(2, 0, rim, packed))
    wait_recv(x_copy, 0, (2,))
    halos = unpack_edges(rim, 2 * CX)
    for s, x in cells:
        put_field(3, s, x, finish(2, 0, s, x, halos[s * CX + x]))
    packed = pack_edges(base_all(3, 0, supply))

    for s in range(2):
        for n in (2, 1):
            sensor_field(s * STEPS + n - 1)

    def span(x):
        return slice(x * NZ, x * NZ + NZ)

    def forcing(state, s, x, n):
        return cnt[span(x)] * state - obsf[s * STEPS + n - 1, span(x)]

    loads[4].wait()
    packed_cnt = pack_edges([cnt[span(x)] for s in range(2) for x in range(CX)])
    packed_goal = pack_edges(
        [tgt[s, x] + obsf[s * STEPS + 3, span(x)] for s in range(2) for x in range(CX)]
    )

    rim = take_y(3)
    edges = next_edges(3, 0, rim, packed)
    send_edges(4, edges + packed_cnt * edges - packed_goal)
    wait_recv(x_copy, 0, (3,))
    halos = unpack_edges(rim, 2 * CX)
    for s, x in cells:
        value = finish(3, 0, s, x, halos[s * CX + x])
        out_c[s, x] = value
        adj = value - tgt[s, x] + forcing(value, s, x, 4)
        summed[s, x] = adj
        put_field(4, s, x, adj)

    for n in (3, 2, 1):
        slot = 7 - n
        packed = pack_edges(
            base_all(
                slot, 1, lambda s, x: forcing(fields[n, s, 1 + x, mid, :], s, x, n)
            )
        )
        rim = take_y(slot)
        send_edges(slot + 1, next_edges(slot, 1, rim, packed))
        wait_recv(x_copy, 0, (slot,))
        halos = unpack_edges(rim, 2 * CX)
        for s, x in cells:
            adj = finish(slot, 1, s, x, halos[s * CX + x])
            summed[s, x] = summed[s, x] + adj
            put_field(slot + 1, s, x, adj)

    stacked = jnp.concatenate(
        [
            summed[s, fx, bz * 8 : bz * 8 + 8, :]
            for s in range(2)
            for bz in range(BZ)
            for fx in range(FX)
        ],
        axis=0,
    )
    sums = []
    for s in range(2):
        parts = split3(stacked[s * BZ * 32 : (s + 1) * BZ * 32])
        total = jnp.zeros((32, 2 * many_a), F32)
        for g in range(2):
            q0, q1, q2 = [dot_nt(part, at_y[g]) for part in parts]
            picked = q0 + q1 + q2
            part = jnp.zeros((32, 2 * many_a), F32)
            for bz in range(BZ):
                part = part + jnp.where(bz_row == bz, picked[bz * 32 : bz * 32 + 32], 0.0)
            total = total + foot_g[g] * part
        both = jnp.sum(total, axis=0, keepdims=True)
        sums.append(both + pltpu.roll(both, many_a, 1))
    if 2 * many_a < CY:
        sums = [
            jnp.concatenate([v, jnp.zeros((1, CY - 2 * many_a), F32)], axis=1) for v in sums
        ]
    grad_o[...] = jnp.concatenate(sums + [jnp.zeros((6, CY), F32)], axis=0)

    @pl.loop(1, gyn)
    def _(t):
        grad_to(t).start()

    grad_i[own_tile, :] = grad_o[...]

    base_all(7, 1, None)
    rim = take_y(7)
    wait_recv(x_copy, 0, (7,))
    halos = unpack_edges(rim, 2 * CX)
    for s, x in cells:
        out_s[s, x] = finish(7, 1, s, x, halos[s * CX + x])

    @pl.loop(1, gyn)
    def _(t):
        grad_of(t).wait_recv()

    pick_lane = (iota((CY, acts), 0) == me_y * 4 + arank).astype(F32)
    brought = dot_nn(grad_i[...], pick_lane, HIGH)
    mine = jnp.where(to_tile, brought, 0.0)
    for s in range(2):
        out_g[s : s + 1, :] = jnp.sum(
            jnp.where((slot_row & 7) == s, mine, 0.0), axis=0, keepdims=True
        )

    both_sides(edge_copy, 1, wait_send, range(9))
    both_sides(x_copy, 0, wait_send, range(10))
    both_sides(edge_x_copy, 0, wait_send, range(1, 7))

    @pl.loop(1, gyn)
    def _(t):
        act_to(t).wait_send()
        sen_to(t).wait_send()
        grad_to(t).wait_send()

    @pl.loop(1, gxn)
    def _(t):
        sn2_copy(t, True).wait_send()


def store_kernel(state, sensitivity, gradient, out_c, out_s, out_g, sem):
    copies = [
        pltpu.make_async_copy(source, sink, sem.at[i])
        for i, (source, sink) in enumerate(
            ((state, out_c), (sensitivity, out_s), (gradient, out_g))
        )
    ]
    for copy in copies:
        copy.start()
    for copy in copies:
        copy.wait()


def per_device(
    gxn,
    gyn,
    initial_state,
    eddy_diffusivity,
    velocity,
    target,
    sensor_cell,
    sensor_owner,
    observations,
    actuator_block,
    actuator_owner,
    controls,
    footprint,
):
    sens = sensor_cell.shape[0]
    acts = actuator_block.shape[0]
    rows = gyn * 8
    hbm = pl.BlockSpec(memory_space=pltpu.HBM)
    vmem = pl.BlockSpec(memory_space=pltpu.VMEM)
    dma = pltpu.SemaphoreType.DMA
    big = jax.ShapeDtypeStruct((2, CX, NZ, CY), F32)
    state, sensitivity, gradient = pl.pallas_call(
        functools.partial(whole_kernel, gxn, gyn),
        out_shape=(
            pltpu.VMEM((2, CX, NZ, CY), F32),
            pltpu.VMEM((2, CX, NZ, CY), F32),
            pltpu.VMEM((2, acts), F32),
        ),
        in_specs=[hbm] * 11,
        out_specs=(vmem, vmem, vmem),
        scratch_shapes=[
            pltpu.VMEM((1, sens), jnp.int32),
            pltpu.VMEM((1, sens), jnp.int32),
            pltpu.VMEM((2, STEPS, sens), F32),
            pltpu.VMEM((1, acts), jnp.int32),
            pltpu.VMEM((1, acts), jnp.int32),
            pltpu.VMEM((2, acts), F32),
            pltpu.VMEM((acts, CY), F32),
            pltpu.VMEM((8, 2, CX + 2, PZ, CY), F32),
            pltpu.VMEM((CX + 2, PZ, CY), F32),
            pltpu.VMEM((CX + 2, PZ, CY), F32),
            pltpu.VMEM((2, CX, PZ, CY), F32),
            pltpu.VMEM((2, CX, NZ, CY), F32),
            pltpu.VMEM((2, 2, 8, CX, NZ, CY), F32),
            pltpu.VMEM((2, 8, CY), F32),
            pltpu.VMEM((2, 8, CY), F32),
            pltpu.VMEM((2, CX, NZ, CY), F32),
            pltpu.VMEM((2, CX, NZ, CY), F32),
            pltpu.VMEM((CX * NZ, CY), F32),
            pltpu.VMEM((2 * STEPS, CX * NZ, CY), F32),
            pltpu.VMEM((2, CX, NZ, CY), F32),
            pltpu.VMEM((rows, CY), F32),
            pltpu.VMEM((rows, CY), F32),
            pltpu.VMEM((rows, CY), F32),
            pltpu.VMEM((rows, CY), F32),
            pltpu.VMEM((gxn, gyn, CY), F32),
            pltpu.VMEM((gxn, gyn, CY), F32),
            pltpu.VMEM((9, 8, CY), F32),
            pltpu.VMEM((9, 8, CY), F32),
            pltpu.VMEM((9, 8, CY), F32),
            pltpu.VMEM((7, 8, CY), F32),
            pltpu.VMEM((7, 8, CY), F32),
            pltpu.VMEM((8, CY), F32),
            pltpu.VMEM((rows, CY), F32),
            dma((12,)),
            dma((10, 2)),
            dma((10, 2)),
            dma((9, 2)),
            dma((9, 2)),
            dma((7, 2)),
            dma((7, 2)),
            dma((gyn,)),
            dma((gyn,)),
            dma((gyn,)),
            dma((gyn,)),
            dma((gxn,)),
            dma((gxn,)),
            dma((gyn,)),
            dma((gyn,)),
        ],
        compiler_params=pltpu.CompilerParams(
            collective_id=0, has_side_effects=True, vmem_limit_bytes=64000000
        ),
        name="whole",
    )(
        initial_state,
        eddy_diffusivity,
        velocity,
        target,
        sensor_cell.reshape(1, sens),
        sensor_owner.reshape(1, sens),
        jnp.transpose(observations, (1, 2, 0)),
        actuator_block.reshape(1, acts),
        actuator_owner.reshape(1, acts),
        controls.T,
        footprint,
    )
    state, sensitivity, gradient = pl.pallas_call(
        store_kernel,
        out_shape=(big, big, jax.ShapeDtypeStruct((2, acts), F32)),
        in_specs=[vmem] * 3,
        out_specs=(hbm,) * 3,
        scratch_shapes=[dma((3,))],
        compiler_params=pltpu.CompilerParams(vmem_limit_bytes=1 << 20),
        name="store",
    )(state, sensitivity, gradient)
    return state, sensitivity, gradient.T


def solution(mesh):
    in_specs = (
        P(None, "gx", None, "gy"),
        P("gx", None, "gy"),
        P(None, "gx", None, "gy"),
        P(None, "gx", None, "gy"),
        P(("gx", "gy")),
        P(("gx", "gy"), None),
        P(("gx", "gy"), None, None),
        P(("gx", "gy")),
        P(("gx", "gy"), None),
        P(("gx", "gy"), None),
        P(("gx", "gy"), None),
    )
    out_specs = (P(None, "gx", None, "gy"), P(None, "gx", None, "gy"), P(("gx", "gy"), None))
    return jax.shard_map(
        functools.partial(per_device, mesh.shape["gx"], mesh.shape["gy"]),
        mesh=mesh,
        in_specs=in_specs,
        out_specs=out_specs,
        check_vma=False,
    )
```

```python
import functools

import jax
import jax.numpy as jnp
from jax import lax
from jax.experimental import pallas as pl
from jax.experimental.pallas import tpu as pltpu
from jax.sharding import PartitionSpec as P

MESH = pl.DeviceIdType.MESH
F32 = jnp.float32
BF16 = jnp.bfloat16
HIGH = lax.Precision.HIGHEST

CX = 4
NZ = 48
CY = 128
FX = 4
FZ = 8
FY = 4
BZ = NZ // FZ
STEPS = 4
ZV = NZ // 8
PZ = NZ + 16
Z0 = 8
prandtl = 0.85
SCALES = (1.0, 1.0 / prandtl)


def iota(shape, dim):
    return lax.broadcasted_iota(jnp.int32, shape, dim)


def dot_nn(a, b, precision=None):
    return lax.dot_general(
        a, b, (((1,), (0,)), ((), ())), precision=precision, preferred_element_type=F32
    )


def dot_nt(a, b, precision=None):
    return lax.dot_general(
        a, b, (((1,), (1,)), ((), ())), precision=precision, preferred_element_type=F32
    )


def split3(x):
    hi = x.astype(BF16)
    rest = x - hi.astype(F32)
    mid = rest.astype(BF16)
    low = (rest - mid.astype(F32)).astype(BF16)
    return hi, mid, low


def rank_of(onehot):
    count = onehot.shape[1]
    earlier = (iota((count, count), 0) < iota((count, count), 1)).astype(F32)
    before = dot_nn(onehot, earlier)
    return jnp.sum(onehot * before, axis=0, keepdims=True).astype(jnp.int32)


def lanes8():
    return iota((8, CY), 1)


def pack_cols(planes):
    group = lax.shift_right_logical(lanes8(), 3)
    tiles = []
    for j in range(ZV // 2):
        tile = jnp.zeros((8, CY), F32)
        for odd in range(2):
            zv = 2 * j + odd
            for p, plane in enumerate(planes):
                turned = pltpu.roll(plane[zv * 8 : zv * 8 + 8], 8 * p + 4 + 64 * odd, 1)
                tile = jnp.where(group == p + 8 * odd, turned, tile)
        tiles.append(tile)
    return jnp.concatenate(tiles, axis=0)


def join_cols(own, left, right):
    lane = lanes8()
    low, first = lane < 64, (lane & 7) < 4
    rows = []
    for j in range(ZV // 2):
        part = slice(8 * j, 8 * j + 8)
        lhs = jnp.where(first, left[part], own[part])
        rhs = jnp.where(first, own[part], right[part])
        rows.append(jnp.where(low, lhs, pltpu.roll(rhs, 64, 1)))
        rows.append(jnp.where(low, pltpu.roll(lhs, 64, 1), rhs))
    return jnp.concatenate(rows, axis=0)


def halo_planes(region, number):
    lane = iota((NZ, CY), 1)
    both = jnp.where((lane & 7) == 4, pltpu.roll(region, 1, 1), pltpu.roll(region, 63, 1))
    return [pltpu.roll(both, CY - (8 * p + 4), 1) for p in range(number)]


def squeeze_x(region, x):
    slot = lax.shift_right_logical(lanes8(), 3) & 3
    tiles = []
    for first in (0, 4):
        tile = jnp.zeros((8, CY), F32)
        for k in range(first, min(first + 4, ZV)):
            shift = (8 * (k - first - x)) % CY
            part = region[8 * k : 8 * k + 8]
            tile = jnp.where(slot == k - first, pltpu.roll(part, shift, 1) if shift else part, tile)
        tiles.append(tile)
    return jnp.concatenate(tiles, axis=0)


def spread_x(tiles, x):
    rows = []
    for k in range(ZV):
        shift = (8 * (x - k % 4)) % CY
        part = tiles[8 * (k // 4) : 8 * (k // 4) + 8]
        rows.append(pltpu.roll(part, shift, 1) if shift else part)
    return jnp.concatenate(rows, axis=0)


def beside_x(region, below, above):
    slot = lax.shift_right_logical(iota((NZ, CY), 1), 3) & 3
    minus = jnp.where(slot == 0, spread_x(below, 0), pltpu.roll(region, 8, 1))
    plus = jnp.where(slot == 3, spread_x(above, 3), pltpu.roll(region, CY - 8, 1))
    return plus, minus


def beside_y(plane, halo):
    lane = iota(plane.shape, 1)
    above = jnp.where(lane == CY - 1, halo, pltpu.roll(plane, CY - 1, 1))
    below = jnp.where(lane == 0, halo, pltpu.roll(plane, 1, 1))
    return above, below


def whole_kernel(
    gxn,
    gyn,
    c0_h,
    kap_h,
    vel_h,
    tgt_h,
    cell_h,
    own_h,
    obs_h,
    ablk_h,
    aown_h,
    ctl_h,
    foot_h,
    out_c,
    out_s,
    out_g,
    cell_r,
    own_r,
    obs_r,
    ablk_r,
    aown_r,
    ctl_r,
    foot_r,
    fields,
    kap,
    velx,
    velyz,
    tgt,
    cof,
    rim_f,
    rim_c,
    rim_k,
    bas,
    src,
    cnt,
    obsf,
    summed,
    act_o,
    act_i,
    sen_o,
    sen_i,
    sn2_o,
    sn2_i,
    edge_o,
    edge_l,
    edge_r,
    rim_o,
    rim_d,
    rim_u,
    grad_o,
    grad_i,
    loc_sem,
    xs_sem,
    xr_sem,
    es_sem,
    er_sem,
    fs_sem,
    fr_sem,
    as_sem,
    ar_sem,
    ss_sem,
    sr_sem,
    ts_sem,
    tr_sem,
    gs_sem,
    gr_sem,
):
    me_x = lax.axis_index("gx")
    me_y = lax.axis_index("gy")
    lg_y = gyn.bit_length() - 1
    mid = slice(Z0, Z0 + NZ)

    smalls = [
        pltpu.make_async_copy(source, sink, loc_sem.at[5 + i])
        for i, (source, sink) in enumerate(
            (
                (aown_h, aown_r),
                (ablk_h, ablk_r),
                (ctl_h, ctl_r),
                (foot_h, foot_r),
                (own_h, own_r),
                (cell_h, cell_r),
                (obs_h, obs_r),
            )
        )
    ]
    for load in smalls:
        load.start()
    loads = [
        pltpu.make_async_copy(c0_h, fields.at[0, :, 1 : 1 + CX, mid, :], loc_sem.at[0]),
        pltpu.make_async_copy(kap_h, kap.at[1 : 1 + CX, mid, :], loc_sem.at[1]),
        pltpu.make_async_copy(vel_h.at[0], velx.at[1 : 1 + CX, mid, :], loc_sem.at[2]),
        pltpu.make_async_copy(vel_h.at[1:3], velyz.at[:, :, mid, :], loc_sem.at[3]),
        pltpu.make_async_copy(tgt_h, tgt, loc_sem.at[4]),
    ]
    for load in loads:
        load.start()

    barrier = pltpu.get_barrier_semaphore()

    @pl.loop(1, gyn)
    def _(t):
        pl.semaphore_signal(
            barrier, inc=1, device_id=(me_x, lax.rem(me_y + t, gyn)), device_id_type=MESH
        )

    @pl.loop(1, gxn)
    def _(t):
        pl.semaphore_signal(
            barrier, inc=1, device_id=(lax.rem(me_x + t, gxn), me_y), device_id_type=MESH
        )

    for load in smalls:
        load.wait()
    rows = gyn * 8
    acts = aown_r.shape[1]
    aown = aown_r[...]
    slot_row = iota((rows, acts), 0)
    arank = rank_of((iota((gyn, acts), 0) == aown).astype(F32))
    to_tile = lax.shift_right_logical(slot_row, 3) == aown
    pick_foot = (to_tile & ((slot_row & 7) == arank)).astype(F32)
    pick_meta = (to_tile & ((slot_row & 7) == arank + 4)).astype(F32)
    meta_row = iota((CY, acts), 0)
    meta = jnp.where(
        meta_row == 0,
        ablk_r[...].astype(F32) + 1.0,
        jnp.where(
            meta_row == 1, ctl_r[0:1, :], jnp.where(meta_row == 2, ctl_r[1:2, :], 0.0)
        ),
    )
    act_o[...] = dot_nn(pick_foot, foot_r[...], HIGH) + dot_nt(pick_meta, meta, HIGH)

    sens = own_r.shape[1]
    owner = own_r[...]
    spot = (owner & (gyn - 1)) * 8 + lax.shift_right_logical(owner, lg_y)
    pick_sens = (iota((rows, sens), 0) == spot).astype(F32)
    srank = rank_of(pick_sens)
    datum = jnp.concatenate(
        [
            cell_r[...].astype(F32) + 1.0,
            obs_r[0],
            obs_r[1],
            jnp.zeros((7, sens), F32),
        ],
        axis=0,
    )
    spread = [jnp.where(srank == k, datum, 0.0) for k in range(4)]
    spread.append(jnp.zeros((64, sens), F32))
    sen_o[...] = dot_nt(pick_sens, jnp.concatenate(spread, axis=0), HIGH)

    zero_rows = jnp.zeros((8, CY), F32)
    for slot in range(8):
        for s in range(2):
            for x in range(1, 1 + CX):
                fields[slot, s, x, 0:8, :] = zero_rows
                fields[slot, s, x, Z0 + NZ : PZ, :] = zero_rows
    for x in range(1, 1 + CX):
        kap[x, 0:8, :] = zero_rows
        kap[x, Z0 + NZ : PZ, :] = zero_rows
        velyz[1, x - 1, 0:8, :] = zero_rows
        velyz[1, x - 1, Z0 + NZ : PZ, :] = zero_rows
    for slot in range(7):
        rim_f[slot, 0:8, :] = zero_rows
        rim_f[slot, Z0 + NZ : PZ, :] = zero_rows
    for slot in range(2):
        rim_k[slot, 0:8, :] = zero_rows
        rim_k[slot, Z0 + NZ : PZ, :] = zero_rows
    zero_plane = jnp.zeros((NZ, CY), F32)

    def zero_side(x):
        for slot in range(8):
            for s in range(2):
                fields[slot, s, x, mid, :] = zero_plane
        kap[x, mid, :] = zero_plane
        velx[x, mid, :] = zero_plane

    @pl.when(me_x == 0)
    def _():
        zero_side(0)
        rim_d[...] = jnp.zeros_like(rim_d)

    @pl.when(me_x == gxn - 1)
    def _():
        zero_side(CX + 1)
        rim_u[...] = jnp.zeros_like(rim_u)

    @pl.when(me_y == 0)
    def _():
        edge_l[...] = jnp.zeros_like(edge_l)

    @pl.when(me_y == gyn - 1)
    def _():
        edge_r[...] = jnp.zeros_like(edge_r)

    for load in loads[:4]:
        load.wait()

    edge_o[0] = pack_cols([fields[0, s, 1 + x, mid, :] for s in range(2) for x in range(CX)])
    edge_o[1] = pack_cols(
        [kap[1 + x, mid, :] for x in range(CX)] + [velx[1 + x, mid, :] for x in range(CX)]
    )
    edge_o[2] = pack_cols([velyz[f, x, mid, :] for f in range(2) for x in range(CX)])

    pl.semaphore_wait(barrier, gyn - 1 + gxn - 1)

    def to_peer_y(source, sink, send, recv):
        def make(t):
            there = lax.rem(me_y + t, gyn)
            return pltpu.make_async_remote_copy(
                src_ref=source(there),
                dst_ref=sink(me_y),
                send_sem=send.at[t],
                recv_sem=recv.at[t],
                device_id=(me_x, there),
                device_id_type=MESH,
            )

        return make

    def of_peer_y(source, sink, send, recv):
        def make(t):
            there = lax.rem(me_y + gyn - t, gyn)
            return pltpu.make_async_remote_copy(
                src_ref=source(there),
                dst_ref=sink(there),
                send_sem=send.at[t],
                recv_sem=recv.at[t],
                device_id=(me_x, there),
                device_id_type=MESH,
            )

        return make

    def tile_of(ref):
        return lambda d: ref.at[pl.ds(pl.multiple_of(d * 8, 8), 8), :]

    act_to = to_peer_y(tile_of(act_o), tile_of(act_i), as_sem, ar_sem)
    act_of = of_peer_y(tile_of(act_o), tile_of(act_i), as_sem, ar_sem)
    sen_to = to_peer_y(tile_of(sen_o), tile_of(sen_i), ss_sem, sr_sem)
    sen_of = of_peer_y(tile_of(sen_o), tile_of(sen_i), ss_sem, sr_sem)
    same = lambda d: grad_o
    grad_to = to_peer_y(same, tile_of(grad_i), gs_sem, gr_sem)
    grad_of = of_peer_y(same, tile_of(grad_i), gs_sem, gr_sem)

    def edge_copy(slot, side):
        there = me_y - 1 if side == 0 else me_y + 1
        sink = edge_r if side == 0 else edge_l
        return pltpu.make_async_remote_copy(
            src_ref=edge_o.at[slot],
            dst_ref=sink.at[slot],
            send_sem=es_sem.at[slot, side],
            recv_sem=er_sem.at[slot, side],
            device_id=(me_x, there),
            device_id_type=MESH,
        )

    def rim_copy(slot, side):
        there = me_x - 1 if side == 0 else me_x + 1
        sink = rim_u if side == 0 else rim_d
        return pltpu.make_async_remote_copy(
            src_ref=rim_o.at[slot, side],
            dst_ref=sink.at[slot],
            send_sem=fs_sem.at[slot, side],
            recv_sem=fr_sem.at[slot, side],
            device_id=(there, me_y),
            device_id_type=MESH,
        )

    def x_copy(slot, side):
        there = me_x - 1 if side == 0 else me_x + 1
        sink = CX + 1 if side == 0 else 0
        own = 0 if side == 0 else CX - 1
        if slot == 0:
            source = c0_h.at[:, own]
            dest = fields.at[0, :, sink, mid, :]
        elif slot < 8:
            source = fields.at[slot, :, own + 1, mid, :]
            dest = fields.at[slot, :, sink, mid, :]
        elif slot == 8:
            source = kap_h.at[own]
            dest = kap.at[sink, mid, :]
        else:
            source = vel_h.at[0, own]
            dest = velx.at[sink, mid, :]
        return pltpu.make_async_remote_copy(
            src_ref=source,
            dst_ref=dest,
            send_sem=xs_sem.at[slot, side],
            recv_sem=xr_sem.at[slot, side],
            device_id=(there, me_y),
            device_id_type=MESH,
        )

    has = (
        (me_x > 0, me_x < gxn - 1),
        (me_y > 0, me_y < gyn - 1),
    )

    def both_sides(maker, axis, action, slots):
        for side in (0, 1):

            @pl.when(has[axis][side])
            def _(side=side):
                for slot in slots:
                    action(maker(slot, side))

    def start(copy):
        copy.start()

    def wait_send(copy):
        copy.wait_send()

    def wait_recv(maker, axis, slots):
        for side in (0, 1):

            @pl.when(has[axis][1 - side])
            def _(side=side):
                for slot in slots:
                    maker(slot, side).wait_recv()

    @pl.loop(1, gyn)
    def _(t):
        act_to(t).start()

    both_sides(edge_copy, 1, start, (1, 2, 0))
    both_sides(x_copy, 0, start, (8, 9, 0))

    @pl.loop(1, gyn)
    def _(t):
        sen_to(t).start()

    own_tile = pl.ds(pl.multiple_of(me_y * 8, 8), 8)
    act_i[own_tile, :] = act_o[own_tile, :]
    sen_i[own_tile, :] = sen_o[own_tile, :]

    def take_region(slot):
        wait_recv(edge_copy, 1, (slot,))
        return join_cols(edge_o[slot], edge_l[slot], edge_r[slot])

    def send_rim(slot, region):
        rim_o[slot, 0] = squeeze_x(region, 0)
        rim_o[slot, 1] = squeeze_x(region, CX - 1)
        both_sides(rim_copy, 0, start, (slot,))

    def take_rim(slot, region):
        wait_recv(rim_copy, 0, (slot,))
        return beside_x(region, rim_d[slot], rim_u[slot])

    region_a = take_region(1)
    send_rim(1, region_a)
    region_b = take_region(2)
    rim_f[0, mid, :] = take_region(0)
    send_rim(0, rim_f[0, mid, :])
    halos = halo_planes(region_a, CX) + halo_planes(region_b, CX)
    lane = iota((NZ, CY), 1)
    wait_recv(x_copy, 0, (8, 9))
    for x in range(CX):
        here = kap[1 + x, mid, :]
        kyp, kym = beside_y(here, halos[x])
        around = (
            kap[2 + x, mid, :],
            kap[x, mid, :],
            kyp,
            kym,
            kap[1 + x, Z0 + 1 : Z0 + NZ + 1, :],
            kap[1 + x, Z0 - 1 : Z0 + NZ - 1, :],
        )
        faces = [0.5 * (here + other) for other in around]
        total = faces[0] + faces[1] + faces[2] + faces[3] + faces[4] + faces[5]
        uy = velyz[0, x, mid, :]
        uyp, uym = beside_y(uy, halos[CX + x])
        ux = velx[1 + x, mid, :]
        uz = velyz[1, x, mid, :]
        drifts = (
            (-0.5 * ux, 0.5 * ux, -0.5 * uy, 0.5 * uy, -0.5 * uz, 0.5 * uz),
            (
                0.5 * velx[2 + x, mid, :],
                -0.5 * velx[x, mid, :],
                0.5 * uyp,
                -0.5 * uym,
                0.5 * velyz[1, x, Z0 + 1 : Z0 + NZ + 1, :],
                -0.5 * velyz[1, x, Z0 - 1 : Z0 + NZ - 1, :],
            ),
        )
        for s in range(2):
            scale = SCALES[s]
            cof[0, s, 7, x] = 1.0 - scale * total
            for d in range(2):
                parts = []
                for f in range(6):
                    scaled = faces[f] if s == 0 else scale * faces[f]
                    parts.append(scaled + drifts[d][f])
                for f in (0, 1, 4, 5):
                    cof[d, s, f, x] = parts[f]
                cof[d, s, 2, x] = jnp.where(lane == CY - 1, 0.0, parts[2])
                cof[d, s, 3, x] = jnp.where(lane == 0, 0.0, parts[3])
                cof[d, s, 6, x] = jnp.where(
                    lane == CY - 1, parts[2], jnp.where(lane == 0, parts[3], 0.0)
                )

    cells = [(s, x) for x in (0, CX - 1, 1, 2) for s in range(2)]

    def base(slot, d, s, x):
        here = fields[slot, s, 1 + x, mid, :]
        value = (
            cof[0, s, 7, x] * here
            + cof[d, s, 2, x] * pltpu.roll(here, CY - 1, 1)
            + cof[d, s, 3, x] * pltpu.roll(here, 1, 1)
            + cof[d, s, 4, x] * fields[slot, s, 1 + x, Z0 + 1 : Z0 + NZ + 1, :]
            + cof[d, s, 5, x] * fields[slot, s, 1 + x, Z0 - 1 : Z0 + NZ - 1, :]
        )
        if x < CX - 1:
            value = value + cof[d, s, 0, x] * fields[slot, s, 2 + x, mid, :]
        if x > 0:
            value = value + cof[d, s, 1, x] * fields[slot, s, x, mid, :]
        return value

    def base_all(slot, d, extra):
        for s, x in cells:
            value = base(slot, d, s, x)
            bas[s, x] = value if extra is None else value + extra(s, x)

    def finish(slot, d, s, x, halo):
        value = bas[s, x] + cof[d, s, 6, x] * halo
        if x == 0:
            value = value + cof[d, s, 1, x] * fields[slot, s, 0, mid, :]
        if x == CX - 1:
            value = value + cof[d, s, 0, x] * fields[slot, s, CX + 1, mid, :]
        return value

    def finish_all(slot, d, region, put):
        halos = halo_planes(region, 2 * CX)
        wait_recv(x_copy, 0, (slot,))
        for s, x in cells:
            put(s, x, finish(slot, d, s, x, halos[s * CX + x]))

    def send_cols(slot, planes):
        edge_o[slot] = pack_cols(planes)
        both_sides(edge_copy, 1, start, (slot,))

    def put_field(slot, s, x, value):
        fields[slot, s, 1 + x, mid, :] = value
        if x == CX - 1 and s == 1:
            both_sides(x_copy, 0, start, (slot,))

    base_all(0, 0, None)

    def keep_base(s, x, value):
        bas[s, x] = value

    finish_all(0, 0, rim_f[0, mid, :], keep_base)

    second = (lane & 32) != 0
    outside = ((lane < 64) & ((lane & 7) < 4) & (me_y == 0)) | (
        (lane >= 64) & ((lane & 7) >= 4) & (me_y == gyn - 1)
    )
    keep = jnp.where(outside, 0.0, 1.0)
    scale_r = jnp.where(second, SCALES[1], SCALES[0])

    def first_of(v):
        return jnp.where(second, pltpu.roll(v, 32, 1), v)

    def second_of(v):
        return jnp.where(second, v, pltpu.roll(v, CY - 32, 1))

    plus_a, minus_a = take_rim(1, region_a)
    here = first_of(region_a)
    rim_k[0, mid, :] = here
    uz = second_of(region_b)
    rim_k[1, mid, :] = uz
    uy = first_of(region_b)
    ux = second_of(region_a)
    up, down = slice(Z0 + 1, Z0 + NZ + 1), slice(Z0 - 1, Z0 + NZ - 1)
    around = (
        first_of(plus_a),
        first_of(minus_a),
        pltpu.roll(here, CY - 1, 1),
        pltpu.roll(here, 1, 1),
        rim_k[0, up, :],
        rim_k[0, down, :],
    )
    faces = [0.5 * (here + other) for other in around]
    total = faces[0] + faces[1] + faces[2] + faces[3] + faces[4] + faces[5]
    rim_c[0, 6] = keep * (1.0 - scale_r * total)
    drifts = (
        (-0.5 * ux, 0.5 * ux, -0.5 * uy, 0.5 * uy, -0.5 * uz, 0.5 * uz),
        (
            0.5 * second_of(plus_a),
            -0.5 * second_of(minus_a),
            0.5 * pltpu.roll(uy, CY - 1, 1),
            -0.5 * pltpu.roll(uy, 1, 1),
            0.5 * rim_k[1, up, :],
            -0.5 * rim_k[1, down, :],
        ),
    )
    for d in range(2):
        for f in range(6):
            rim_c[d, f] = keep * (scale_r * faces[f] + drifts[d][f])

    def rim_step(slot, rim_slot, d):
        region = rim_f[slot, mid, :]
        plus, minus = take_rim(rim_slot, region)
        return (
            rim_c[0, 6] * region
            + rim_c[d, 2] * pltpu.roll(region, CY - 1, 1)
            + rim_c[d, 3] * pltpu.roll(region, 1, 1)
            + rim_c[d, 4] * rim_f[slot, up, :]
            + rim_c[d, 5] * rim_f[slot, down, :]
            + rim_c[d, 0] * plus
            + rim_c[d, 1] * minus
        )

    rim_f[1, mid, :] = rim_step(0, 0, 0)

    @pl.loop(1, gyn)
    def _(t):
        act_of(t).wait_recv()

    many_a = gyn * 4
    sub = iota((8, CY), 0)
    foots, metas = [], []
    for i in range(gyn // 2):
        one, two = act_i[16 * i : 16 * i + 8, :], act_i[16 * i + 8 : 16 * i + 16, :]
        foots.append(jnp.where(sub < 4, one, pltpu.roll(two, 4, 0)))
        metas.append(jnp.where(sub < 4, pltpu.roll(one, 4, 0), two))
    foot = jnp.concatenate(foots * 2, axis=0)
    meta = jnp.concatenate(metas * 2, axis=0)
    sel = (iota((8, CY), 0) == iota((8, CY), 1)).astype(BF16)
    meta_parts = split3(meta)
    m0, m1, m2 = [dot_nt(sel, part) for part in meta_parts]
    meta_rows = m0 + m1 + m2
    blk_row = (meta_rows[0:1] + 0.5).astype(jnp.int32) - 1
    bz_row = jnp.where(blk_row >= 0, lax.shift_right_arithmetic(blk_row, 5), -1)
    blk_col = (meta[:, 0:1] + 0.5).astype(jnp.int32) - 1
    half_col = (iota((2 * many_a, 1), 0) >= many_a).astype(jnp.int32)
    first_y = jnp.where(blk_col >= 0, (blk_col & 31) * FY + half_col, -8)
    at_y = [
        (iota((2 * many_a, CY), 1) == first_y + 2 * g).astype(F32).astype(BF16)
        for g in range(2)
    ]
    perm_row = iota((CY, CY), 0)
    perm = (
        (iota((CY, CY), 1) == (perm_row & 31) * FY + lax.shift_right_logical(perm_row, 5))
        .astype(F32)
        .astype(BF16)
    )
    f0, f1, f2 = [dot_nt(perm, part) for part in split3(foot)]
    foot_t = f0 + f1 + f2
    half_row = iota((32, 2 * many_a), 1) < many_a
    foot_g = [
        jnp.where(half_row, foot_t[64 * g : 64 * g + 32], foot_t[64 * g + 32 : 64 * g + 64])
        for g in range(2)
    ]
    weights = [
        jnp.where(bz_row == bz, meta_rows[1 + s : 2 + s], 0.0)
        for s in range(2)
        for bz in range(BZ)
    ]
    spots = jnp.concatenate(at_y, axis=0)
    for s in range(2):
        left = jnp.concatenate(
            [
                jnp.concatenate([foot_g[g] * weights[s * BZ + bz] for bz in range(BZ)], axis=0)
                for g in range(2)
            ],
            axis=1,
        )
        p0, p1, p2 = [dot_nn(part, spots) for part in split3(left)]
        placed = p0 + p1 + p2
        for bz in range(BZ):
            for fx in range(FX):
                row = bz * 32 + fx * 8
                src[s, fx, bz * 8 : bz * 8 + 8, :] = placed[row : row + 8]

    send_cols(3, [src[s, x] for s in range(2) for x in range(CX)])
    for s, x in cells:
        put_field(1, s, x, bas[s, x] + src[s, x])

    @pl.loop(1, gyn)
    def _(t):
        sen_of(t).wait_recv()

    for d in range(gxn):
        sn2_o[d] = sen_i[pl.ds(d, gyn, stride=8), :]

    def sn2_copy(t, sending):
        there = lax.rem(me_x + t, gxn) if sending else lax.rem(me_x + gxn - t, gxn)
        return pltpu.make_async_remote_copy(
            src_ref=sn2_o.at[there],
            dst_ref=sn2_i.at[me_x] if sending else sn2_i.at[there],
            send_sem=ts_sem.at[t],
            recv_sem=tr_sem.at[t],
            device_id=(there, me_y),
            device_id_type=MESH,
        )

    @pl.loop(1, gxn)
    def _(t):
        sn2_copy(t, True).start()

    sn2_i[me_x] = sn2_o[me_x]

    supply = lambda s, x: src[s, x]
    base_all(1, 0, supply)

    supply_r = take_region(3)
    rim_f[1, mid, :] = rim_f[1, mid, :] + supply_r
    send_rim(2, rim_f[1, mid, :])
    finish_all(1, 0, rim_f[1, mid, :], lambda s, x, v: put_field(2, s, x, v))
    base_all(2, 0, supply)

    @pl.loop(1, gxn)
    def _(t):
        sn2_copy(t, False).wait_recv()

    records = jnp.concatenate([sn2_i[d] for d in range(gxn)], axis=0)
    many = records.shape[0]
    take = (iota((64, CY), 0) == iota((64, CY), 1)).astype(BF16)
    r0, r1, r2 = [dot_nt(take, part) for part in split3(records)]
    lanes_t = r0 + r1 + r2
    pick_zx, at_lane = [], []
    for k in range(4):
        cell_row = (lanes_t[16 * k : 16 * k + 1] + 0.5).astype(jnp.int32) - 1
        zx = lax.shift_right_arithmetic(cell_row, 7)
        pick_zx.append(iota((CX * NZ, many), 0) == zx)
        cell_col = (records[:, 16 * k : 16 * k + 1] + 0.5).astype(jnp.int32) - 1
        where_y = jnp.where(cell_col >= 0, cell_col & (CY - 1), -1)
        at_lane.append((iota((many, CY), 1) == where_y).astype(F32).astype(BF16))
    at_lanes = jnp.concatenate(at_lane, axis=0)
    one_zx = jnp.concatenate([p.astype(F32).astype(BF16) for p in pick_zx], axis=1)
    cnt[...] = dot_nn(one_zx, at_lanes)

    def sensor_field(ch):
        rows_of = [lanes_t[16 * k + 1 + ch : 16 * k + 2 + ch] for k in range(4)]
        left = jnp.concatenate(
            [jnp.where(pick_zx[k], rows_of[k], 0.0) for k in range(4)], axis=1
        )
        o0, o1, o2 = [dot_nn(part, at_lanes) for part in split3(left)]
        obsf[ch] = o0 + o1 + o2

    for s in range(2):
        for n in (4, 3):
            sensor_field(s * STEPS + n - 1)

    rim_f[2, mid, :] = rim_step(1, 2, 0) + supply_r
    send_rim(3, rim_f[2, mid, :])
    finish_all(2, 0, rim_f[2, mid, :], lambda s, x, v: put_field(3, s, x, v))
    base_all(3, 0, supply)

    for s in range(2):
        for n in (2, 1):
            sensor_field(s * STEPS + n - 1)

    def span(x):
        return slice(x * NZ, x * NZ + NZ)

    def forcing(state, s, x, n):
        return cnt[span(x)] * state - obsf[s * STEPS + n - 1, span(x)]

    loads[4].wait()
    for n in (3, 2, 1):
        send_cols(
            3 + n,
            [
                forcing(fields[n, s, 1 + x, mid, :], s, x, n)
                for s in range(2)
                for x in range(CX)
            ],
        )

    def last(s, x, value):
        out_c[s, x] = value
        adj = value - tgt[s, x] + forcing(value, s, x, 4)
        summed[s, x] = adj
        put_field(4, s, x, adj)

    finish_all(3, 0, rim_step(2, 3, 0) + supply_r, last)
    send_cols(7, [summed[s, x] for s in range(2) for x in range(CX)])

    for n in (3, 2, 1):
        slot = 7 - n
        base_all(slot, 1, lambda s, x: forcing(fields[n, s, 1 + x, mid, :], s, x, n))
        if n == 3:
            region = take_region(7)
        else:
            pushed = take_region(4 + n)
            region = rim_step(slot - 1, slot - 1, 1) + pushed
        rim_f[slot, mid, :] = region
        send_rim(slot, region)

        def put(s, x, adj):
            summed[s, x] = summed[s, x] + adj
            put_field(slot + 1, s, x, adj)

        finish_all(slot, 1, region, put)

    stacked = jnp.concatenate(
        [
            summed[s, fx, bz * 8 : bz * 8 + 8, :]
            for s in range(2)
            for bz in range(BZ)
            for fx in range(FX)
        ],
        axis=0,
    )
    sums = []
    for s in range(2):
        parts = split3(stacked[s * BZ * 32 : (s + 1) * BZ * 32])
        total = jnp.zeros((32, 2 * many_a), F32)
        for g in range(2):
            q0, q1, q2 = [dot_nt(part, at_y[g]) for part in parts]
            picked = q0 + q1 + q2
            part = jnp.zeros((32, 2 * many_a), F32)
            for bz in range(BZ):
                part = part + jnp.where(bz_row == bz, picked[bz * 32 : bz * 32 + 32], 0.0)
            total = total + foot_g[g] * part
        both = jnp.sum(total, axis=0, keepdims=True)
        sums.append(both + pltpu.roll(both, many_a, 1))
    if 2 * many_a < CY:
        sums = [
            jnp.concatenate([v, jnp.zeros((1, CY - 2 * many_a), F32)], axis=1) for v in sums
        ]
    grad_o[...] = jnp.concatenate(sums + [jnp.zeros((6, CY), F32)], axis=0)

    @pl.loop(1, gyn)
    def _(t):
        grad_to(t).start()

    grad_i[own_tile, :] = grad_o[...]

    base_all(7, 1, None)
    region = rim_step(6, 6, 1) + take_region(4)

    def keep_out(s, x, value):
        out_s[s, x] = value

    finish_all(7, 1, region, keep_out)

    @pl.loop(1, gyn)
    def _(t):
        grad_of(t).wait_recv()

    pick_lane = (iota((CY, acts), 0) == me_y * 4 + arank).astype(F32)
    brought = dot_nn(grad_i[...], pick_lane, HIGH)
    mine = jnp.where(to_tile, brought, 0.0)
    for s in range(2):
        out_g[s : s + 1, :] = jnp.sum(
            jnp.where((slot_row & 7) == s, mine, 0.0), axis=0, keepdims=True
        )

    both_sides(edge_copy, 1, wait_send, range(8))
    both_sides(x_copy, 0, wait_send, range(10))
    both_sides(rim_copy, 0, wait_send, range(7))

    @pl.loop(1, gyn)
    def _(t):
        act_to(t).wait_send()
        sen_to(t).wait_send()
        grad_to(t).wait_send()

    @pl.loop(1, gxn)
    def _(t):
        sn2_copy(t, True).wait_send()


def store_kernel(state, sensitivity, gradient, out_c, out_s, out_g, sem):
    copies = [
        pltpu.make_async_copy(source, sink, sem.at[i])
        for i, (source, sink) in enumerate(
            ((state, out_c), (sensitivity, out_s), (gradient, out_g))
        )
    ]
    for copy in copies:
        copy.start()
    for copy in copies:
        copy.wait()


def per_device(
    gxn,
    gyn,
    initial_state,
    eddy_diffusivity,
    velocity,
    target,
    sensor_cell,
    sensor_owner,
    observations,
    actuator_block,
    actuator_owner,
    controls,
    footprint,
):
    sens = sensor_cell.shape[0]
    acts = actuator_block.shape[0]
    rows = gyn * 8
    hbm = pl.BlockSpec(memory_space=pltpu.HBM)
    vmem = pl.BlockSpec(memory_space=pltpu.VMEM)
    dma = pltpu.SemaphoreType.DMA
    big = jax.ShapeDtypeStruct((2, CX, NZ, CY), F32)
    state, sensitivity, gradient = pl.pallas_call(
        functools.partial(whole_kernel, gxn, gyn),
        out_shape=(
            pltpu.VMEM((2, CX, NZ, CY), F32),
            pltpu.VMEM((2, CX, NZ, CY), F32),
            pltpu.VMEM((2, acts), F32),
        ),
        in_specs=[hbm] * 11,
        out_specs=(vmem, vmem, vmem),
        scratch_shapes=[
            pltpu.VMEM((1, sens), jnp.int32),
            pltpu.VMEM((1, sens), jnp.int32),
            pltpu.VMEM((2, STEPS, sens), F32),
            pltpu.VMEM((1, acts), jnp.int32),
            pltpu.VMEM((1, acts), jnp.int32),
            pltpu.VMEM((2, acts), F32),
            pltpu.VMEM((acts, CY), F32),
            pltpu.VMEM((8, 2, CX + 2, PZ, CY), F32),
            pltpu.VMEM((CX + 2, PZ, CY), F32),
            pltpu.VMEM((CX + 2, PZ, CY), F32),
            pltpu.VMEM((2, CX, PZ, CY), F32),
            pltpu.VMEM((2, CX, NZ, CY), F32),
            pltpu.VMEM((2, 2, 8, CX, NZ, CY), F32),
            pltpu.VMEM((7, PZ, CY), F32),
            pltpu.VMEM((2, 7, NZ, CY), F32),
            pltpu.VMEM((2, PZ, CY), F32),
            pltpu.VMEM((2, CX, NZ, CY), F32),
            pltpu.VMEM((2, CX, NZ, CY), F32),
            pltpu.VMEM((CX * NZ, CY), F32),
            pltpu.VMEM((2 * STEPS, CX * NZ, CY), F32),
            pltpu.VMEM((2, CX, NZ, CY), F32),
            pltpu.VMEM((rows, CY), F32),
            pltpu.VMEM((rows, CY), F32),
            pltpu.VMEM((rows, CY), F32),
            pltpu.VMEM((rows, CY), F32),
            pltpu.VMEM((gxn, gyn, CY), F32),
            pltpu.VMEM((gxn, gyn, CY), F32),
            pltpu.VMEM((8, NZ // 2, CY), F32),
            pltpu.VMEM((8, NZ // 2, CY), F32),
            pltpu.VMEM((8, NZ // 2, CY), F32),
            pltpu.VMEM((7, 2, 16, CY), F32),
            pltpu.VMEM((7, 16, CY), F32),
            pltpu.VMEM((7, 16, CY), F32),
            pltpu.VMEM((8, CY), F32),
            pltpu.VMEM((rows, CY), F32),
            dma((12,)),
            dma((10, 2)),
            dma((10, 2)),
            dma((8, 2)),
            dma((8, 2)),
            dma((7, 2)),
            dma((7, 2)),
            dma((gyn,)),
            dma((gyn,)),
            dma((gyn,)),
            dma((gyn,)),
            dma((gxn,)),
            dma((gxn,)),
            dma((gyn,)),
            dma((gyn,)),
        ],
        compiler_params=pltpu.CompilerParams(
            collective_id=0, has_side_effects=True, vmem_limit_bytes=64000000
        ),
        name="whole",
    )(
        initial_state,
        eddy_diffusivity,
        velocity,
        target,
        sensor_cell.reshape(1, sens),
        sensor_owner.reshape(1, sens),
        jnp.transpose(observations, (1, 2, 0)),
        actuator_block.reshape(1, acts),
        actuator_owner.reshape(1, acts),
        controls.T,
        footprint,
    )
    state, sensitivity, gradient = pl.pallas_call(
        store_kernel,
        out_shape=(big, big, jax.ShapeDtypeStruct((2, acts), F32)),
        in_specs=[vmem] * 3,
        out_specs=(hbm,) * 3,
        scratch_shapes=[dma((3,))],
        compiler_params=pltpu.CompilerParams(vmem_limit_bytes=1 << 20),
        name="store",
    )(state, sensitivity, gradient)
    return state, sensitivity, gradient.T


def solution(mesh):
    in_specs = (
        P(None, "gx", None, "gy"),
        P("gx", None, "gy"),
        P(None, "gx", None, "gy"),
        P(None, "gx", None, "gy"),
        P(("gx", "gy")),
        P(("gx", "gy"), None),
        P(("gx", "gy"), None, None),
        P(("gx", "gy")),
        P(("gx", "gy"), None),
        P(("gx", "gy"), None),
        P(("gx", "gy"), None),
    )
    out_specs = (P(None, "gx", None, "gy"), P(None, "gx", None, "gy"), P(("gx", "gy"), None))
    return jax.shard_map(
        functools.partial(per_device, mesh.shape["gx"], mesh.shape["gy"]),
        mesh=mesh,
        in_specs=in_specs,
        out_specs=out_specs,
        check_vma=False,
    )
```

```python
import functools

import jax
import jax.numpy as jnp
from jax import lax
from jax.experimental import pallas as pl
from jax.experimental.pallas import tpu as pltpu
from jax.sharding import PartitionSpec as P

MESH = pl.DeviceIdType.MESH
F32 = jnp.float32
BF16 = jnp.bfloat16
HIGH = lax.Precision.HIGHEST

CX = 4
NZ = 48
CY = 128
FX = 4
FZ = 8
FY = 4
BZ = NZ // FZ
STEPS = 4
ZV = NZ // 8
PZ = NZ + 16
Z0 = 8
PART = NZ // 2
prandtl = 0.85
SCALES = (1.0, 1.0 / prandtl)


def iota(shape, dim):
    return lax.broadcasted_iota(jnp.int32, shape, dim)


def dot_nn(a, b, precision=None):
    return lax.dot_general(
        a, b, (((1,), (0,)), ((), ())), precision=precision, preferred_element_type=F32
    )


def dot_nt(a, b, precision=None):
    return lax.dot_general(
        a, b, (((1,), (1,)), ((), ())), precision=precision, preferred_element_type=F32
    )


def split3(x):
    hi = x.astype(BF16)
    rest = x - hi.astype(F32)
    mid = rest.astype(BF16)
    low = (rest - mid.astype(F32)).astype(BF16)
    return hi, mid, low


def rank_of(onehot):
    count = onehot.shape[1]
    earlier = (iota((count, count), 0) < iota((count, count), 1)).astype(F32)
    before = dot_nn(onehot, earlier)
    return jnp.sum(onehot * before, axis=0, keepdims=True).astype(jnp.int32)


def lanes8():
    return iota((8, CY), 1)


def pack_cols(planes):
    group = lax.shift_right_logical(lanes8(), 3)
    tiles = []
    for j in range(ZV // 2):
        tile = jnp.zeros((8, CY), F32)
        for odd in range(2):
            zv = 2 * j + odd
            for p, plane in enumerate(planes):
                turned = pltpu.roll(plane[zv * 8 : zv * 8 + 8], 8 * p + 4 + 64 * odd, 1)
                tile = jnp.where(group == p + 8 * odd, turned, tile)
        tiles.append(tile)
    return jnp.concatenate(tiles, axis=0)


def join_cols(own, left, right):
    lane = lanes8()
    low, first = lane < 64, (lane & 7) < 4
    rows = []
    for j in range(ZV // 2):
        part = slice(8 * j, 8 * j + 8)
        lhs = jnp.where(first, left[part], own[part])
        rhs = jnp.where(first, own[part], right[part])
        rows.append(jnp.where(low, lhs, pltpu.roll(rhs, 64, 1)))
        rows.append(jnp.where(low, pltpu.roll(lhs, 64, 1), rhs))
    return jnp.concatenate(rows, axis=0)


def halo_planes(region, number):
    lane = iota((NZ, CY), 1)
    both = jnp.where((lane & 7) == 4, pltpu.roll(region, 1, 1), pltpu.roll(region, 63, 1))
    return [pltpu.roll(both, CY - (8 * p + 4), 1) for p in range(number)]


def squeeze_x(region, x):
    slot = lax.shift_right_logical(lanes8(), 3) & 3
    tiles = []
    for first in (0, 4):
        tile = jnp.zeros((8, CY), F32)
        for k in range(first, min(first + 4, ZV)):
            shift = (8 * (k - first - x)) % CY
            part = region[8 * k : 8 * k + 8]
            tile = jnp.where(slot == k - first, pltpu.roll(part, shift, 1) if shift else part, tile)
        tiles.append(tile)
    return jnp.concatenate(tiles, axis=0)


def spread_x(tiles, x):
    rows = []
    for k in range(ZV):
        shift = (8 * (x - k % 4)) % CY
        part = tiles[8 * (k // 4) : 8 * (k // 4) + 8]
        rows.append(pltpu.roll(part, shift, 1) if shift else part)
    return jnp.concatenate(rows, axis=0)


def beside_x(region, below, above):
    slot = lax.shift_right_logical(iota((NZ, CY), 1), 3) & 3
    minus = jnp.where(slot == 0, spread_x(below, 0), pltpu.roll(region, 8, 1))
    plus = jnp.where(slot == 3, spread_x(above, 3), pltpu.roll(region, CY - 8, 1))
    return plus, minus


def beside_y(plane, halo):
    lane = iota(plane.shape, 1)
    above = jnp.where(lane == CY - 1, halo, pltpu.roll(plane, CY - 1, 1))
    below = jnp.where(lane == 0, halo, pltpu.roll(plane, 1, 1))
    return above, below


def whole_kernel(
    gxn,
    gyn,
    c0_h,
    kap_h,
    vel_h,
    tgt_h,
    cell_h,
    own_h,
    obs_h,
    ablk_h,
    aown_h,
    ctl_h,
    foot_h,
    out_c,
    out_s,
    out_g,
    cell_r,
    own_r,
    obs_r,
    ablk_r,
    aown_r,
    ctl_r,
    foot_r,
    fields,
    kap,
    velx,
    velyz,
    tgt,
    cof,
    rim_f,
    rim_c,
    rim_k,
    bas,
    src,
    cnt,
    obsf,
    summed,
    act_o,
    act_i,
    sen_o,
    sen_i,
    sn2_o,
    sn2_i,
    edge_o,
    edge_l,
    edge_r,
    rim_o,
    rim_d,
    rim_u,
    grad_o,
    grad_i,
    loc_sem,
    xs_sem,
    xr_sem,
    es_sem,
    er_sem,
    fs_sem,
    fr_sem,
    as_sem,
    ar_sem,
    ss_sem,
    sr_sem,
    ts_sem,
    tr_sem,
    gs_sem,
    gr_sem,
):
    me_x = lax.axis_index("gx")
    me_y = lax.axis_index("gy")
    lg_y = gyn.bit_length() - 1
    mid = slice(Z0, Z0 + NZ)

    smalls = [
        pltpu.make_async_copy(source, sink, loc_sem.at[5 + i])
        for i, (source, sink) in enumerate(
            (
                (aown_h, aown_r),
                (ablk_h, ablk_r),
                (ctl_h, ctl_r),
                (foot_h, foot_r),
                (own_h, own_r),
                (cell_h, cell_r),
                (obs_h, obs_r),
            )
        )
    ]
    for load in smalls:
        load.start()
    loads = [
        pltpu.make_async_copy(c0_h, fields.at[0, :, 1 : 1 + CX, mid, :], loc_sem.at[0]),
        pltpu.make_async_copy(kap_h, kap.at[1 : 1 + CX, mid, :], loc_sem.at[1]),
        pltpu.make_async_copy(vel_h.at[0], velx.at[1 : 1 + CX, mid, :], loc_sem.at[2]),
        pltpu.make_async_copy(vel_h.at[1:3], velyz.at[:, :, mid, :], loc_sem.at[3]),
        pltpu.make_async_copy(tgt_h, tgt, loc_sem.at[4]),
    ]
    for load in loads:
        load.start()

    barrier = pltpu.get_barrier_semaphore()

    @pl.loop(1, gyn)
    def _(t):
        pl.semaphore_signal(
            barrier, inc=1, device_id=(me_x, lax.rem(me_y + t, gyn)), device_id_type=MESH
        )

    @pl.loop(1, gxn)
    def _(t):
        pl.semaphore_signal(
            barrier, inc=1, device_id=(lax.rem(me_x + t, gxn), me_y), device_id_type=MESH
        )

    for load in smalls:
        load.wait()
    rows = gyn * 8
    acts = aown_r.shape[1]
    aown = aown_r[...]
    slot_row = iota((rows, acts), 0)
    arank = rank_of((iota((gyn, acts), 0) == aown).astype(F32))
    to_tile = lax.shift_right_logical(slot_row, 3) == aown
    pick_foot = (to_tile & ((slot_row & 7) == arank)).astype(F32)
    pick_meta = (to_tile & ((slot_row & 7) == arank + 4)).astype(F32)
    meta_row = iota((CY, acts), 0)
    meta = jnp.where(
        meta_row == 0,
        ablk_r[...].astype(F32) + 1.0,
        jnp.where(
            meta_row == 1, ctl_r[0:1, :], jnp.where(meta_row == 2, ctl_r[1:2, :], 0.0)
        ),
    )
    act_o[...] = dot_nn(pick_foot, foot_r[...], HIGH) + dot_nt(pick_meta, meta, HIGH)

    sens = own_r.shape[1]
    owner = own_r[...]
    spot = (owner & (gyn - 1)) * 8 + lax.shift_right_logical(owner, lg_y)
    pick_sens = (iota((rows, sens), 0) == spot).astype(F32)
    srank = rank_of(pick_sens)
    datum = jnp.concatenate(
        [
            cell_r[...].astype(F32) + 1.0,
            obs_r[0],
            obs_r[1],
            jnp.zeros((7, sens), F32),
        ],
        axis=0,
    )
    spread = [jnp.where(srank == k, datum, 0.0) for k in range(4)]
    spread.append(jnp.zeros((64, sens), F32))
    sen_o[...] = dot_nt(pick_sens, jnp.concatenate(spread, axis=0), HIGH)

    zero_rows = jnp.zeros((8, CY), F32)
    for slot in range(8):
        for s in range(2):
            for x in range(1, 1 + CX):
                fields[slot, s, x, 0:8, :] = zero_rows
                fields[slot, s, x, Z0 + NZ : PZ, :] = zero_rows
    for x in range(1, 1 + CX):
        kap[x, 0:8, :] = zero_rows
        kap[x, Z0 + NZ : PZ, :] = zero_rows
        velyz[1, x - 1, 0:8, :] = zero_rows
        velyz[1, x - 1, Z0 + NZ : PZ, :] = zero_rows
    for slot in range(7):
        rim_f[slot, 0:8, :] = zero_rows
        rim_f[slot, Z0 + NZ : PZ, :] = zero_rows
    for slot in range(2):
        rim_k[slot, 0:8, :] = zero_rows
        rim_k[slot, Z0 + NZ : PZ, :] = zero_rows
    zero_plane = jnp.zeros((NZ, CY), F32)

    def zero_side(x):
        for slot in range(8):
            for s in range(2):
                fields[slot, s, x, mid, :] = zero_plane
        kap[x, mid, :] = zero_plane
        velx[x, mid, :] = zero_plane

    @pl.when(me_x == 0)
    def _():
        zero_side(0)
        rim_d[...] = jnp.zeros_like(rim_d)

    @pl.when(me_x == gxn - 1)
    def _():
        zero_side(CX + 1)
        rim_u[...] = jnp.zeros_like(rim_u)

    @pl.when(me_y == 0)
    def _():
        edge_l[...] = jnp.zeros_like(edge_l)

    @pl.when(me_y == gyn - 1)
    def _():
        edge_r[...] = jnp.zeros_like(edge_r)

    for load in loads[:4]:
        load.wait()

    edge_o[0] = pack_cols([fields[0, s, 1 + x, mid, :] for s in range(2) for x in range(CX)])
    edge_o[1] = pack_cols(
        [kap[1 + x, mid, :] for x in range(CX)] + [velx[1 + x, mid, :] for x in range(CX)]
    )
    edge_o[2] = pack_cols([velyz[f, x, mid, :] for f in range(2) for x in range(CX)])

    cells = [(s, x) for x in (0, CX - 1, 1, 2) for s in range(2)]

    def base(slot, d, s, x):
        here = fields[slot, s, 1 + x, mid, :]
        value = (
            cof[0, s, 7, x] * here
            + cof[d, s, 2, x] * pltpu.roll(here, CY - 1, 1)
            + cof[d, s, 3, x] * pltpu.roll(here, 1, 1)
            + cof[d, s, 4, x] * fields[slot, s, 1 + x, Z0 + 1 : Z0 + NZ + 1, :]
            + cof[d, s, 5, x] * fields[slot, s, 1 + x, Z0 - 1 : Z0 + NZ - 1, :]
        )
        if x < CX - 1:
            value = value + cof[d, s, 0, x] * fields[slot, s, 2 + x, mid, :]
        if x > 0:
            value = value + cof[d, s, 1, x] * fields[slot, s, x, mid, :]
        return value

    def base_all(slot, d, extra):
        for s, x in cells:
            value = base(slot, d, s, x)
            bas[s, x] = value if extra is None else value + extra(s, x)

    pl.semaphore_wait(barrier, gyn - 1 + gxn - 1)

    def to_peer_y(source, sink, send, recv):
        def make(t):
            there = lax.rem(me_y + t, gyn)
            return pltpu.make_async_remote_copy(
                src_ref=source(there),
                dst_ref=sink(me_y),
                send_sem=send.at[t],
                recv_sem=recv.at[t],
                device_id=(me_x, there),
                device_id_type=MESH,
            )

        return make

    def of_peer_y(source, sink, send, recv):
        def make(t):
            there = lax.rem(me_y + gyn - t, gyn)
            return pltpu.make_async_remote_copy(
                src_ref=source(there),
                dst_ref=sink(there),
                send_sem=send.at[t],
                recv_sem=recv.at[t],
                device_id=(me_x, there),
                device_id_type=MESH,
            )

        return make

    def tile_of(ref):
        return lambda d: ref.at[pl.ds(pl.multiple_of(d * 8, 8), 8), :]

    act_to = to_peer_y(tile_of(act_o), tile_of(act_i), as_sem, ar_sem)
    act_of = of_peer_y(tile_of(act_o), tile_of(act_i), as_sem, ar_sem)
    sen_to = to_peer_y(tile_of(sen_o), tile_of(sen_i), ss_sem, sr_sem)
    sen_of = of_peer_y(tile_of(sen_o), tile_of(sen_i), ss_sem, sr_sem)
    same = lambda d: grad_o
    grad_to = to_peer_y(same, tile_of(grad_i), gs_sem, gr_sem)
    grad_of = of_peer_y(same, tile_of(grad_i), gs_sem, gr_sem)

    def edge_copy(slot, side):
        there = me_y - 1 if side == 0 else me_y + 1
        sink = edge_r if side == 0 else edge_l
        return pltpu.make_async_remote_copy(
            src_ref=edge_o.at[slot],
            dst_ref=sink.at[slot],
            send_sem=es_sem.at[slot, side],
            recv_sem=er_sem.at[slot, side],
            device_id=(me_x, there),
            device_id_type=MESH,
        )

    def rim_copy(slot, side):
        there = me_x - 1 if side == 0 else me_x + 1
        sink = rim_u if side == 0 else rim_d
        return pltpu.make_async_remote_copy(
            src_ref=rim_o.at[slot, side],
            dst_ref=sink.at[slot],
            send_sem=fs_sem.at[slot, side],
            recv_sem=fr_sem.at[slot, side],
            device_id=(there, me_y),
            device_id_type=MESH,
        )

    def x_copy(slot, side, chunk=0):
        there = me_x - 1 if side == 0 else me_x + 1
        sink = CX + 1 if side == 0 else 0
        own = 0 if side == 0 else CX - 1
        part = slice(Z0 + PART * (chunk % 2), Z0 + PART * (chunk % 2 + 1))
        if slot < 8:
            source = fields.at[slot, chunk // 2, own + 1, part, :]
            dest = fields.at[slot, chunk // 2, sink, part, :]
        else:
            held = kap if slot == 8 else velx
            source = held.at[own + 1, part, :]
            dest = held.at[sink, part, :]
        return pltpu.make_async_remote_copy(
            src_ref=source,
            dst_ref=dest,
            send_sem=xs_sem.at[slot, side, chunk],
            recv_sem=xr_sem.at[slot, side, chunk],
            device_id=(there, me_y),
            device_id_type=MESH,
        )

    has = (
        (me_x > 0, me_x < gxn - 1),
        (me_y > 0, me_y < gyn - 1),
    )

    def both_sides(maker, axis, action, slots):
        for side in (0, 1):

            @pl.when(has[axis][side])
            def _(side=side):
                for slot in slots:
                    action(maker(slot, side))

    def start(copy):
        copy.start()

    def wait_send(copy):
        copy.wait_send()

    def wait_recv(maker, axis, slots):
        for side in (0, 1):

            @pl.when(has[axis][1 - side])
            def _(side=side):
                for slot in slots:
                    maker(slot, side).wait_recv()

    for chunk in range(2):
        both_sides(lambda a, b: x_copy(a, b, chunk), 0, start, (8, 9))
    for chunk in range(4):
        both_sides(lambda a, b: x_copy(a, b, chunk), 0, start, (0,))

    @pl.loop(1, gyn)
    def _(t):
        act_to(t).start()

    both_sides(edge_copy, 1, start, (1, 2, 0))

    @pl.loop(1, gyn)
    def _(t):
        sen_to(t).start()

    own_tile = pl.ds(pl.multiple_of(me_y * 8, 8), 8)
    act_i[own_tile, :] = act_o[own_tile, :]
    sen_i[own_tile, :] = sen_o[own_tile, :]

    lane = iota((NZ, CY), 1)
    nothing = jnp.zeros((NZ, CY), F32)
    for x in range(CX):
        here = kap[1 + x, mid, :]
        kyp, kym = beside_y(here, nothing)
        around = (
            kap[2 + x, mid, :] if x < CX - 1 else nothing,
            kap[x, mid, :] if x > 0 else nothing,
            kyp,
            kym,
            kap[1 + x, Z0 + 1 : Z0 + NZ + 1, :],
            kap[1 + x, Z0 - 1 : Z0 + NZ - 1, :],
        )
        faces = [0.5 * (here + other) for other in around]
        total = faces[0] + faces[1] + faces[2] + faces[3] + faces[4] + faces[5]
        uy = velyz[0, x, mid, :]
        uyp, uym = beside_y(uy, nothing)
        ux = velx[1 + x, mid, :]
        uz = velyz[1, x, mid, :]
        drifts = (
            (-0.5 * ux, 0.5 * ux, -0.5 * uy, 0.5 * uy, -0.5 * uz, 0.5 * uz),
            (
                0.5 * velx[2 + x, mid, :] if x < CX - 1 else None,
                -0.5 * velx[x, mid, :] if x > 0 else None,
                0.5 * uyp,
                -0.5 * uym,
                0.5 * velyz[1, x, Z0 + 1 : Z0 + NZ + 1, :],
                -0.5 * velyz[1, x, Z0 - 1 : Z0 + NZ - 1, :],
            ),
        )
        for s in range(2):
            scale = SCALES[s]
            cof[0, s, 7, x] = 1.0 - scale * total
            for d in range(2):
                for f in range(6):
                    if (f == 0 and x == CX - 1) or (f == 1 and x == 0):
                        continue
                    part = (faces[f] if s == 0 else scale * faces[f]) + drifts[d][f]
                    if f == 2:
                        part = jnp.where(lane == CY - 1, 0.0, part)
                    if f == 3:
                        part = jnp.where(lane == 0, 0.0, part)
                    cof[d, s, f, x] = part
    base_all(0, 0, None)

    def take_region(slot):
        wait_recv(edge_copy, 1, (slot,))
        return join_cols(edge_o[slot], edge_l[slot], edge_r[slot])

    def send_rim(slot, region):
        rim_o[slot, 0] = squeeze_x(region, 0)
        rim_o[slot, 1] = squeeze_x(region, CX - 1)
        both_sides(rim_copy, 0, start, (slot,))

    def take_rim(slot, region):
        wait_recv(rim_copy, 0, (slot,))
        return beside_x(region, rim_d[slot], rim_u[slot])

    region_a = take_region(1)
    send_rim(1, region_a)
    region_b = take_region(2)
    rim_f[0, mid, :] = take_region(0)
    send_rim(0, rim_f[0, mid, :])
    halos = halo_planes(region_a, CX) + halo_planes(region_b, CX)
    def send_cols(slot, planes):
        edge_o[slot] = pack_cols(planes)
        both_sides(edge_copy, 1, start, (slot,))

    @pl.loop(1, gyn)
    def _(t):
        act_of(t).wait_recv()

    many_a = gyn * 4
    sub = iota((8, CY), 0)
    foots, metas = [], []
    for i in range(gyn // 2):
        one, two = act_i[16 * i : 16 * i + 8, :], act_i[16 * i + 8 : 16 * i + 16, :]
        foots.append(jnp.where(sub < 4, one, pltpu.roll(two, 4, 0)))
        metas.append(jnp.where(sub < 4, pltpu.roll(one, 4, 0), two))
    foot = jnp.concatenate(foots * 2, axis=0)
    meta = jnp.concatenate(metas * 2, axis=0)
    sel = (iota((8, CY), 0) == iota((8, CY), 1)).astype(BF16)
    meta_parts = split3(meta)
    m0, m1, m2 = [dot_nt(sel, part) for part in meta_parts]
    meta_rows = m0 + m1 + m2
    blk_row = (meta_rows[0:1] + 0.5).astype(jnp.int32) - 1
    bz_row = jnp.where(blk_row >= 0, lax.shift_right_arithmetic(blk_row, 5), -1)
    blk_col = (meta[:, 0:1] + 0.5).astype(jnp.int32) - 1
    half_col = (iota((2 * many_a, 1), 0) >= many_a).astype(jnp.int32)
    first_y = jnp.where(blk_col >= 0, (blk_col & 31) * FY + half_col, -8)
    at_y = [
        (iota((2 * many_a, CY), 1) == first_y + 2 * g).astype(F32).astype(BF16)
        for g in range(2)
    ]
    perm_row = iota((CY, CY), 0)
    perm = (
        (iota((CY, CY), 1) == (perm_row & 31) * FY + lax.shift_right_logical(perm_row, 5))
        .astype(F32)
        .astype(BF16)
    )
    f0, f1, f2 = [dot_nt(perm, part) for part in split3(foot)]
    foot_t = f0 + f1 + f2
    half_row = iota((32, 2 * many_a), 1) < many_a
    foot_g = [
        jnp.where(half_row, foot_t[64 * g : 64 * g + 32], foot_t[64 * g + 32 : 64 * g + 64])
        for g in range(2)
    ]
    weights = [
        jnp.where(bz_row == bz, meta_rows[1 + s : 2 + s], 0.0)
        for s in range(2)
        for bz in range(BZ)
    ]
    spots = jnp.concatenate(at_y, axis=0)
    for s in range(2):
        left = jnp.concatenate(
            [
                jnp.concatenate([foot_g[g] * weights[s * BZ + bz] for bz in range(BZ)], axis=0)
                for g in range(2)
            ],
            axis=1,
        )
        p0, p1, p2 = [dot_nn(part, spots) for part in split3(left)]
        placed = p0 + p1 + p2
        for bz in range(BZ):
            for fx in range(FX):
                row = bz * 32 + fx * 8
                src[s, fx, bz * 8 : bz * 8 + 8, :] = placed[row : row + 8]

    send_cols(3, [src[s, x] for s in range(2) for x in range(CX)])
    for chunk in range(2):
        wait_recv(lambda a, b: x_copy(a, b, chunk), 0, (8, 9))
    sign_y = jnp.where(lane == CY - 1, 1.0, jnp.where(lane == 0, -1.0, 0.0))
    on_y = sign_y != 0.0
    for x in range(CX):
        here = kap[1 + x, mid, :]
        missing = jnp.where(on_y, 0.5 * halos[x], 0.0)
        face_y = jnp.where(on_y, 0.5 * (here + halos[x]), 0.0)
        drift_y = (
            -0.5 * sign_y * velyz[0, x, mid, :],
            0.5 * sign_y * halos[CX + x],
        )
        if x in (0, CX - 1):
            far = 0 if x == 0 else CX + 1
            sign = -0.5 if x == 0 else 0.5
            missing = missing + 0.5 * kap[far, mid, :]
            face_x = 0.5 * (here + kap[far, mid, :])
            drift_x = (-sign * velx[1 + x, mid, :], sign * velx[far, mid, :])
        for s in range(2):
            scaled = missing if s == 0 else SCALES[s] * missing
            cof[0, s, 7, x] = cof[0, s, 7, x] - scaled
            bas[s, x] = bas[s, x] - scaled * fields[0, s, 1 + x, mid, :]
            for d in range(2):
                cof[d, s, 6, x] = SCALES[s] * face_y + drift_y[d]
                if x in (0, CX - 1):
                    cof[d, s, 1 if x == 0 else 0, x] = SCALES[s] * face_x + drift_x[d]

    whole = slice(0, NZ)

    def finish(slot, d, s, x, halo, part):
        value = bas[s, x, part] + cof[d, s, 6, x, part] * halo[part]
        far = slice(Z0 + part.start, Z0 + part.stop)
        if x == 0:
            value = value + cof[d, s, 1, x, part] * fields[slot, s, 0, far, :]
        if x == CX - 1:
            value = value + cof[d, s, 0, x, part] * fields[slot, s, CX + 1, far, :]
        return value

    def put_field(slot, s, x, part, value):
        fields[slot, s, 1 + x, slice(Z0 + part.start, Z0 + part.stop), :] = value

    def send_chunk(slot, chunk):
        both_sides(lambda a, b: x_copy(a, b, chunk), 0, start, (slot,))

    def finish_all(slot, d, region, put, onward):
        halos = halo_planes(region, 2 * CX)
        for chunk in range(4):
            s, z = chunk // 2, chunk % 2
            part = slice(z * PART, z * PART + PART)
            wait_recv(lambda a, b: x_copy(a, b, chunk), 0, (slot,))
            for x in (0, CX - 1):
                put(s, x, part, finish(slot, d, s, x, halos[s * CX + x], part))
            if onward:
                send_chunk(onward, chunk)
        for s in range(2):
            for x in range(1, CX - 1):
                put(s, x, whole, finish(slot, d, s, x, halos[s * CX + x], whole))

    def keep_base(s, x, part, value):
        bas[s, x, part] = value

    finish_all(0, 0, rim_f[0, mid, :], keep_base, 0)

    for chunk in range(4):
        s, z = chunk // 2, chunk % 2
        part = slice(z * PART, z * PART + PART)
        for x in (0, CX - 1):
            put_field(1, s, x, part, bas[s, x, part] + src[s, x, part])
        send_chunk(1, chunk)
    for s in range(2):
        for x in range(1, CX - 1):
            put_field(1, s, x, whole, bas[s, x] + src[s, x])

    second = (lane & 32) != 0
    outside = ((lane < 64) & ((lane & 7) < 4) & (me_y == 0)) | (
        (lane >= 64) & ((lane & 7) >= 4) & (me_y == gyn - 1)
    )
    keep = jnp.where(outside, 0.0, 1.0)
    scale_r = jnp.where(second, SCALES[1], SCALES[0])

    def first_of(v):
        return jnp.where(second, pltpu.roll(v, 32, 1), v)

    def second_of(v):
        return jnp.where(second, v, pltpu.roll(v, CY - 32, 1))

    plus_a, minus_a = take_rim(1, region_a)
    here = first_of(region_a)
    rim_k[0, mid, :] = here
    uz = second_of(region_b)
    rim_k[1, mid, :] = uz
    uy = first_of(region_b)
    ux = second_of(region_a)
    up, down = slice(Z0 + 1, Z0 + NZ + 1), slice(Z0 - 1, Z0 + NZ - 1)
    around = (
        first_of(plus_a),
        first_of(minus_a),
        pltpu.roll(here, CY - 1, 1),
        pltpu.roll(here, 1, 1),
        rim_k[0, up, :],
        rim_k[0, down, :],
    )
    faces = [0.5 * (here + other) for other in around]
    total = faces[0] + faces[1] + faces[2] + faces[3] + faces[4] + faces[5]
    rim_c[0, 6] = keep * (1.0 - scale_r * total)
    drifts = (
        (-0.5 * ux, 0.5 * ux, -0.5 * uy, 0.5 * uy, -0.5 * uz, 0.5 * uz),
        (
            0.5 * second_of(plus_a),
            -0.5 * second_of(minus_a),
            0.5 * pltpu.roll(uy, CY - 1, 1),
            -0.5 * pltpu.roll(uy, 1, 1),
            0.5 * rim_k[1, up, :],
            -0.5 * rim_k[1, down, :],
        ),
    )
    for d in range(2):
        for f in range(6):
            rim_c[d, f] = keep * (scale_r * faces[f] + drifts[d][f])

    def rim_step(slot, rim_slot, d):
        region = rim_f[slot, mid, :]
        plus, minus = take_rim(rim_slot, region)
        return (
            rim_c[0, 6] * region
            + rim_c[d, 2] * pltpu.roll(region, CY - 1, 1)
            + rim_c[d, 3] * pltpu.roll(region, 1, 1)
            + rim_c[d, 4] * rim_f[slot, up, :]
            + rim_c[d, 5] * rim_f[slot, down, :]
            + rim_c[d, 0] * plus
            + rim_c[d, 1] * minus
        )

    rim_f[1, mid, :] = rim_step(0, 0, 0)

    @pl.loop(1, gyn)
    def _(t):
        sen_of(t).wait_recv()

    for d in range(gxn):
        sn2_o[d] = sen_i[pl.ds(d, gyn, stride=8), :]

    def sn2_copy(t, sending):
        there = lax.rem(me_x + t, gxn) if sending else lax.rem(me_x + gxn - t, gxn)
        return pltpu.make_async_remote_copy(
            src_ref=sn2_o.at[there],
            dst_ref=sn2_i.at[me_x] if sending else sn2_i.at[there],
            send_sem=ts_sem.at[t],
            recv_sem=tr_sem.at[t],
            device_id=(there, me_y),
            device_id_type=MESH,
        )

    @pl.loop(1, gxn)
    def _(t):
        sn2_copy(t, True).start()

    sn2_i[me_x] = sn2_o[me_x]

    supply = lambda s, x: src[s, x]
    base_all(1, 0, supply)

    supply_r = take_region(3)
    rim_f[1, mid, :] = rim_f[1, mid, :] + supply_r
    send_rim(2, rim_f[1, mid, :])
    finish_all(1, 0, rim_f[1, mid, :], functools.partial(put_field, 2), 2)
    base_all(2, 0, supply)

    @pl.loop(1, gxn)
    def _(t):
        sn2_copy(t, False).wait_recv()

    records = jnp.concatenate([sn2_i[d] for d in range(gxn)], axis=0)
    many = records.shape[0]
    take = (iota((64, CY), 0) == iota((64, CY), 1)).astype(BF16)
    r0, r1, r2 = [dot_nt(take, part) for part in split3(records)]
    lanes_t = r0 + r1 + r2
    pick_zx, at_lane = [], []
    for k in range(4):
        cell_row = (lanes_t[16 * k : 16 * k + 1] + 0.5).astype(jnp.int32) - 1
        zx = lax.shift_right_arithmetic(cell_row, 7)
        pick_zx.append(iota((CX * NZ, many), 0) == zx)
        cell_col = (records[:, 16 * k : 16 * k + 1] + 0.5).astype(jnp.int32) - 1
        where_y = jnp.where(cell_col >= 0, cell_col & (CY - 1), -1)
        at_lane.append((iota((many, CY), 1) == where_y).astype(F32).astype(BF16))
    at_lanes = jnp.concatenate(at_lane, axis=0)
    one_zx = jnp.concatenate([p.astype(F32).astype(BF16) for p in pick_zx], axis=1)
    cnt[...] = dot_nn(one_zx, at_lanes)

    def sensor_field(ch):
        rows_of = [lanes_t[16 * k + 1 + ch : 16 * k + 2 + ch] for k in range(4)]
        left = jnp.concatenate(
            [jnp.where(pick_zx[k], rows_of[k], 0.0) for k in range(4)], axis=1
        )
        o0, o1, o2 = [dot_nn(part, at_lanes) for part in split3(left)]
        obsf[ch] = o0 + o1 + o2

    for s in range(2):
        sensor_field(s * STEPS + 3)

    rim_f[2, mid, :] = rim_step(1, 2, 0) + supply_r
    send_rim(3, rim_f[2, mid, :])
    finish_all(2, 0, rim_f[2, mid, :], functools.partial(put_field, 3), 3)
    base_all(3, 0, supply)

    for s in range(2):
        sensor_field(s * STEPS + 2)

    def span(x):
        return slice(x * NZ, x * NZ + NZ)

    def forcing(state, s, x, n):
        return cnt[span(x)] * state - obsf[s * STEPS + n - 1, span(x)]

    loads[4].wait()
    def send_forcing(n):
        send_cols(
            3 + n,
            [
                forcing(fields[n, s, 1 + x, mid, :], s, x, n)
                for s in range(2)
                for x in range(CX)
            ],
        )

    send_forcing(3)

    def last(s, x, part, value):
        out_c[s, x, part] = value
        flat = slice(x * NZ + part.start, x * NZ + part.stop)
        push = cnt[flat] * value - obsf[s * STEPS + 3, flat]
        adj = value - tgt[s, x, part] + push
        summed[s, x, part] = adj
        put_field(4, s, x, part, adj)

    finish_all(3, 0, rim_step(2, 3, 0) + supply_r, last, 4)
    send_cols(7, [summed[s, x] for s in range(2) for x in range(CX)])

    for n in (3, 2, 1):
        slot = 7 - n
        base_all(slot, 1, lambda s, x: forcing(fields[n, s, 1 + x, mid, :], s, x, n))
        if n > 1:
            for s in range(2):
                sensor_field(s * STEPS + n - 2)
            send_forcing(n - 1)
        if n == 3:
            region = take_region(7)
        else:
            pushed = take_region(4 + n)
            region = rim_step(slot - 1, slot - 1, 1) + pushed
        rim_f[slot, mid, :] = region
        send_rim(slot, region)

        def put(s, x, part, adj):
            summed[s, x, part] = summed[s, x, part] + adj
            put_field(slot + 1, s, x, part, adj)

        finish_all(slot, 1, region, put, slot + 1)

    stacked = jnp.concatenate(
        [
            summed[s, fx, bz * 8 : bz * 8 + 8, :]
            for s in range(2)
            for bz in range(BZ)
            for fx in range(FX)
        ],
        axis=0,
    )
    sums = []
    for s in range(2):
        parts = split3(stacked[s * BZ * 32 : (s + 1) * BZ * 32])
        total = jnp.zeros((32, 2 * many_a), F32)
        for g in range(2):
            q0, q1, q2 = [dot_nt(part, at_y[g]) for part in parts]
            picked = q0 + q1 + q2
            part = jnp.zeros((32, 2 * many_a), F32)
            for bz in range(BZ):
                part = part + jnp.where(bz_row == bz, picked[bz * 32 : bz * 32 + 32], 0.0)
            total = total + foot_g[g] * part
        both = jnp.sum(total, axis=0, keepdims=True)
        sums.append(both + pltpu.roll(both, many_a, 1))
    if 2 * many_a < CY:
        sums = [
            jnp.concatenate([v, jnp.zeros((1, CY - 2 * many_a), F32)], axis=1) for v in sums
        ]
    grad_o[...] = jnp.concatenate(sums + [jnp.zeros((6, CY), F32)], axis=0)

    @pl.loop(1, gyn)
    def _(t):
        grad_to(t).start()

    grad_i[own_tile, :] = grad_o[...]

    base_all(7, 1, None)
    region = rim_step(6, 6, 1) + take_region(4)

    def keep_out(s, x, part, value):
        out_s[s, x, part] = value

    finish_all(7, 1, region, keep_out, 0)

    both_sides(edge_copy, 1, wait_send, range(8))
    both_sides(x_copy, 0, wait_send, range(10))
    both_sides(lambda a, b: x_copy(a, b, 1), 0, wait_send, range(10))
    for chunk in range(2, 4):
        both_sides(lambda a, b: x_copy(a, b, chunk), 0, wait_send, range(8))
    both_sides(rim_copy, 0, wait_send, range(7))

    @pl.loop(1, gyn)
    def _(t):
        act_to(t).wait_send()
        sen_to(t).wait_send()

    @pl.loop(1, gxn)
    def _(t):
        sn2_copy(t, True).wait_send()

    @pl.loop(1, gyn)
    def _(t):
        grad_of(t).wait_recv()

    pick_lane = (iota((CY, acts), 0) == me_y * 4 + arank).astype(F32)
    brought = dot_nn(grad_i[...], pick_lane, HIGH)
    mine = jnp.where(to_tile, brought, 0.0)
    for s in range(2):
        out_g[s : s + 1, :] = jnp.sum(
            jnp.where((slot_row & 7) == s, mine, 0.0), axis=0, keepdims=True
        )

    @pl.loop(1, gyn)
    def _(t):
        grad_to(t).wait_send()


def store_kernel(state, sensitivity, gradient, out_c, out_s, out_g, sem):
    copies = [
        pltpu.make_async_copy(source, sink, sem.at[i])
        for i, (source, sink) in enumerate(
            ((state, out_c), (sensitivity, out_s), (gradient, out_g))
        )
    ]
    for copy in copies:
        copy.start()
    for copy in copies:
        copy.wait()


def per_device(
    gxn,
    gyn,
    initial_state,
    eddy_diffusivity,
    velocity,
    target,
    sensor_cell,
    sensor_owner,
    observations,
    actuator_block,
    actuator_owner,
    controls,
    footprint,
):
    sens = sensor_cell.shape[0]
    acts = actuator_block.shape[0]
    rows = gyn * 8
    hbm = pl.BlockSpec(memory_space=pltpu.HBM)
    vmem = pl.BlockSpec(memory_space=pltpu.VMEM)
    dma = pltpu.SemaphoreType.DMA
    big = jax.ShapeDtypeStruct((2, CX, NZ, CY), F32)
    state, sensitivity, gradient = pl.pallas_call(
        functools.partial(whole_kernel, gxn, gyn),
        out_shape=(
            pltpu.VMEM((2, CX, NZ, CY), F32),
            pltpu.VMEM((2, CX, NZ, CY), F32),
            pltpu.VMEM((2, acts), F32),
        ),
        in_specs=[hbm] * 11,
        out_specs=(vmem, vmem, vmem),
        scratch_shapes=[
            pltpu.VMEM((1, sens), jnp.int32),
            pltpu.VMEM((1, sens), jnp.int32),
            pltpu.VMEM((2, STEPS, sens), F32),
            pltpu.VMEM((1, acts), jnp.int32),
            pltpu.VMEM((1, acts), jnp.int32),
            pltpu.VMEM((2, acts), F32),
            pltpu.VMEM((acts, CY), F32),
            pltpu.VMEM((8, 2, CX + 2, PZ, CY), F32),
            pltpu.VMEM((CX + 2, PZ, CY), F32),
            pltpu.VMEM((CX + 2, PZ, CY), F32),
            pltpu.VMEM((2, CX, PZ, CY), F32),
            pltpu.VMEM((2, CX, NZ, CY), F32),
            pltpu.VMEM((2, 2, 8, CX, NZ, CY), F32),
            pltpu.VMEM((7, PZ, CY), F32),
            pltpu.VMEM((2, 7, NZ, CY), F32),
            pltpu.VMEM((2, PZ, CY), F32),
            pltpu.VMEM((2, CX, NZ, CY), F32),
            pltpu.VMEM((2, CX, NZ, CY), F32),
            pltpu.VMEM((CX * NZ, CY), F32),
            pltpu.VMEM((2 * STEPS, CX * NZ, CY), F32),
            pltpu.VMEM((2, CX, NZ, CY), F32),
            pltpu.VMEM((rows, CY), F32),
            pltpu.VMEM((rows, CY), F32),
            pltpu.VMEM((rows, CY), F32),
            pltpu.VMEM((rows, CY), F32),
            pltpu.VMEM((gxn, gyn, CY), F32),
            pltpu.VMEM((gxn, gyn, CY), F32),
            pltpu.VMEM((8, NZ // 2, CY), F32),
            pltpu.VMEM((8, NZ // 2, CY), F32),
            pltpu.VMEM((8, NZ // 2, CY), F32),
            pltpu.VMEM((7, 2, 16, CY), F32),
            pltpu.VMEM((7, 16, CY), F32),
            pltpu.VMEM((7, 16, CY), F32),
            pltpu.VMEM((8, CY), F32),
            pltpu.VMEM((rows, CY), F32),
            dma((12,)),
            dma((10, 2, 4)),
            dma((10, 2, 4)),
            dma((8, 2)),
            dma((8, 2)),
            dma((7, 2)),
            dma((7, 2)),
            dma((gyn,)),
            dma((gyn,)),
            dma((gyn,)),
            dma((gyn,)),
            dma((gxn,)),
            dma((gxn,)),
            dma((gyn,)),
            dma((gyn,)),
        ],
        compiler_params=pltpu.CompilerParams(
            collective_id=0, has_side_effects=True, vmem_limit_bytes=64000000
        ),
        name="whole",
    )(
        initial_state,
        eddy_diffusivity,
        velocity,
        target,
        sensor_cell.reshape(1, sens),
        sensor_owner.reshape(1, sens),
        jnp.transpose(observations, (1, 2, 0)),
        actuator_block.reshape(1, acts),
        actuator_owner.reshape(1, acts),
        controls.T,
        footprint,
    )
    state, sensitivity, gradient = pl.pallas_call(
        store_kernel,
        out_shape=(big, big, jax.ShapeDtypeStruct((2, acts), F32)),
        in_specs=[vmem] * 3,
        out_specs=(hbm,) * 3,
        scratch_shapes=[dma((3,))],
        compiler_params=pltpu.CompilerParams(vmem_limit_bytes=1 << 20),
        name="store",
    )(state, sensitivity, gradient)
    return state, sensitivity, gradient.T


def solution(mesh):
    in_specs = (
        P(None, "gx", None, "gy"),
        P("gx", None, "gy"),
        P(None, "gx", None, "gy"),
        P(None, "gx", None, "gy"),
        P(("gx", "gy")),
        P(("gx", "gy"), None),
        P(("gx", "gy"), None, None),
        P(("gx", "gy")),
        P(("gx", "gy"), None),
        P(("gx", "gy"), None),
        P(("gx", "gy"), None),
    )
    out_specs = (P(None, "gx", None, "gy"), P(None, "gx", None, "gy"), P(("gx", "gy"), None))
    return jax.shard_map(
        functools.partial(per_device, mesh.shape["gx"], mesh.shape["gy"]),
        mesh=mesh,
        in_specs=in_specs,
        out_specs=out_specs,
        check_vma=False,
    )
```

```python
import functools

import jax
import jax.numpy as jnp
from jax import lax
from jax.experimental import pallas as pl
from jax.experimental.pallas import tpu as pltpu
from jax.sharding import PartitionSpec as P

MESH = pl.DeviceIdType.MESH
F32 = jnp.float32
BF16 = jnp.bfloat16
HIGH = lax.Precision.HIGHEST

CX = 4
NZ = 48
CY = 128
FX = 4
FZ = 8
FY = 4
BZ = NZ // FZ
STEPS = 4
ZV = NZ // 8
PZ = NZ + 16
Z0 = 8
prandtl = 0.85
SCALES = (1.0, 1.0 / prandtl)


def iota(shape, dim):
    return lax.broadcasted_iota(jnp.int32, shape, dim)


def dot_nn(a, b, precision=None):
    return lax.dot_general(
        a, b, (((1,), (0,)), ((), ())), precision=precision, preferred_element_type=F32
    )


def dot_nt(a, b, precision=None):
    return lax.dot_general(
        a, b, (((1,), (1,)), ((), ())), precision=precision, preferred_element_type=F32
    )


def split3(x):
    hi = x.astype(BF16)
    rest = x - hi.astype(F32)
    mid = rest.astype(BF16)
    low = (rest - mid.astype(F32)).astype(BF16)
    return hi, mid, low


def rank_of(onehot):
    count = onehot.shape[1]
    earlier = (iota((count, count), 0) < iota((count, count), 1)).astype(F32)
    before = dot_nn(onehot, earlier)
    return jnp.sum(onehot * before, axis=0, keepdims=True).astype(jnp.int32)


def lanes8():
    return iota((8, CY), 1)


def pack_cols(planes):
    group = lax.shift_right_logical(lanes8(), 3)
    tiles = []
    for j in range(ZV // 2):
        tile = jnp.zeros((8, CY), F32)
        for odd in range(2):
            zv = 2 * j + odd
            for p, plane in enumerate(planes):
                turned = pltpu.roll(plane[zv * 8 : zv * 8 + 8], 8 * p + 4 + 64 * odd, 1)
                tile = jnp.where(group == p + 8 * odd, turned, tile)
        tiles.append(tile)
    return jnp.concatenate(tiles, axis=0)


def join_cols(own, left, right):
    lane = lanes8()
    low, first = lane < 64, (lane & 7) < 4
    rows = []
    for j in range(ZV // 2):
        part = slice(8 * j, 8 * j + 8)
        lhs = jnp.where(first, left[part], own[part])
        rhs = jnp.where(first, own[part], right[part])
        rows.append(jnp.where(low, lhs, pltpu.roll(rhs, 64, 1)))
        rows.append(jnp.where(low, pltpu.roll(lhs, 64, 1), rhs))
    return jnp.concatenate(rows, axis=0)


def halo_planes(region, number):
    lane = iota((NZ, CY), 1)
    both = jnp.where((lane & 7) == 4, pltpu.roll(region, 1, 1), pltpu.roll(region, 63, 1))
    return [pltpu.roll(both, CY - (8 * p + 4), 1) for p in range(number)]


def squeeze_x(region, x):
    slot = lax.shift_right_logical(lanes8(), 3) & 3
    tiles = []
    for first in (0, 4):
        tile = jnp.zeros((8, CY), F32)
        for k in range(first, min(first + 4, ZV)):
            shift = (8 * (k - first - x)) % CY
            part = region[8 * k : 8 * k + 8]
            tile = jnp.where(slot == k - first, pltpu.roll(part, shift, 1) if shift else part, tile)
        tiles.append(tile)
    return jnp.concatenate(tiles, axis=0)


def spread_x(tiles, x):
    rows = []
    for k in range(ZV):
        shift = (8 * (x - k % 4)) % CY
        part = tiles[8 * (k // 4) : 8 * (k // 4) + 8]
        rows.append(pltpu.roll(part, shift, 1) if shift else part)
    return jnp.concatenate(rows, axis=0)


def beside_x(region, below, above):
    slot = lax.shift_right_logical(iota((NZ, CY), 1), 3) & 3
    minus = jnp.where(slot == 0, spread_x(below, 0), pltpu.roll(region, 8, 1))
    plus = jnp.where(slot == 3, spread_x(above, 3), pltpu.roll(region, CY - 8, 1))
    return plus, minus


def beside_y(plane, halo):
    lane = iota(plane.shape, 1)
    above = jnp.where(lane == CY - 1, halo, pltpu.roll(plane, CY - 1, 1))
    below = jnp.where(lane == 0, halo, pltpu.roll(plane, 1, 1))
    return above, below


def whole_kernel(
    gxn,
    gyn,
    c0_h,
    kap_h,
    vel_h,
    tgt_h,
    cell_h,
    own_h,
    obs_h,
    ablk_h,
    aown_h,
    ctl_h,
    foot_h,
    out_c,
    out_s,
    out_g,
    cell_r,
    own_r,
    obs_r,
    ablk_r,
    aown_r,
    ctl_r,
    foot_r,
    fields,
    kap,
    velx,
    velyz,
    tgt,
    cof,
    rim_f,
    rim_c,
    rim_k,
    bas,
    src,
    cnt,
    obsf,
    summed,
    act_o,
    act_i,
    sen_o,
    sen_i,
    sn2_o,
    sn2_i,
    edge_o,
    edge_l,
    edge_r,
    rim_o,
    rim_d,
    rim_u,
    grad_o,
    grad_i,
    loc_sem,
    xs_sem,
    xr_sem,
    es_sem,
    er_sem,
    fs_sem,
    fr_sem,
    as_sem,
    ar_sem,
    ss_sem,
    sr_sem,
    ts_sem,
    tr_sem,
    gs_sem,
    gr_sem,
):
    me_x = lax.axis_index("gx")
    me_y = lax.axis_index("gy")
    lg_y = gyn.bit_length() - 1
    mid = slice(Z0, Z0 + NZ)

    far_first = [t for t in (10, 6, 9, 11, 14, 7, 5, 13, 8, 2, 3, 12, 15, 4, 1) if t < gyn]
    barrier = pltpu.get_barrier_semaphore()
    for t in far_first:
        pl.semaphore_signal(
            barrier, inc=1, device_id=(me_x, lax.rem(me_y + t, gyn)), device_id_type=MESH
        )
    for t in range(1, gxn):
        pl.semaphore_signal(
            barrier, inc=1, device_id=(lax.rem(me_x + t, gxn), me_y), device_id_type=MESH
        )

    smalls = [
        pltpu.make_async_copy(source, sink, loc_sem.at[5 + i])
        for i, (source, sink) in enumerate(
            (
                (aown_h, aown_r),
                (ablk_h, ablk_r),
                (ctl_h, ctl_r),
                (foot_h, foot_r),
                (own_h, own_r),
                (cell_h, cell_r),
                (obs_h, obs_r),
            )
        )
    ]
    for load in smalls:
        load.start()
    loads = [
        pltpu.make_async_copy(c0_h, fields.at[0, :, 1 : 1 + CX, mid, :], loc_sem.at[0]),
        pltpu.make_async_copy(kap_h, kap.at[1 : 1 + CX, mid, :], loc_sem.at[1]),
        pltpu.make_async_copy(vel_h.at[0], velx.at[1 : 1 + CX, mid, :], loc_sem.at[2]),
        pltpu.make_async_copy(vel_h.at[1:3], velyz.at[:, :, mid, :], loc_sem.at[3]),
        pltpu.make_async_copy(tgt_h, tgt, loc_sem.at[4]),
    ]
    for load in loads:
        load.start()

    for load in smalls:
        load.wait()
    rows = gyn * 8
    acts = aown_r.shape[1]
    aown = aown_r[...]
    slot_row = iota((rows, acts), 0)
    arank = rank_of((iota((gyn, acts), 0) == aown).astype(F32))
    to_tile = lax.shift_right_logical(slot_row, 3) == aown
    pick_foot = (to_tile & ((slot_row & 7) == arank)).astype(F32)
    pick_meta = (to_tile & ((slot_row & 7) == arank + 4)).astype(F32)
    meta_row = iota((CY, acts), 0)
    meta = jnp.where(
        meta_row == 0,
        ablk_r[...].astype(F32) + 1.0,
        jnp.where(
            meta_row == 1, ctl_r[0:1, :], jnp.where(meta_row == 2, ctl_r[1:2, :], 0.0)
        ),
    )
    act_o[...] = dot_nn(pick_foot, foot_r[...], HIGH) + dot_nt(pick_meta, meta, HIGH)

    sens = own_r.shape[1]
    owner = own_r[...]
    spot = (owner & (gyn - 1)) * 8 + lax.shift_right_logical(owner, lg_y)
    pick_sens = (iota((rows, sens), 0) == spot).astype(F32)
    srank = rank_of(pick_sens)
    datum = jnp.concatenate(
        [
            cell_r[...].astype(F32) + 1.0,
            obs_r[0],
            obs_r[1],
            jnp.zeros((7, sens), F32),
        ],
        axis=0,
    )
    spread = [jnp.where(srank == k, datum, 0.0) for k in range(4)]
    spread.append(jnp.zeros((64, sens), F32))
    sen_o[...] = dot_nt(pick_sens, jnp.concatenate(spread, axis=0), HIGH)

    zero_rows = jnp.zeros((8, CY), F32)
    for slot in range(8):
        for s in range(2):
            for x in range(1, 1 + CX):
                fields[slot, s, x, 0:8, :] = zero_rows
                fields[slot, s, x, Z0 + NZ : PZ, :] = zero_rows
    for x in range(1, 1 + CX):
        kap[x, 0:8, :] = zero_rows
        kap[x, Z0 + NZ : PZ, :] = zero_rows
        velyz[1, x - 1, 0:8, :] = zero_rows
        velyz[1, x - 1, Z0 + NZ : PZ, :] = zero_rows
    for slot in range(7):
        rim_f[slot, 0:8, :] = zero_rows
        rim_f[slot, Z0 + NZ : PZ, :] = zero_rows
    for slot in range(2):
        rim_k[slot, 0:8, :] = zero_rows
        rim_k[slot, Z0 + NZ : PZ, :] = zero_rows
    zero_plane = jnp.zeros((NZ, CY), F32)

    def zero_side(x):
        for slot in range(8):
            for s in range(2):
                fields[slot, s, x, mid, :] = zero_plane
        kap[x, mid, :] = zero_plane
        velx[x, mid, :] = zero_plane

    @pl.when(me_x == 0)
    def _():
        zero_side(0)
        rim_d[...] = jnp.zeros_like(rim_d)

    @pl.when(me_x == gxn - 1)
    def _():
        zero_side(CX + 1)
        rim_u[...] = jnp.zeros_like(rim_u)

    @pl.when(me_y == 0)
    def _():
        edge_l[...] = jnp.zeros_like(edge_l)

    @pl.when(me_y == gyn - 1)
    def _():
        edge_r[...] = jnp.zeros_like(edge_r)

    for load in loads[:4]:
        load.wait()

    edge_o[0] = pack_cols([fields[0, s, 1 + x, mid, :] for s in range(2) for x in range(CX)])
    edge_o[1] = pack_cols(
        [kap[1 + x, mid, :] for x in range(CX)] + [velx[1 + x, mid, :] for x in range(CX)]
    )
    edge_o[2] = pack_cols([velyz[f, x, mid, :] for f in range(2) for x in range(CX)])

    cells = [(s, x) for x in (0, CX - 1, 1, 2) for s in range(2)]

    def base(slot, d, s, x):
        here = fields[slot, s, 1 + x, mid, :]
        value = (
            cof[0, s, 7, x] * here
            + cof[d, s, 2, x] * pltpu.roll(here, CY - 1, 1)
            + cof[d, s, 3, x] * pltpu.roll(here, 1, 1)
            + cof[d, s, 4, x] * fields[slot, s, 1 + x, Z0 + 1 : Z0 + NZ + 1, :]
            + cof[d, s, 5, x] * fields[slot, s, 1 + x, Z0 - 1 : Z0 + NZ - 1, :]
        )
        if x < CX - 1:
            value = value + cof[d, s, 0, x] * fields[slot, s, 2 + x, mid, :]
        if x > 0:
            value = value + cof[d, s, 1, x] * fields[slot, s, x, mid, :]
        return value

    def base_all(slot, d, extra):
        for s, x in cells:
            value = base(slot, d, s, x)
            bas[s, x] = value if extra is None else value + extra(s, x)

    pl.semaphore_wait(barrier, gyn - 1 + gxn - 1)

    def to_peer_y(source, sink, send, recv):
        def make(t):
            there = lax.rem(me_y + t, gyn)
            return pltpu.make_async_remote_copy(
                src_ref=source(there),
                dst_ref=sink(me_y),
                send_sem=send.at[t],
                recv_sem=recv.at[t],
                device_id=(me_x, there),
                device_id_type=MESH,
            )

        return make

    def of_peer_y(source, sink, send, recv):
        def make(t):
            there = lax.rem(me_y + gyn - t, gyn)
            return pltpu.make_async_remote_copy(
                src_ref=source(there),
                dst_ref=sink(there),
                send_sem=send.at[t],
                recv_sem=recv.at[t],
                device_id=(me_x, there),
                device_id_type=MESH,
            )

        return make

    def tile_of(ref):
        return lambda d: ref.at[pl.ds(pl.multiple_of(d * 8, 8), 8), :]

    act_to = to_peer_y(tile_of(act_o), tile_of(act_i), as_sem, ar_sem)
    act_of = of_peer_y(tile_of(act_o), tile_of(act_i), as_sem, ar_sem)
    sen_to = to_peer_y(tile_of(sen_o), tile_of(sen_i), ss_sem, sr_sem)
    sen_of = of_peer_y(tile_of(sen_o), tile_of(sen_i), ss_sem, sr_sem)
    same = lambda d: grad_o
    grad_to = to_peer_y(same, tile_of(grad_i), gs_sem, gr_sem)
    grad_of = of_peer_y(same, tile_of(grad_i), gs_sem, gr_sem)

    def edge_copy(slot, side):
        there = me_y - 1 if side == 0 else me_y + 1
        sink = edge_r if side == 0 else edge_l
        return pltpu.make_async_remote_copy(
            src_ref=edge_o.at[slot],
            dst_ref=sink.at[slot],
            send_sem=es_sem.at[slot, side],
            recv_sem=er_sem.at[slot, side],
            device_id=(me_x, there),
            device_id_type=MESH,
        )

    def rim_copy(slot, side):
        there = me_x - 1 if side == 0 else me_x + 1
        sink = rim_u if side == 0 else rim_d
        return pltpu.make_async_remote_copy(
            src_ref=rim_o.at[slot, side],
            dst_ref=sink.at[slot],
            send_sem=fs_sem.at[slot, side],
            recv_sem=fr_sem.at[slot, side],
            device_id=(there, me_y),
            device_id_type=MESH,
        )

    def x_copy(slot, side, chunk=0):
        there = me_x - 1 if side == 0 else me_x + 1
        sink = CX + 1 if side == 0 else 0
        own = 0 if side == 0 else CX - 1
        part = mid
        if slot < 8:
            source = fields.at[slot, chunk, own + 1, part, :]
            dest = fields.at[slot, chunk, sink, part, :]
        else:
            held = kap if slot == 8 else velx
            source = held.at[own + 1, part, :]
            dest = held.at[sink, part, :]
        return pltpu.make_async_remote_copy(
            src_ref=source,
            dst_ref=dest,
            send_sem=xs_sem.at[slot, side, chunk],
            recv_sem=xr_sem.at[slot, side, chunk],
            device_id=(there, me_y),
            device_id_type=MESH,
        )

    has = (
        (me_x > 0, me_x < gxn - 1),
        (me_y > 0, me_y < gyn - 1),
    )

    def both_sides(maker, axis, action, slots):
        for side in (0, 1):

            @pl.when(has[axis][side])
            def _(side=side):
                for slot in slots:
                    action(maker(slot, side))

    def start(copy):
        copy.start()

    def wait_send(copy):
        copy.wait_send()

    def wait_recv(maker, axis, slots):
        for side in (0, 1):

            @pl.when(has[axis][1 - side])
            def _(side=side):
                for slot in slots:
                    maker(slot, side).wait_recv()

    both_sides(x_copy, 0, start, (8,))
    for chunk in range(2):
        both_sides(lambda a, b: x_copy(a, b, chunk), 0, start, (0,))
    both_sides(x_copy, 0, start, (9,))

    for t in far_first:
        act_to(t).start()

    both_sides(edge_copy, 1, start, (1, 2, 0))

    @pl.loop(1, gyn)
    def _(t):
        sen_to(t).start()

    own_tile = pl.ds(pl.multiple_of(me_y * 8, 8), 8)
    act_i[own_tile, :] = act_o[own_tile, :]
    sen_i[own_tile, :] = sen_o[own_tile, :]

    lane = iota((NZ, CY), 1)
    nothing = jnp.zeros((NZ, CY), F32)
    for x in range(CX):
        here = kap[1 + x, mid, :]
        kyp, kym = beside_y(here, nothing)
        around = (
            kap[2 + x, mid, :] if x < CX - 1 else nothing,
            kap[x, mid, :] if x > 0 else nothing,
            kyp,
            kym,
            kap[1 + x, Z0 + 1 : Z0 + NZ + 1, :],
            kap[1 + x, Z0 - 1 : Z0 + NZ - 1, :],
        )
        faces = [0.5 * (here + other) for other in around]
        total = faces[0] + faces[1] + faces[2] + faces[3] + faces[4] + faces[5]
        uy = velyz[0, x, mid, :]
        uyp, uym = beside_y(uy, nothing)
        ux = velx[1 + x, mid, :]
        uz = velyz[1, x, mid, :]
        drifts = (
            (-0.5 * ux, 0.5 * ux, -0.5 * uy, 0.5 * uy, -0.5 * uz, 0.5 * uz),
            (
                0.5 * velx[2 + x, mid, :] if x < CX - 1 else None,
                -0.5 * velx[x, mid, :] if x > 0 else None,
                0.5 * uyp,
                -0.5 * uym,
                0.5 * velyz[1, x, Z0 + 1 : Z0 + NZ + 1, :],
                -0.5 * velyz[1, x, Z0 - 1 : Z0 + NZ - 1, :],
            ),
        )
        for s in range(2):
            scale = SCALES[s]
            cof[0, s, 7, x] = 1.0 - scale * total
            for d in range(2):
                for f in range(6):
                    if (f == 0 and x == CX - 1) or (f == 1 and x == 0):
                        continue
                    part = (faces[f] if s == 0 else scale * faces[f]) + drifts[d][f]
                    if f == 2:
                        part = jnp.where(lane == CY - 1, 0.0, part)
                    if f == 3:
                        part = jnp.where(lane == 0, 0.0, part)
                    cof[d, s, f, x] = part
    base_all(0, 0, None)

    def take_region(slot):
        wait_recv(edge_copy, 1, (slot,))
        return join_cols(edge_o[slot], edge_l[slot], edge_r[slot])

    def send_rim(slot, region):
        rim_o[slot, 0] = squeeze_x(region, 0)
        rim_o[slot, 1] = squeeze_x(region, CX - 1)
        both_sides(rim_copy, 0, start, (slot,))

    def take_rim(slot, region):
        wait_recv(rim_copy, 0, (slot,))
        return beside_x(region, rim_d[slot], rim_u[slot])

    region_a = take_region(1)
    send_rim(1, region_a)
    region_b = take_region(2)
    rim_f[0, mid, :] = take_region(0)
    send_rim(0, rim_f[0, mid, :])
    halos = halo_planes(region_a, CX) + halo_planes(region_b, CX)
    def send_cols(slot, planes):
        edge_o[slot] = pack_cols(planes)
        both_sides(edge_copy, 1, start, (slot,))

    @pl.loop(1, gyn)
    def _(t):
        act_of(t).wait_recv()

    many_a = gyn * 4
    sub = iota((8, CY), 0)
    foots, metas = [], []
    for i in range(gyn // 2):
        one, two = act_i[16 * i : 16 * i + 8, :], act_i[16 * i + 8 : 16 * i + 16, :]
        foots.append(jnp.where(sub < 4, one, pltpu.roll(two, 4, 0)))
        metas.append(jnp.where(sub < 4, pltpu.roll(one, 4, 0), two))
    foot = jnp.concatenate(foots * 2, axis=0)
    meta = jnp.concatenate(metas * 2, axis=0)
    sel = (iota((8, CY), 0) == iota((8, CY), 1)).astype(BF16)
    meta_parts = split3(meta)
    m0, m1, m2 = [dot_nt(sel, part) for part in meta_parts]
    meta_rows = m0 + m1 + m2
    blk_row = (meta_rows[0:1] + 0.5).astype(jnp.int32) - 1
    bz_row = jnp.where(blk_row >= 0, lax.shift_right_arithmetic(blk_row, 5), -1)
    blk_col = (meta[:, 0:1] + 0.5).astype(jnp.int32) - 1
    half_col = (iota((2 * many_a, 1), 0) >= many_a).astype(jnp.int32)
    first_y = jnp.where(blk_col >= 0, (blk_col & 31) * FY + half_col, -8)
    at_y = [
        (iota((2 * many_a, CY), 1) == first_y + 2 * g).astype(F32).astype(BF16)
        for g in range(2)
    ]
    perm_row = iota((CY, CY), 0)
    perm = (
        (iota((CY, CY), 1) == (perm_row & 31) * FY + lax.shift_right_logical(perm_row, 5))
        .astype(F32)
        .astype(BF16)
    )
    f0, f1, f2 = [dot_nt(perm, part) for part in split3(foot)]
    foot_t = f0 + f1 + f2
    half_row = iota((32, 2 * many_a), 1) < many_a
    foot_g = [
        jnp.where(half_row, foot_t[64 * g : 64 * g + 32], foot_t[64 * g + 32 : 64 * g + 64])
        for g in range(2)
    ]
    weights = [
        jnp.where(bz_row == bz, meta_rows[1 + s : 2 + s], 0.0)
        for s in range(2)
        for bz in range(BZ)
    ]
    spots = jnp.concatenate(at_y, axis=0)
    for s in range(2):
        left = jnp.concatenate(
            [
                jnp.concatenate([foot_g[g] * weights[s * BZ + bz] for bz in range(BZ)], axis=0)
                for g in range(2)
            ],
            axis=1,
        )
        p0, p1, p2 = [dot_nn(part, spots) for part in split3(left)]
        placed = p0 + p1 + p2
        for bz in range(BZ):
            for fx in range(FX):
                row = bz * 32 + fx * 8
                src[s, fx, bz * 8 : bz * 8 + 8, :] = placed[row : row + 8]

    send_cols(3, [src[s, x] for s in range(2) for x in range(CX)])
    wait_recv(x_copy, 0, (8,))
    sign_y = jnp.where(lane == CY - 1, 1.0, jnp.where(lane == 0, -1.0, 0.0))
    on_y = sign_y != 0.0
    for x in range(CX):
        here = kap[1 + x, mid, :]
        missing = jnp.where(on_y, 0.5 * halos[x], 0.0)
        face_y = jnp.where(on_y, 0.5 * (here + halos[x]), 0.0)
        drift_y = (
            -0.5 * sign_y * velyz[0, x, mid, :],
            0.5 * sign_y * halos[CX + x],
        )
        if x in (0, CX - 1):
            far = 0 if x == 0 else CX + 1
            sign = -0.5 if x == 0 else 0.5
            missing = missing + 0.5 * kap[far, mid, :]
            face_x = 0.5 * (here + kap[far, mid, :])
            drift_x = -sign * velx[1 + x, mid, :]
        for s in range(2):
            scaled = missing if s == 0 else SCALES[s] * missing
            cof[0, s, 7, x] = cof[0, s, 7, x] - scaled
            bas[s, x] = bas[s, x] - scaled * fields[0, s, 1 + x, mid, :]
            for d in range(2):
                cof[d, s, 6, x] = SCALES[s] * face_y + drift_y[d]
            if x in (0, CX - 1):
                cof[0, s, 1 if x == 0 else 0, x] = SCALES[s] * face_x + drift_x

    whole = slice(0, NZ)

    def finish(slot, d, s, x, halo, part):
        value = bas[s, x, part] + cof[d, s, 6, x, part] * halo[part]
        far = slice(Z0 + part.start, Z0 + part.stop)
        if x == 0:
            value = value + cof[d, s, 1, x, part] * fields[slot, s, 0, far, :]
        if x == CX - 1:
            value = value + cof[d, s, 0, x, part] * fields[slot, s, CX + 1, far, :]
        return value

    def put_field(slot, s, x, part, value):
        fields[slot, s, 1 + x, slice(Z0 + part.start, Z0 + part.stop), :] = value

    def send_chunk(slot, chunk):
        both_sides(lambda a, b: x_copy(a, b, chunk), 0, start, (slot,))

    def finish_all(slot, d, region, put, onward):
        halos = halo_planes(region, 2 * CX)
        for chunk in range(2):
            s, part = chunk, whole
            wait_recv(lambda a, b: x_copy(a, b, chunk), 0, (slot,))
            for x in (0, CX - 1):
                put(s, x, part, finish(slot, d, s, x, halos[s * CX + x], part))
            if onward:
                send_chunk(onward, chunk)
        for s in range(2):
            for x in range(1, CX - 1):
                put(s, x, whole, finish(slot, d, s, x, halos[s * CX + x], whole))

    def keep_base(s, x, part, value):
        bas[s, x, part] = value

    finish_all(0, 0, rim_f[0, mid, :], keep_base, 0)

    for chunk in range(2):
        s, part = chunk, whole
        for x in (0, CX - 1):
            put_field(1, s, x, part, bas[s, x, part] + src[s, x, part])
        send_chunk(1, chunk)
    for s in range(2):
        for x in range(1, CX - 1):
            put_field(1, s, x, whole, bas[s, x] + src[s, x])

    wait_recv(x_copy, 0, (9,))
    for x, far, sign, f in ((0, 0, -0.5, 1), (CX - 1, CX + 1, 0.5, 0)):
        face_x = 0.5 * (kap[1 + x, mid, :] + kap[far, mid, :])
        for s in range(2):
            cof[1, s, f, x] = SCALES[s] * face_x + sign * velx[far, mid, :]

    second = (lane & 32) != 0
    outside = ((lane < 64) & ((lane & 7) < 4) & (me_y == 0)) | (
        (lane >= 64) & ((lane & 7) >= 4) & (me_y == gyn - 1)
    )
    keep = jnp.where(outside, 0.0, 1.0)
    scale_r = jnp.where(second, SCALES[1], SCALES[0])

    def first_of(v):
        return jnp.where(second, pltpu.roll(v, 32, 1), v)

    def second_of(v):
        return jnp.where(second, v, pltpu.roll(v, CY - 32, 1))

    plus_a, minus_a = take_rim(1, region_a)
    here = first_of(region_a)
    rim_k[0, mid, :] = here
    uz = second_of(region_b)
    rim_k[1, mid, :] = uz
    uy = first_of(region_b)
    ux = second_of(region_a)
    up, down = slice(Z0 + 1, Z0 + NZ + 1), slice(Z0 - 1, Z0 + NZ - 1)
    around = (
        first_of(plus_a),
        first_of(minus_a),
        pltpu.roll(here, CY - 1, 1),
        pltpu.roll(here, 1, 1),
        rim_k[0, up, :],
        rim_k[0, down, :],
    )
    faces = [0.5 * (here + other) for other in around]
    total = faces[0] + faces[1] + faces[2] + faces[3] + faces[4] + faces[5]
    rim_c[0, 6] = keep * (1.0 - scale_r * total)
    drifts = (
        (-0.5 * ux, 0.5 * ux, -0.5 * uy, 0.5 * uy, -0.5 * uz, 0.5 * uz),
        (
            0.5 * second_of(plus_a),
            -0.5 * second_of(minus_a),
            0.5 * pltpu.roll(uy, CY - 1, 1),
            -0.5 * pltpu.roll(uy, 1, 1),
            0.5 * rim_k[1, up, :],
            -0.5 * rim_k[1, down, :],
        ),
    )
    for d in range(2):
        for f in range(6):
            rim_c[d, f] = keep * (scale_r * faces[f] + drifts[d][f])

    def rim_step(slot, rim_slot, d):
        region = rim_f[slot, mid, :]
        plus, minus = take_rim(rim_slot, region)
        return (
            rim_c[0, 6] * region
            + rim_c[d, 2] * pltpu.roll(region, CY - 1, 1)
            + rim_c[d, 3] * pltpu.roll(region, 1, 1)
            + rim_c[d, 4] * rim_f[slot, up, :]
            + rim_c[d, 5] * rim_f[slot, down, :]
            + rim_c[d, 0] * plus
            + rim_c[d, 1] * minus
        )

    rim_f[1, mid, :] = rim_step(0, 0, 0)

    @pl.loop(1, gyn)
    def _(t):
        sen_of(t).wait_recv()

    for d in range(gxn):
        held = sen_i[pl.ds(d, gyn, stride=8), :]
        half = gyn // 2
        sn2_o[d] = jnp.where(
            iota((half, CY), 1) < 64, held[:half], pltpu.roll(held[half:], 64, 1)
        )

    def sn2_copy(t, sending):
        there = lax.rem(me_x + t, gxn) if sending else lax.rem(me_x + gxn - t, gxn)
        return pltpu.make_async_remote_copy(
            src_ref=sn2_o.at[there],
            dst_ref=sn2_i.at[me_x] if sending else sn2_i.at[there],
            send_sem=ts_sem.at[t],
            recv_sem=tr_sem.at[t],
            device_id=(there, me_y),
            device_id_type=MESH,
        )

    @pl.loop(1, gxn)
    def _(t):
        sn2_copy(t, True).start()

    sn2_i[me_x] = sn2_o[me_x]

    supply = lambda s, x: src[s, x]
    base_all(1, 0, supply)

    supply_r = take_region(3)
    rim_f[1, mid, :] = rim_f[1, mid, :] + supply_r
    send_rim(2, rim_f[1, mid, :])
    finish_all(1, 0, rim_f[1, mid, :], functools.partial(put_field, 2), 2)
    base_all(2, 0, supply)

    @pl.loop(1, gxn)
    def _(t):
        sn2_copy(t, False).wait_recv()

    both = jnp.concatenate([sn2_i[d] for d in range(gxn)], axis=0)
    records = jnp.concatenate([both, pltpu.roll(both, 64, 1)], axis=0)
    many = records.shape[0]
    take = (iota((64, CY), 0) == iota((64, CY), 1)).astype(BF16)
    r0, r1, r2 = [dot_nt(take, part) for part in split3(records)]
    lanes_t = r0 + r1 + r2
    pick_zx, at_lane = [], []
    for k in range(4):
        cell_row = (lanes_t[16 * k : 16 * k + 1] + 0.5).astype(jnp.int32) - 1
        zx = lax.shift_right_arithmetic(cell_row, 7)
        pick_zx.append(iota((CX * NZ, many), 0) == zx)
        cell_col = (records[:, 16 * k : 16 * k + 1] + 0.5).astype(jnp.int32) - 1
        where_y = jnp.where(cell_col >= 0, cell_col & (CY - 1), -1)
        at_lane.append((iota((many, CY), 1) == where_y).astype(F32).astype(BF16))
    at_lanes = jnp.concatenate(at_lane, axis=0)
    one_zx = jnp.concatenate([p.astype(F32).astype(BF16) for p in pick_zx], axis=1)
    cnt[...] = dot_nn(one_zx, at_lanes)

    def sensor_field(ch):
        rows_of = [lanes_t[16 * k + 1 + ch : 16 * k + 2 + ch] for k in range(4)]
        left = jnp.concatenate(
            [jnp.where(pick_zx[k], rows_of[k], 0.0) for k in range(4)], axis=1
        )
        o0, o1, o2 = [dot_nn(part, at_lanes) for part in split3(left)]
        obsf[ch] = o0 + o1 + o2

    for s in range(2):
        sensor_field(s * STEPS + 3)

    rim_f[2, mid, :] = rim_step(1, 2, 0) + supply_r
    send_rim(3, rim_f[2, mid, :])
    finish_all(2, 0, rim_f[2, mid, :], functools.partial(put_field, 3), 3)
    base_all(3, 0, supply)

    for s in range(2):
        sensor_field(s * STEPS + 2)

    def span(x):
        return slice(x * NZ, x * NZ + NZ)

    def forcing(state, s, x, n):
        return cnt[span(x)] * state - obsf[s * STEPS + n - 1, span(x)]

    loads[4].wait()
    def send_forcing(n):
        send_cols(
            3 + n,
            [
                forcing(fields[n, s, 1 + x, mid, :], s, x, n)
                for s in range(2)
                for x in range(CX)
            ],
        )

    send_forcing(3)

    def last(s, x, part, value):
        out_c[s, x, part] = value
        flat = slice(x * NZ + part.start, x * NZ + part.stop)
        push = cnt[flat] * value - obsf[s * STEPS + 3, flat]
        adj = value - tgt[s, x, part] + push
        summed[s, x, part] = adj
        put_field(4, s, x, part, adj)

    finish_all(3, 0, rim_step(2, 3, 0) + supply_r, last, 4)
    send_cols(7, [summed[s, x] for s in range(2) for x in range(CX)])

    for n in (3, 2, 1):
        slot = 7 - n
        base_all(slot, 1, lambda s, x: forcing(fields[n, s, 1 + x, mid, :], s, x, n))
        if n > 1:
            for s in range(2):
                sensor_field(s * STEPS + n - 2)
            send_forcing(n - 1)
        if n == 3:
            region = take_region(7)
        else:
            pushed = take_region(4 + n)
            region = rim_step(slot - 1, slot - 1, 1) + pushed
        rim_f[slot, mid, :] = region
        send_rim(slot, region)

        def put(s, x, part, adj):
            summed[s, x, part] = summed[s, x, part] + adj
            put_field(slot + 1, s, x, part, adj)

        finish_all(slot, 1, region, put, slot + 1)

    stacked = jnp.concatenate(
        [
            summed[s, fx, bz * 8 : bz * 8 + 8, :]
            for s in range(2)
            for bz in range(BZ)
            for fx in range(FX)
        ],
        axis=0,
    )
    sums = []
    q0, q1, q2 = [dot_nt(part, spots) for part in split3(stacked)]
    picked = q0 + q1 + q2
    for s in range(2):
        total = jnp.zeros((32, 2 * many_a), F32)
        for g in range(2):
            part = jnp.zeros((32, 2 * many_a), F32)
            span_g = slice(g * 2 * many_a, (g + 1) * 2 * many_a)
            for bz in range(BZ):
                row = (s * BZ + bz) * 32
                part = part + jnp.where(bz_row == bz, picked[row : row + 32, span_g], 0.0)
            total = total + foot_g[g] * part
        both = jnp.sum(total, axis=0, keepdims=True)
        sums.append(both + pltpu.roll(both, many_a, 1))
    if 2 * many_a < CY:
        sums = [
            jnp.concatenate([v, jnp.zeros((1, CY - 2 * many_a), F32)], axis=1) for v in sums
        ]
    grad_o[...] = jnp.concatenate(sums + [jnp.zeros((6, CY), F32)], axis=0)

    @pl.loop(1, gyn)
    def _(t):
        grad_to(t).start()

    grad_i[own_tile, :] = grad_o[...]

    base_all(7, 1, None)
    region = rim_step(6, 6, 1) + take_region(4)

    def keep_out(s, x, part, value):
        out_s[s, x, part] = value

    finish_all(7, 1, region, keep_out, 0)

    both_sides(edge_copy, 1, wait_send, range(8))
    both_sides(x_copy, 0, wait_send, range(10))
    both_sides(lambda a, b: x_copy(a, b, 1), 0, wait_send, range(8))
    both_sides(rim_copy, 0, wait_send, range(7))

    @pl.loop(1, gyn)
    def _(t):
        act_to(t).wait_send()
        sen_to(t).wait_send()

    @pl.loop(1, gxn)
    def _(t):
        sn2_copy(t, True).wait_send()

    @pl.loop(1, gyn)
    def _(t):
        grad_of(t).wait_recv()

    pick_lane = (iota((CY, acts), 0) == me_y * 4 + arank).astype(F32)
    brought = dot_nn(grad_i[...], pick_lane, HIGH)
    mine = jnp.where(to_tile, brought, 0.0)
    for s in range(2):
        out_g[s : s + 1, :] = jnp.sum(
            jnp.where((slot_row & 7) == s, mine, 0.0), axis=0, keepdims=True
        )

    @pl.loop(1, gyn)
    def _(t):
        grad_to(t).wait_send()


def store_kernel(state, sensitivity, gradient, out_c, out_s, out_g, sem):
    copies = [
        pltpu.make_async_copy(source, sink, sem.at[i])
        for i, (source, sink) in enumerate(
            ((state, out_c), (sensitivity, out_s), (gradient, out_g))
        )
    ]
    for copy in copies:
        copy.start()
    for copy in copies:
        copy.wait()


def per_device(
    gxn,
    gyn,
    initial_state,
    eddy_diffusivity,
    velocity,
    target,
    sensor_cell,
    sensor_owner,
    observations,
    actuator_block,
    actuator_owner,
    controls,
    footprint,
):
    sens = sensor_cell.shape[0]
    acts = actuator_block.shape[0]
    rows = gyn * 8
    hbm = pl.BlockSpec(memory_space=pltpu.HBM)
    vmem = pl.BlockSpec(memory_space=pltpu.VMEM)
    dma = pltpu.SemaphoreType.DMA
    big = jax.ShapeDtypeStruct((2, CX, NZ, CY), F32)
    state, sensitivity, gradient = pl.pallas_call(
        functools.partial(whole_kernel, gxn, gyn),
        out_shape=(
            pltpu.VMEM((2, CX, NZ, CY), F32),
            pltpu.VMEM((2, CX, NZ, CY), F32),
            pltpu.VMEM((2, acts), F32),
        ),
        in_specs=[hbm] * 11,
        out_specs=(vmem, vmem, vmem),
        scratch_shapes=[
            pltpu.VMEM((1, sens), jnp.int32),
            pltpu.VMEM((1, sens), jnp.int32),
            pltpu.VMEM((2, STEPS, sens), F32),
            pltpu.VMEM((1, acts), jnp.int32),
            pltpu.VMEM((1, acts), jnp.int32),
            pltpu.VMEM((2, acts), F32),
            pltpu.VMEM((acts, CY), F32),
            pltpu.VMEM((8, 2, CX + 2, PZ, CY), F32),
            pltpu.VMEM((CX + 2, PZ, CY), F32),
            pltpu.VMEM((CX + 2, PZ, CY), F32),
            pltpu.VMEM((2, CX, PZ, CY), F32),
            pltpu.VMEM((2, CX, NZ, CY), F32),
            pltpu.VMEM((2, 2, 8, CX, NZ, CY), F32),
            pltpu.VMEM((7, PZ, CY), F32),
            pltpu.VMEM((2, 7, NZ, CY), F32),
            pltpu.VMEM((2, PZ, CY), F32),
            pltpu.VMEM((2, CX, NZ, CY), F32),
            pltpu.VMEM((2, CX, NZ, CY), F32),
            pltpu.VMEM((CX * NZ, CY), F32),
            pltpu.VMEM((2 * STEPS, CX * NZ, CY), F32),
            pltpu.VMEM((2, CX, NZ, CY), F32),
            pltpu.VMEM((rows, CY), F32),
            pltpu.VMEM((rows, CY), F32),
            pltpu.VMEM((rows, CY), F32),
            pltpu.VMEM((rows, CY), F32),
            pltpu.VMEM((gxn, gyn // 2, CY), F32),
            pltpu.VMEM((gxn, gyn // 2, CY), F32),
            pltpu.VMEM((8, NZ // 2, CY), F32),
            pltpu.VMEM((8, NZ // 2, CY), F32),
            pltpu.VMEM((8, NZ // 2, CY), F32),
            pltpu.VMEM((7, 2, 16, CY), F32),
            pltpu.VMEM((7, 16, CY), F32),
            pltpu.VMEM((7, 16, CY), F32),
            pltpu.VMEM((8, CY), F32),
            pltpu.VMEM((rows, CY), F32),
            dma((12,)),
            dma((10, 2, 2)),
            dma((10, 2, 2)),
            dma((8, 2)),
            dma((8, 2)),
            dma((7, 2)),
            dma((7, 2)),
            dma((gyn,)),
            dma((gyn,)),
            dma((gyn,)),
            dma((gyn,)),
            dma((gxn,)),
            dma((gxn,)),
            dma((gyn,)),
            dma((gyn,)),
        ],
        compiler_params=pltpu.CompilerParams(
            collective_id=0, has_side_effects=True, vmem_limit_bytes=64000000
        ),
        name="whole",
    )(
        initial_state,
        eddy_diffusivity,
        velocity,
        target,
        sensor_cell.reshape(1, sens),
        sensor_owner.reshape(1, sens),
        jnp.transpose(observations, (1, 2, 0)),
        actuator_block.reshape(1, acts),
        actuator_owner.reshape(1, acts),
        controls.T,
        footprint,
    )
    state, sensitivity, gradient = pl.pallas_call(
        store_kernel,
        out_shape=(big, big, jax.ShapeDtypeStruct((2, acts), F32)),
        in_specs=[vmem] * 3,
        out_specs=(hbm,) * 3,
        scratch_shapes=[dma((3,))],
        compiler_params=pltpu.CompilerParams(vmem_limit_bytes=1 << 20),
        name="store",
    )(state, sensitivity, gradient)
    return state, sensitivity, gradient.T


def solution(mesh):
    in_specs = (
        P(None, "gx", None, "gy"),
        P("gx", None, "gy"),
        P(None, "gx", None, "gy"),
        P(None, "gx", None, "gy"),
        P(("gx", "gy")),
        P(("gx", "gy"), None),
        P(("gx", "gy"), None, None),
        P(("gx", "gy")),
        P(("gx", "gy"), None),
        P(("gx", "gy"), None),
        P(("gx", "gy"), None),
    )
    out_specs = (P(None, "gx", None, "gy"), P(None, "gx", None, "gy"), P(("gx", "gy"), None))
    return jax.shard_map(
        functools.partial(per_device, mesh.shape["gx"], mesh.shape["gy"]),
        mesh=mesh,
        in_specs=in_specs,
        out_specs=out_specs,
        check_vma=False,
    )
```

```python
import functools

import jax
import jax.numpy as jnp
from jax import lax
from jax.experimental import pallas as pl
from jax.experimental.pallas import tpu as pltpu
from jax.sharding import PartitionSpec as P

MESH = pl.DeviceIdType.MESH
F32 = jnp.float32
BF16 = jnp.bfloat16
HIGH = lax.Precision.HIGHEST

CX = 4
NZ = 48
CY = 128
FX = 4
FZ = 8
FY = 4
BZ = NZ // FZ
STEPS = 4
ZV = NZ // 8
PZ = NZ + 16
Z0 = 8
prandtl = 0.85
SCALES = (1.0, 1.0 / prandtl)


def iota(shape, dim):
    return lax.broadcasted_iota(jnp.int32, shape, dim)


def dot_nn(a, b, precision=None):
    return lax.dot_general(
        a, b, (((1,), (0,)), ((), ())), precision=precision, preferred_element_type=F32
    )


def dot_nt(a, b, precision=None):
    return lax.dot_general(
        a, b, (((1,), (1,)), ((), ())), precision=precision, preferred_element_type=F32
    )


def split3(x):
    hi = x.astype(BF16)
    rest = x - hi.astype(F32)
    mid = rest.astype(BF16)
    low = (rest - mid.astype(F32)).astype(BF16)
    return hi, mid, low


def rank_of(onehot):
    count = onehot.shape[1]
    earlier = (iota((count, count), 0) < iota((count, count), 1)).astype(F32)
    before = dot_nn(onehot, earlier)
    return jnp.sum(onehot * before, axis=0, keepdims=True).astype(jnp.int32)


def lanes8():
    return iota((8, CY), 1)


def pack_cols(planes):
    group = lax.shift_right_logical(lanes8(), 3)
    tiles = []
    for j in range(ZV // 2):
        tile = jnp.zeros((8, CY), F32)
        for odd in range(2):
            zv = 2 * j + odd
            for p, plane in enumerate(planes):
                turned = pltpu.roll(plane[zv * 8 : zv * 8 + 8], 8 * p + 4 + 64 * odd, 1)
                tile = jnp.where(group == p + 8 * odd, turned, tile)
        tiles.append(tile)
    return jnp.concatenate(tiles, axis=0)


def join_cols(own, left, right):
    lane = lanes8()
    low, first = lane < 64, (lane & 7) < 4
    rows = []
    for j in range(ZV // 2):
        part = slice(8 * j, 8 * j + 8)
        lhs = jnp.where(first, left[part], own[part])
        rhs = jnp.where(first, own[part], right[part])
        rows.append(jnp.where(low, lhs, pltpu.roll(rhs, 64, 1)))
        rows.append(jnp.where(low, pltpu.roll(lhs, 64, 1), rhs))
    return jnp.concatenate(rows, axis=0)


def halo_planes(region, number):
    lane = iota((NZ, CY), 1)
    both = jnp.where((lane & 7) == 4, pltpu.roll(region, 1, 1), pltpu.roll(region, 63, 1))
    return [pltpu.roll(both, CY - (8 * p + 4), 1) for p in range(number)]


def squeeze_x(region, x):
    slot = lax.shift_right_logical(lanes8(), 3) & 3
    tiles = []
    for first in (0, 4):
        tile = jnp.zeros((8, CY), F32)
        for k in range(first, min(first + 4, ZV)):
            shift = (8 * (k - first - x)) % CY
            part = region[8 * k : 8 * k + 8]
            tile = jnp.where(slot == k - first, pltpu.roll(part, shift, 1) if shift else part, tile)
        tiles.append(tile)
    return jnp.concatenate(tiles, axis=0)


def spread_x(tiles, x):
    rows = []
    for k in range(ZV):
        shift = (8 * (x - k % 4)) % CY
        part = tiles[8 * (k // 4) : 8 * (k // 4) + 8]
        rows.append(pltpu.roll(part, shift, 1) if shift else part)
    return jnp.concatenate(rows, axis=0)


def beside_x(region, below, above):
    slot = lax.shift_right_logical(iota((NZ, CY), 1), 3) & 3
    minus = jnp.where(slot == 0, spread_x(below, 0), pltpu.roll(region, 8, 1))
    plus = jnp.where(slot == 3, spread_x(above, 3), pltpu.roll(region, CY - 8, 1))
    return plus, minus


def beside_y(plane, halo):
    lane = iota(plane.shape, 1)
    above = jnp.where(lane == CY - 1, halo, pltpu.roll(plane, CY - 1, 1))
    below = jnp.where(lane == 0, halo, pltpu.roll(plane, 1, 1))
    return above, below


def whole_kernel(
    gxn,
    gyn,
    c0_h,
    kap_h,
    vel_h,
    tgt_h,
    cell_h,
    own_h,
    obs_h,
    ablk_h,
    aown_h,
    ctl_h,
    foot_h,
    out_c,
    out_s,
    out_g,
    cell_r,
    own_r,
    obs_r,
    ablk_r,
    aown_r,
    ctl_r,
    foot_r,
    fields,
    kap,
    velx,
    velyz,
    tgt,
    cof,
    rim_f,
    rim_c,
    rim_k,
    bas,
    src,
    cnt,
    obsf,
    summed,
    act_o,
    act_i,
    sen_o,
    sen_i,
    sn2_o,
    sn2_i,
    edge_o,
    edge_l,
    edge_r,
    rim_o,
    rim_d,
    rim_u,
    grad_o,
    grad_i,
    loc_sem,
    xs_sem,
    xr_sem,
    es_sem,
    er_sem,
    fs_sem,
    fr_sem,
    as_sem,
    ar_sem,
    ss_sem,
    sr_sem,
    ts_sem,
    tr_sem,
    gs_sem,
    gr_sem,
):
    me_x = lax.axis_index("gx")
    me_y = lax.axis_index("gy")
    lg_y = gyn.bit_length() - 1
    mid = slice(Z0, Z0 + NZ)

    far_first = [t for t in (10, 6, 9, 11, 14, 7, 5, 13, 8, 2, 3, 12, 15, 4, 1) if t < gyn]
    barrier = pltpu.get_barrier_semaphore()
    for t in far_first:
        pl.semaphore_signal(
            barrier, inc=1, device_id=(me_x, lax.rem(me_y + t, gyn)), device_id_type=MESH
        )
    for t in range(1, gxn):
        pl.semaphore_signal(
            barrier, inc=1, device_id=(lax.rem(me_x + t, gxn), me_y), device_id_type=MESH
        )

    smalls = [
        pltpu.make_async_copy(source, sink, loc_sem.at[5 + i])
        for i, (source, sink) in enumerate(
            (
                (aown_h, aown_r),
                (ablk_h, ablk_r),
                (ctl_h, ctl_r),
                (foot_h, foot_r),
                (own_h, own_r),
                (cell_h, cell_r),
                (obs_h, obs_r),
            )
        )
    ]
    for load in smalls:
        load.start()
    loads = [
        pltpu.make_async_copy(c0_h, fields.at[0, :, 1 : 1 + CX, mid, :], loc_sem.at[0]),
        pltpu.make_async_copy(kap_h, kap.at[1 : 1 + CX, mid, :], loc_sem.at[1]),
        pltpu.make_async_copy(vel_h.at[0], velx.at[1 : 1 + CX, mid, :], loc_sem.at[2]),
        pltpu.make_async_copy(vel_h.at[1:3], velyz.at[:, :, mid, :], loc_sem.at[3]),
        pltpu.make_async_copy(tgt_h, tgt, loc_sem.at[4]),
    ]
    for load in loads:
        load.start()

    for load in smalls:
        load.wait()
    rows = gyn * 8
    acts = aown_r.shape[1]
    aown = aown_r[...]
    slot_row = iota((rows, acts), 0)
    arank = rank_of((iota((gyn, acts), 0) == aown).astype(F32))
    to_tile = lax.shift_right_logical(slot_row, 3) == aown
    pick_foot = (to_tile & ((slot_row & 7) == arank)).astype(F32)
    pick_meta = (to_tile & ((slot_row & 7) == arank + 4)).astype(F32)
    meta_row = iota((CY, acts), 0)
    meta = jnp.where(
        meta_row == 0,
        ablk_r[...].astype(F32) + 1.0,
        jnp.where(
            meta_row == 1, ctl_r[0:1, :], jnp.where(meta_row == 2, ctl_r[1:2, :], 0.0)
        ),
    )
    act_o[...] = dot_nn(pick_foot, foot_r[...], HIGH) + dot_nt(pick_meta, meta, HIGH)

    sens = own_r.shape[1]
    owner = own_r[...]
    spot = (owner & (gyn - 1)) * 8 + lax.shift_right_logical(owner, lg_y)
    pick_sens = (iota((rows, sens), 0) == spot).astype(F32)
    srank = rank_of(pick_sens)
    datum = jnp.concatenate(
        [
            cell_r[...].astype(F32) + 1.0,
            obs_r[0],
            obs_r[1],
            jnp.zeros((7, sens), F32),
        ],
        axis=0,
    )
    spread = [jnp.where(srank == k, datum, 0.0) for k in range(4)]
    spread.append(jnp.zeros((64, sens), F32))
    sen_o[...] = dot_nt(pick_sens, jnp.concatenate(spread, axis=0), HIGH)

    zero_rows = jnp.zeros((8, CY), F32)
    for slot in range(8):
        for s in range(2):
            for x in range(1, 1 + CX):
                fields[slot, s, x, 0:8, :] = zero_rows
                fields[slot, s, x, Z0 + NZ : PZ, :] = zero_rows
    for x in range(1, 1 + CX):
        kap[x, 0:8, :] = zero_rows
        kap[x, Z0 + NZ : PZ, :] = zero_rows
        velyz[1, x - 1, 0:8, :] = zero_rows
        velyz[1, x - 1, Z0 + NZ : PZ, :] = zero_rows
    for slot in range(7):
        rim_f[slot, 0:8, :] = zero_rows
        rim_f[slot, Z0 + NZ : PZ, :] = zero_rows
    for slot in range(2):
        rim_k[slot, 0:8, :] = zero_rows
        rim_k[slot, Z0 + NZ : PZ, :] = zero_rows
    zero_plane = jnp.zeros((NZ, CY), F32)

    def zero_side(x):
        for slot in range(8):
            for s in range(2):
                fields[slot, s, x, mid, :] = zero_plane
        kap[x, mid, :] = zero_plane
        velx[x, mid, :] = zero_plane

    @pl.when(me_x == 0)
    def _():
        zero_side(0)
        rim_d[...] = jnp.zeros_like(rim_d)

    @pl.when(me_x == gxn - 1)
    def _():
        zero_side(CX + 1)
        rim_u[...] = jnp.zeros_like(rim_u)

    @pl.when(me_y == 0)
    def _():
        edge_l[...] = jnp.zeros_like(edge_l)

    @pl.when(me_y == gyn - 1)
    def _():
        edge_r[...] = jnp.zeros_like(edge_r)

    for load in loads[:4]:
        load.wait()

    edge_o[0] = pack_cols([fields[0, s, 1 + x, mid, :] for s in range(2) for x in range(CX)])
    edge_o[1] = pack_cols(
        [kap[1 + x, mid, :] for x in range(CX)] + [velx[1 + x, mid, :] for x in range(CX)]
    )
    edge_o[2] = pack_cols([velyz[f, x, mid, :] for f in range(2) for x in range(CX)])

    cells = [(s, x) for x in (0, CX - 1, 1, 2) for s in range(2)]

    def base(slot, d, s, x):
        here = fields[slot, s, 1 + x, mid, :]
        value = (
            cof[0, s, 7, x] * here
            + cof[d, s, 2, x] * pltpu.roll(here, CY - 1, 1)
            + cof[d, s, 3, x] * pltpu.roll(here, 1, 1)
            + cof[d, s, 4, x] * fields[slot, s, 1 + x, Z0 + 1 : Z0 + NZ + 1, :]
            + cof[d, s, 5, x] * fields[slot, s, 1 + x, Z0 - 1 : Z0 + NZ - 1, :]
        )
        if x < CX - 1:
            value = value + cof[d, s, 0, x] * fields[slot, s, 2 + x, mid, :]
        if x > 0:
            value = value + cof[d, s, 1, x] * fields[slot, s, x, mid, :]
        return value

    def base_all(slot, d, extra):
        for s, x in cells:
            value = base(slot, d, s, x)
            bas[s, x] = value if extra is None else value + extra(s, x)

    pl.semaphore_wait(barrier, gyn - 1 + gxn - 1)

    def to_peer_y(source, sink, send, recv):
        def make(t):
            there = lax.rem(me_y + t, gyn)
            return pltpu.make_async_remote_copy(
                src_ref=source(there),
                dst_ref=sink(me_y),
                send_sem=send.at[t],
                recv_sem=recv.at[t],
                device_id=(me_x, there),
                device_id_type=MESH,
            )

        return make

    def of_peer_y(source, sink, send, recv):
        def make(t):
            there = lax.rem(me_y + gyn - t, gyn)
            return pltpu.make_async_remote_copy(
                src_ref=source(there),
                dst_ref=sink(there),
                send_sem=send.at[t],
                recv_sem=recv.at[t],
                device_id=(me_x, there),
                device_id_type=MESH,
            )

        return make

    def tile_of(ref):
        return lambda d: ref.at[pl.ds(pl.multiple_of(d * 8, 8), 8), :]

    act_to = to_peer_y(tile_of(act_o), tile_of(act_i), as_sem, ar_sem)
    act_of = of_peer_y(tile_of(act_o), tile_of(act_i), as_sem, ar_sem)
    sen_to = to_peer_y(tile_of(sen_o), tile_of(sen_i), ss_sem, sr_sem)
    sen_of = of_peer_y(tile_of(sen_o), tile_of(sen_i), ss_sem, sr_sem)
    same = lambda d: grad_o
    grad_to = to_peer_y(same, tile_of(grad_i), gs_sem, gr_sem)
    grad_of = of_peer_y(same, tile_of(grad_i), gs_sem, gr_sem)

    def edge_copy(slot, side):
        there = me_y - 1 if side == 0 else me_y + 1
        sink = edge_r if side == 0 else edge_l
        return pltpu.make_async_remote_copy(
            src_ref=edge_o.at[slot],
            dst_ref=sink.at[slot],
            send_sem=es_sem.at[slot, side],
            recv_sem=er_sem.at[slot, side],
            device_id=(me_x, there),
            device_id_type=MESH,
        )

    def rim_copy(slot, side):
        there = me_x - 1 if side == 0 else me_x + 1
        sink = rim_u if side == 0 else rim_d
        return pltpu.make_async_remote_copy(
            src_ref=rim_o.at[slot, side],
            dst_ref=sink.at[slot],
            send_sem=fs_sem.at[slot, side],
            recv_sem=fr_sem.at[slot, side],
            device_id=(there, me_y),
            device_id_type=MESH,
        )

    def x_copy(slot, side, chunk=0):
        there = me_x - 1 if side == 0 else me_x + 1
        sink = CX + 1 if side == 0 else 0
        own = 0 if side == 0 else CX - 1
        part = mid
        if slot < 8:
            source = fields.at[slot, chunk, own + 1, part, :]
            dest = fields.at[slot, chunk, sink, part, :]
        else:
            held = kap if slot == 8 else velx
            source = held.at[own + 1, part, :]
            dest = held.at[sink, part, :]
        return pltpu.make_async_remote_copy(
            src_ref=source,
            dst_ref=dest,
            send_sem=xs_sem.at[slot, side, chunk],
            recv_sem=xr_sem.at[slot, side, chunk],
            device_id=(there, me_y),
            device_id_type=MESH,
        )

    has = (
        (me_x > 0, me_x < gxn - 1),
        (me_y > 0, me_y < gyn - 1),
    )

    def both_sides(maker, axis, action, slots):
        for side in (0, 1):

            @pl.when(has[axis][side])
            def _(side=side):
                for slot in slots:
                    action(maker(slot, side))

    def start(copy):
        copy.start()

    def wait_send(copy):
        copy.wait_send()

    def wait_recv(maker, axis, slots):
        for side in (0, 1):

            @pl.when(has[axis][1 - side])
            def _(side=side):
                for slot in slots:
                    maker(slot, side).wait_recv()

    both_sides(x_copy, 0, start, (8,))
    for chunk in range(2):
        both_sides(lambda a, b: x_copy(a, b, chunk), 0, start, (0,))
    both_sides(x_copy, 0, start, (9,))

    for t in far_first:
        act_to(t).start()

    both_sides(edge_copy, 1, start, (1, 2, 0))

    @pl.loop(1, gyn)
    def _(t):
        sen_to(t).start()

    own_tile = pl.ds(pl.multiple_of(me_y * 8, 8), 8)
    act_i[own_tile, :] = act_o[own_tile, :]
    sen_i[own_tile, :] = sen_o[own_tile, :]

    lane = iota((NZ, CY), 1)
    nothing = jnp.zeros((NZ, CY), F32)
    for x in range(CX):
        here = kap[1 + x, mid, :]
        kyp, kym = beside_y(here, nothing)
        around = (
            kap[2 + x, mid, :] if x < CX - 1 else nothing,
            kap[x, mid, :] if x > 0 else nothing,
            kyp,
            kym,
            kap[1 + x, Z0 + 1 : Z0 + NZ + 1, :],
            kap[1 + x, Z0 - 1 : Z0 + NZ - 1, :],
        )
        faces = [0.5 * (here + other) for other in around]
        total = faces[0] + faces[1] + faces[2] + faces[3] + faces[4] + faces[5]
        uy = velyz[0, x, mid, :]
        uyp, uym = beside_y(uy, nothing)
        ux = velx[1 + x, mid, :]
        uz = velyz[1, x, mid, :]
        drifts = (
            (-0.5 * ux, 0.5 * ux, -0.5 * uy, 0.5 * uy, -0.5 * uz, 0.5 * uz),
            (
                0.5 * velx[2 + x, mid, :] if x < CX - 1 else None,
                -0.5 * velx[x, mid, :] if x > 0 else None,
                0.5 * uyp,
                -0.5 * uym,
                0.5 * velyz[1, x, Z0 + 1 : Z0 + NZ + 1, :],
                -0.5 * velyz[1, x, Z0 - 1 : Z0 + NZ - 1, :],
            ),
        )
        for s in range(2):
            scale = SCALES[s]
            cof[0, s, 7, x] = 1.0 - scale * total
            for d in range(2):
                for f in range(6):
                    if (f == 0 and x == CX - 1) or (f == 1 and x == 0):
                        continue
                    part = (faces[f] if s == 0 else scale * faces[f]) + drifts[d][f]
                    if f == 2:
                        part = jnp.where(lane == CY - 1, 0.0, part)
                    if f == 3:
                        part = jnp.where(lane == 0, 0.0, part)
                    cof[d, s, f, x] = part
    base_all(0, 0, None)

    def take_region(slot):
        wait_recv(edge_copy, 1, (slot,))
        return join_cols(edge_o[slot], edge_l[slot], edge_r[slot])

    def send_rim(slot, region):
        rim_o[slot, 0] = squeeze_x(region, 0)
        rim_o[slot, 1] = squeeze_x(region, CX - 1)
        both_sides(rim_copy, 0, start, (slot,))

    def take_rim(slot, region):
        wait_recv(rim_copy, 0, (slot,))
        return beside_x(region, rim_d[slot], rim_u[slot])

    region_a = take_region(1)
    send_rim(1, region_a)
    region_b = take_region(2)
    rim_f[0, mid, :] = take_region(0)
    send_rim(0, rim_f[0, mid, :])
    halos = halo_planes(region_a, CX) + halo_planes(region_b, CX)
    def send_cols(slot, planes):
        edge_o[slot] = pack_cols(planes)
        both_sides(edge_copy, 1, start, (slot,))

    @pl.loop(1, gyn)
    def _(t):
        act_of(t).wait_recv()

    many_a = gyn * 4
    sub = iota((8, CY), 0)
    foots, metas = [], []
    for i in range(gyn // 2):
        one, two = act_i[16 * i : 16 * i + 8, :], act_i[16 * i + 8 : 16 * i + 16, :]
        foots.append(jnp.where(sub < 4, one, pltpu.roll(two, 4, 0)))
        metas.append(jnp.where(sub < 4, pltpu.roll(one, 4, 0), two))
    foot = jnp.concatenate(foots * 2, axis=0)
    meta = jnp.concatenate(metas * 2, axis=0)
    sel = (iota((8, CY), 0) == iota((8, CY), 1)).astype(BF16)
    meta_parts = split3(meta)
    m0, m1, m2 = [dot_nt(sel, part) for part in meta_parts]
    meta_rows = m0 + m1 + m2
    blk_row = (meta_rows[0:1] + 0.5).astype(jnp.int32) - 1
    bz_row = jnp.where(blk_row >= 0, lax.shift_right_arithmetic(blk_row, 5), -1)
    blk_col = (meta[:, 0:1] + 0.5).astype(jnp.int32) - 1
    half_col = (iota((2 * many_a, 1), 0) >= many_a).astype(jnp.int32)
    first_y = jnp.where(blk_col >= 0, (blk_col & 31) * FY + half_col, -8)
    at_y = [
        (iota((2 * many_a, CY), 1) == first_y + 2 * g).astype(F32).astype(BF16)
        for g in range(2)
    ]
    perm_row = iota((CY, CY), 0)
    perm = (
        (iota((CY, CY), 1) == (perm_row & 31) * FY + lax.shift_right_logical(perm_row, 5))
        .astype(F32)
        .astype(BF16)
    )
    f0, f1, f2 = [dot_nt(perm, part) for part in split3(foot)]
    foot_t = f0 + f1 + f2
    half_row = iota((32, 2 * many_a), 1) < many_a
    foot_g = [
        jnp.where(half_row, foot_t[64 * g : 64 * g + 32], foot_t[64 * g + 32 : 64 * g + 64])
        for g in range(2)
    ]
    weights = [
        jnp.where(bz_row == bz, meta_rows[1 + s : 2 + s], 0.0)
        for s in range(2)
        for bz in range(BZ)
    ]
    spots = jnp.concatenate(at_y, axis=0)
    for s in range(2):
        left = jnp.concatenate(
            [
                jnp.concatenate([foot_g[g] * weights[s * BZ + bz] for bz in range(BZ)], axis=0)
                for g in range(2)
            ],
            axis=1,
        )
        p0, p1, p2 = [dot_nn(part, spots) for part in split3(left)]
        placed = p0 + p1 + p2
        for bz in range(BZ):
            for fx in range(FX):
                row = bz * 32 + fx * 8
                src[s, fx, bz * 8 : bz * 8 + 8, :] = placed[row : row + 8]

    send_cols(3, [src[s, x] for s in range(2) for x in range(CX)])
    wait_recv(x_copy, 0, (8,))
    sign_y = jnp.where(lane == CY - 1, 1.0, jnp.where(lane == 0, -1.0, 0.0))
    on_y = sign_y != 0.0
    for x in range(CX):
        here = kap[1 + x, mid, :]
        missing = jnp.where(on_y, 0.5 * halos[x], 0.0)
        face_y = jnp.where(on_y, 0.5 * (here + halos[x]), 0.0)
        drift_y = (
            -0.5 * sign_y * velyz[0, x, mid, :],
            0.5 * sign_y * halos[CX + x],
        )
        if x in (0, CX - 1):
            far = 0 if x == 0 else CX + 1
            sign = -0.5 if x == 0 else 0.5
            missing = missing + 0.5 * kap[far, mid, :]
            face_x = 0.5 * (here + kap[far, mid, :])
            drift_x = -sign * velx[1 + x, mid, :]
        for s in range(2):
            scaled = missing if s == 0 else SCALES[s] * missing
            cof[0, s, 7, x] = cof[0, s, 7, x] - scaled
            bas[s, x] = bas[s, x] - scaled * fields[0, s, 1 + x, mid, :]
            for d in range(2):
                cof[d, s, 6, x] = SCALES[s] * face_y + drift_y[d]
            if x in (0, CX - 1):
                cof[0, s, 1 if x == 0 else 0, x] = SCALES[s] * face_x + drift_x

    whole = slice(0, NZ)

    def finish(slot, d, s, x, halo, part):
        value = bas[s, x, part] + cof[d, s, 6, x, part] * halo[part]
        far = slice(Z0 + part.start, Z0 + part.stop)
        if x == 0:
            value = value + cof[d, s, 1, x, part] * fields[slot, s, 0, far, :]
        if x == CX - 1:
            value = value + cof[d, s, 0, x, part] * fields[slot, s, CX + 1, far, :]
        return value

    def put_field(slot, s, x, part, value):
        fields[slot, s, 1 + x, slice(Z0 + part.start, Z0 + part.stop), :] = value

    def send_chunk(slot, chunk):
        both_sides(lambda a, b: x_copy(a, b, chunk), 0, start, (slot,))

    def finish_all(slot, d, region, put, onward):
        halos = halo_planes(region, 2 * CX)
        for chunk in range(2):
            s, part = chunk, whole
            wait_recv(lambda a, b: x_copy(a, b, chunk), 0, (slot,))
            for x in (0, CX - 1):
                put(s, x, part, finish(slot, d, s, x, halos[s * CX + x], part))
            if onward:
                send_chunk(onward, chunk)
        for s in range(2):
            for x in range(1, CX - 1):
                put(s, x, whole, finish(slot, d, s, x, halos[s * CX + x], whole))

    def keep_base(s, x, part, value):
        bas[s, x, part] = value

    finish_all(0, 0, rim_f[0, mid, :], keep_base, 0)

    for chunk in range(2):
        s, part = chunk, whole
        for x in (0, CX - 1):
            put_field(1, s, x, part, bas[s, x, part] + src[s, x, part])
        send_chunk(1, chunk)
    for s in range(2):
        for x in range(1, CX - 1):
            put_field(1, s, x, whole, bas[s, x] + src[s, x])

    wait_recv(x_copy, 0, (9,))
    for x, far, sign, f in ((0, 0, -0.5, 1), (CX - 1, CX + 1, 0.5, 0)):
        face_x = 0.5 * (kap[1 + x, mid, :] + kap[far, mid, :])
        for s in range(2):
            cof[1, s, f, x] = SCALES[s] * face_x + sign * velx[far, mid, :]

    second = (lane & 32) != 0
    outside = ((lane < 64) & ((lane & 7) < 4) & (me_y == 0)) | (
        (lane >= 64) & ((lane & 7) >= 4) & (me_y == gyn - 1)
    )
    keep = jnp.where(outside, 0.0, 1.0)
    scale_r = jnp.where(second, SCALES[1], SCALES[0])

    def first_of(v):
        return jnp.where(second, pltpu.roll(v, 32, 1), v)

    def second_of(v):
        return jnp.where(second, v, pltpu.roll(v, CY - 32, 1))

    plus_a, minus_a = take_rim(1, region_a)
    here = first_of(region_a)
    rim_k[0, mid, :] = here
    uz = second_of(region_b)
    rim_k[1, mid, :] = uz
    uy = first_of(region_b)
    ux = second_of(region_a)
    up, down = slice(Z0 + 1, Z0 + NZ + 1), slice(Z0 - 1, Z0 + NZ - 1)
    around = (
        first_of(plus_a),
        first_of(minus_a),
        pltpu.roll(here, CY - 1, 1),
        pltpu.roll(here, 1, 1),
        rim_k[0, up, :],
        rim_k[0, down, :],
    )
    faces = [0.5 * (here + other) for other in around]
    total = faces[0] + faces[1] + faces[2] + faces[3] + faces[4] + faces[5]
    rim_c[0, 6] = keep * (1.0 - scale_r * total)
    drifts = (
        (-0.5 * ux, 0.5 * ux, -0.5 * uy, 0.5 * uy, -0.5 * uz, 0.5 * uz),
        (
            0.5 * second_of(plus_a),
            -0.5 * second_of(minus_a),
            0.5 * pltpu.roll(uy, CY - 1, 1),
            -0.5 * pltpu.roll(uy, 1, 1),
            0.5 * rim_k[1, up, :],
            -0.5 * rim_k[1, down, :],
        ),
    )
    for d in range(2):
        for f in range(6):
            rim_c[d, f] = keep * (scale_r * faces[f] + drifts[d][f])

    def rim_step(slot, rim_slot, d):
        region = rim_f[slot, mid, :]
        plus, minus = take_rim(rim_slot, region)
        return (
            rim_c[0, 6] * region
            + rim_c[d, 2] * pltpu.roll(region, CY - 1, 1)
            + rim_c[d, 3] * pltpu.roll(region, 1, 1)
            + rim_c[d, 4] * rim_f[slot, up, :]
            + rim_c[d, 5] * rim_f[slot, down, :]
            + rim_c[d, 0] * plus
            + rim_c[d, 1] * minus
        )

    rim_f[1, mid, :] = rim_step(0, 0, 0)

    @pl.loop(1, gyn)
    def _(t):
        sen_of(t).wait_recv()

    for d in range(gxn):
        held = sen_i[pl.ds(d, gyn, stride=8), :]
        half = gyn // 2
        sn2_o[d] = jnp.where(
            iota((half, CY), 1) < 64, held[:half], pltpu.roll(held[half:], 64, 1)
        )

    def sn2_copy(t, sending):
        there = lax.rem(me_x + t, gxn) if sending else lax.rem(me_x + gxn - t, gxn)
        return pltpu.make_async_remote_copy(
            src_ref=sn2_o.at[there],
            dst_ref=sn2_i.at[me_x] if sending else sn2_i.at[there],
            send_sem=ts_sem.at[t],
            recv_sem=tr_sem.at[t],
            device_id=(there, me_y),
            device_id_type=MESH,
        )

    @pl.loop(1, gxn)
    def _(t):
        sn2_copy(t, True).start()

    sn2_i[me_x] = sn2_o[me_x]

    supply = lambda s, x: src[s, x]
    base_all(1, 0, supply)

    supply_r = take_region(3)
    rim_f[1, mid, :] = rim_f[1, mid, :] + supply_r
    send_rim(2, rim_f[1, mid, :])
    finish_all(1, 0, rim_f[1, mid, :], functools.partial(put_field, 2), 2)
    base_all(2, 0, supply)

    @pl.loop(1, gxn)
    def _(t):
        sn2_copy(t, False).wait_recv()

    both = jnp.concatenate([sn2_i[d] for d in range(gxn)], axis=0)
    records = jnp.concatenate([both, pltpu.roll(both, 64, 1)], axis=0)
    many = records.shape[0]
    take = (iota((64, CY), 0) == iota((64, CY), 1)).astype(BF16)
    r0, r1, r2 = [dot_nt(take, part) for part in split3(records)]
    lanes_t = r0 + r1 + r2
    pick_zx, at_lane = [], []
    for k in range(4):
        cell_row = (lanes_t[16 * k : 16 * k + 1] + 0.5).astype(jnp.int32) - 1
        zx = lax.shift_right_arithmetic(cell_row, 7)
        pick_zx.append(iota((CX * NZ, many), 0) == zx)
        cell_col = (records[:, 16 * k : 16 * k + 1] + 0.5).astype(jnp.int32) - 1
        where_y = jnp.where(cell_col >= 0, cell_col & (CY - 1), -1)
        at_lane.append((iota((many, CY), 1) == where_y).astype(F32).astype(BF16))
    at_lanes = jnp.concatenate(at_lane, axis=0)
    one_zx = jnp.concatenate([p.astype(F32).astype(BF16) for p in pick_zx], axis=1)
    cnt[...] = dot_nn(one_zx, at_lanes)

    def sensor_field(ch):
        rows_of = [lanes_t[16 * k + 1 + ch : 16 * k + 2 + ch] for k in range(4)]
        left = jnp.concatenate(
            [jnp.where(pick_zx[k], rows_of[k], 0.0) for k in range(4)], axis=1
        )
        o0, o1, o2 = [dot_nn(part, at_lanes) for part in split3(left)]
        obsf[ch] = o0 + o1 + o2

    for s in range(2):
        sensor_field(s * STEPS + 3)

    rim_f[2, mid, :] = rim_step(1, 2, 0) + supply_r
    send_rim(3, rim_f[2, mid, :])
    finish_all(2, 0, rim_f[2, mid, :], functools.partial(put_field, 3), 3)
    base_all(3, 0, supply)

    for s in range(2):
        sensor_field(s * STEPS + 2)

    def span(x):
        return slice(x * NZ, x * NZ + NZ)

    def forcing(state, s, x, n):
        return cnt[span(x)] * state - obsf[s * STEPS + n - 1, span(x)]

    loads[4].wait()
    def send_forcing(n):
        send_cols(
            3 + n,
            [
                forcing(fields[n, s, 1 + x, mid, :], s, x, n)
                for s in range(2)
                for x in range(CX)
            ],
        )

    send_forcing(3)

    def last(s, x, part, value):
        out_c[s, x, part] = value
        flat = slice(x * NZ + part.start, x * NZ + part.stop)
        push = cnt[flat] * value - obsf[s * STEPS + 3, flat]
        adj = value - tgt[s, x, part] + push
        summed[s, x, part] = adj
        put_field(4, s, x, part, adj)

    finish_all(3, 0, rim_step(2, 3, 0) + supply_r, last, 4)
    send_cols(7, [summed[s, x] for s in range(2) for x in range(CX)])

    for n in (3, 2, 1):
        slot = 7 - n
        base_all(slot, 1, lambda s, x: forcing(fields[n, s, 1 + x, mid, :], s, x, n))
        if n > 1:
            for s in range(2):
                sensor_field(s * STEPS + n - 2)
            send_forcing(n - 1)
        if n == 3:
            region = take_region(7)
        else:
            pushed = take_region(4 + n)
            region = rim_step(slot - 1, slot - 1, 1) + pushed
        rim_f[slot, mid, :] = region
        send_rim(slot, region)

        def put(s, x, part, adj):
            summed[s, x, part] = summed[s, x, part] + adj
            put_field(slot + 1, s, x, part, adj)

        finish_all(slot, 1, region, put, slot + 1)

    stacked = jnp.concatenate(
        [
            summed[s, fx, bz * 8 : bz * 8 + 8, :]
            for s in range(2)
            for bz in range(BZ)
            for fx in range(FX)
        ],
        axis=0,
    )
    sums = []
    q0, q1, q2 = [dot_nt(part, spots) for part in split3(stacked)]
    picked = q0 + q1 + q2
    for s in range(2):
        total = jnp.zeros((32, 2 * many_a), F32)
        for g in range(2):
            part = jnp.zeros((32, 2 * many_a), F32)
            span_g = slice(g * 2 * many_a, (g + 1) * 2 * many_a)
            for bz in range(BZ):
                row = (s * BZ + bz) * 32
                part = part + jnp.where(bz_row == bz, picked[row : row + 32, span_g], 0.0)
            total = total + foot_g[g] * part
        both = jnp.sum(total, axis=0, keepdims=True)
        sums.append(both + pltpu.roll(both, many_a, 1))
    if 2 * many_a < CY:
        sums = [
            jnp.concatenate([v, jnp.zeros((1, CY - 2 * many_a), F32)], axis=1) for v in sums
        ]
    grad_o[...] = jnp.concatenate(sums + [jnp.zeros((6, CY), F32)], axis=0)

    for t in far_first:
        grad_to(t).start()

    grad_i[own_tile, :] = grad_o[...]

    base_all(7, 1, None)
    region = rim_step(6, 6, 1) + take_region(4)

    def keep_out(s, x, part, value):
        out_s[s, x, part] = value

    finish_all(7, 1, region, keep_out, 0)

    both_sides(edge_copy, 1, wait_send, range(8))
    both_sides(x_copy, 0, wait_send, range(10))
    both_sides(lambda a, b: x_copy(a, b, 1), 0, wait_send, range(8))
    both_sides(rim_copy, 0, wait_send, range(7))

    @pl.loop(1, gyn)
    def _(t):
        act_to(t).wait_send()
        sen_to(t).wait_send()

    @pl.loop(1, gxn)
    def _(t):
        sn2_copy(t, True).wait_send()

    pick_lane = (iota((CY, acts), 0) == me_y * 4 + arank).astype(F32).astype(BF16)

    @pl.loop(1, gyn)
    def _(t):
        grad_of(t).wait_recv()

    b0, b1, b2 = [dot_nn(part, pick_lane) for part in split3(grad_i[...])]
    brought = b0 + b1 + b2
    mine = jnp.where(to_tile, brought, 0.0)
    for s in range(2):
        out_g[s : s + 1, :] = jnp.sum(
            jnp.where((slot_row & 7) == s, mine, 0.0), axis=0, keepdims=True
        )

    @pl.loop(1, gyn)
    def _(t):
        grad_to(t).wait_send()


def store_kernel(state, sensitivity, gradient, out_c, out_s, out_g, sem):
    copies = [
        pltpu.make_async_copy(source, sink, sem.at[i])
        for i, (source, sink) in enumerate(
            ((state, out_c), (sensitivity, out_s), (gradient, out_g))
        )
    ]
    for copy in copies:
        copy.start()
    for copy in copies:
        copy.wait()


def per_device(
    gxn,
    gyn,
    initial_state,
    eddy_diffusivity,
    velocity,
    target,
    sensor_cell,
    sensor_owner,
    observations,
    actuator_block,
    actuator_owner,
    controls,
    footprint,
):
    sens = sensor_cell.shape[0]
    acts = actuator_block.shape[0]
    rows = gyn * 8
    hbm = pl.BlockSpec(memory_space=pltpu.HBM)
    vmem = pl.BlockSpec(memory_space=pltpu.VMEM)
    dma = pltpu.SemaphoreType.DMA
    big = jax.ShapeDtypeStruct((2, CX, NZ, CY), F32)
    state, sensitivity, gradient = pl.pallas_call(
        functools.partial(whole_kernel, gxn, gyn),
        out_shape=(
            pltpu.VMEM((2, CX, NZ, CY), F32),
            pltpu.VMEM((2, CX, NZ, CY), F32),
            pltpu.VMEM((2, acts), F32),
        ),
        in_specs=[hbm] * 11,
        out_specs=(vmem, vmem, vmem),
        scratch_shapes=[
            pltpu.VMEM((1, sens), jnp.int32),
            pltpu.VMEM((1, sens), jnp.int32),
            pltpu.VMEM((2, STEPS, sens), F32),
            pltpu.VMEM((1, acts), jnp.int32),
            pltpu.VMEM((1, acts), jnp.int32),
            pltpu.VMEM((2, acts), F32),
            pltpu.VMEM((acts, CY), F32),
            pltpu.VMEM((8, 2, CX + 2, PZ, CY), F32),
            pltpu.VMEM((CX + 2, PZ, CY), F32),
            pltpu.VMEM((CX + 2, PZ, CY), F32),
            pltpu.VMEM((2, CX, PZ, CY), F32),
            pltpu.VMEM((2, CX, NZ, CY), F32),
            pltpu.VMEM((2, 2, 8, CX, NZ, CY), F32),
            pltpu.VMEM((7, PZ, CY), F32),
            pltpu.VMEM((2, 7, NZ, CY), F32),
            pltpu.VMEM((2, PZ, CY), F32),
            pltpu.VMEM((2, CX, NZ, CY), F32),
            pltpu.VMEM((2, CX, NZ, CY), F32),
            pltpu.VMEM((CX * NZ, CY), F32),
            pltpu.VMEM((2 * STEPS, CX * NZ, CY), F32),
            pltpu.VMEM((2, CX, NZ, CY), F32),
            pltpu.VMEM((rows, CY), F32),
            pltpu.VMEM((rows, CY), F32),
            pltpu.VMEM((rows, CY), F32),
            pltpu.VMEM((rows, CY), F32),
            pltpu.VMEM((gxn, gyn // 2, CY), F32),
            pltpu.VMEM((gxn, gyn // 2, CY), F32),
            pltpu.VMEM((8, NZ // 2, CY), F32),
            pltpu.VMEM((8, NZ // 2, CY), F32),
            pltpu.VMEM((8, NZ // 2, CY), F32),
            pltpu.VMEM((7, 2, 16, CY), F32),
            pltpu.VMEM((7, 16, CY), F32),
            pltpu.VMEM((7, 16, CY), F32),
            pltpu.VMEM((8, CY), F32),
            pltpu.VMEM((rows, CY), F32),
            dma((12,)),
            dma((10, 2, 2)),
            dma((10, 2, 2)),
            dma((8, 2)),
            dma((8, 2)),
            dma((7, 2)),
            dma((7, 2)),
            dma((gyn,)),
            dma((gyn,)),
            dma((gyn,)),
            dma((gyn,)),
            dma((gxn,)),
            dma((gxn,)),
            dma((gyn,)),
            dma((gyn,)),
        ],
        compiler_params=pltpu.CompilerParams(
            collective_id=0, has_side_effects=True, vmem_limit_bytes=64000000
        ),
        name="whole",
    )(
        initial_state,
        eddy_diffusivity,
        velocity,
        target,
        sensor_cell.reshape(1, sens),
        sensor_owner.reshape(1, sens),
        jnp.transpose(observations, (1, 2, 0)),
        actuator_block.reshape(1, acts),
        actuator_owner.reshape(1, acts),
        controls.T,
        footprint,
    )
    state, sensitivity, gradient = pl.pallas_call(
        store_kernel,
        out_shape=(big, big, jax.ShapeDtypeStruct((2, acts), F32)),
        in_specs=[vmem] * 3,
        out_specs=(hbm,) * 3,
        scratch_shapes=[dma((3,))],
        compiler_params=pltpu.CompilerParams(vmem_limit_bytes=1 << 20),
        name="store",
    )(state, sensitivity, gradient)
    return state, sensitivity, gradient.T


def solution(mesh):
    in_specs = (
        P(None, "gx", None, "gy"),
        P("gx", None, "gy"),
        P(None, "gx", None, "gy"),
        P(None, "gx", None, "gy"),
        P(("gx", "gy")),
        P(("gx", "gy"), None),
        P(("gx", "gy"), None, None),
        P(("gx", "gy")),
        P(("gx", "gy"), None),
        P(("gx", "gy"), None),
        P(("gx", "gy"), None),
    )
    out_specs = (P(None, "gx", None, "gy"), P(None, "gx", None, "gy"), P(("gx", "gy"), None))
    return jax.shard_map(
        functools.partial(per_device, mesh.shape["gx"], mesh.shape["gy"]),
        mesh=mesh,
        in_specs=in_specs,
        out_specs=out_specs,
        check_vma=False,
    )
```
